512 devices in a mesh: section: 8 (over z_hi, x), dp: 64 (over y, z_lo, core).
Axes of the slice: x: 4, y: 4, z: 16 (z_hi: 2, z_lo: 8; z = z_hi * 8 + z_lo), core: 2. Of those that a mesh axis runs over, the one named last changes fastest.
Arguments:
- clips: bfloat16 [128, 8, 2, 8, 256], P('dp'), may hold values from -6 to 6
- cotangent: bfloat16 [128, 8, 2, 8, 256], P('dp'), may hold values from -6 to 6
- spatial_kernel: bfloat16 [8, 2304, 256], P('section'), may hold values from -0.125 to 0.125
- temporal_kernel: bfloat16 [8, 768, 256], P('section'), may hold values from -0.21875 to 0.21875
Outputs:
- grad_spatial: float32 [8, 2304, 256], P('section', 'dp')
- grad_temporal: float32 [8, 768, 256], P('section', 'dp')
The draws below stay inside these ranges and needn't reach their ends.
All inputs are finite; a program needn't handle non-finite values.
Results may differ from the reference program's by a relative error of at most 0.024.
Values may be sent and summed in bfloat16 or wider, within the bound.
A program may use at most 64 MiB of HBM per device.

```python
import math
import jax
import jax.numpy as jnp
from jax import lax

C = 256
FRAMES = 8
HEIGHT = 2
WIDTH = 8
SECTIONS = 8
CLIPS = 128


def levels(key, dims, cuts, smallest, high):
    def one(axis_at, parts):
        heights = jax.random.uniform(jax.random.fold_in(jax.random.fold_in(key, 6), axis_at), (parts,), jnp.float32, smallest / len(cuts), high / len(cuts))
        return jnp.repeat(jnp.exp(heights), dims[axis_at] // parts).reshape((-1,) + (1,) * (len(dims) - axis_at - 1))

    gain = one(*cuts[0])
    for cut in cuts[1:]:
        gain = gain * one(*cut)
    return gain


def centred(rng, shape, width, most, shards=(), held_as=jnp.bfloat16):
    result = jax.random.normal(rng, shape, jnp.float32) * width
    if len(shards) > 0:
        result = levels(rng, shape, shards, -0.22, 0.18) * result
    return jnp.clip(result, min=-most, max=most).astype(held_as)


def setup_inputs(seed: int = 0) -> dict:
    streams_of = jax.random.split(jax.random.key(seed), 5)
    return {
        "clips": centred(streams_of[0], (CLIPS, FRAMES, HEIGHT, WIDTH, C), 1.0, 6.0, ((0, 64),)),
        "cotangent": centred(streams_of[1], (CLIPS, FRAMES, HEIGHT, WIDTH, C), 1.0, 6.0, ((0, 64),)),
        "spatial_kernel": centred(streams_of[2], (SECTIONS, 9 * C, C), (9 * C) ** -0.5, 0.125, ((0, 8),)),
        "temporal_kernel": centred(streams_of[3], (SECTIONS, 3 * C, C), (3 * C) ** -0.5, 0.21875, ((0, 8),)),
    }


def offset_cells(values, axis_no, offset):
    if offset == 0:
        return values
    length = values.shape[axis_no]
    padding = [(0, 0)] * values.ndim
    if offset > 0:
        padding[axis_no] = (0, offset)
        return lax.slice_in_dim(jnp.pad(values, padding), offset, offset + length, axis=axis_no)
    padding[axis_no] = (-offset, 0)
    return lax.slice_in_dim(jnp.pad(values, padding), 0, length, axis=axis_no)

def space_patches(x_tile):
    pieces = [offset_cells(offset_cells(x_tile, 1, row_off), 2, col_off) for row_off in (-1, 0, 1) for col_off in (-1, 0, 1)]
    return jnp.concatenate(pieces, axis=-1).reshape(-1, 9 * x_tile.shape[-1])

def time_patches(h_tile):
    pieces = [offset_cells(h_tile, 0, shift_by) for shift_by in (-1, 0, 1)]
    return jnp.concatenate(pieces, axis=-1).reshape(-1, 3 * h_tile.shape[-1])

def contract_rows(left, right):
    return lax.dot_general(left, right, (((0,), (0,)), ((), ())), preferred_element_type=jnp.float32)

def against_rows(left, right):
    return lax.dot_general(left, right, (((1,), (1,)), ((), ())), preferred_element_type=jnp.float32)

def section_forward(x_tile, w_space, w_time):
    shape = x_tile.shape
    channels = shape[-1]
    p_space = space_patches(x_tile)
    pre_act = jnp.dot(p_space, w_space, preferred_element_type=jnp.float32)
    hidden = jax.nn.silu(pre_act).astype(jnp.bfloat16)
    p_time = time_patches(hidden.reshape(shape))
    branch = jnp.dot(p_time, w_time, preferred_element_type=jnp.float32)
    return (x_tile.reshape(-1, channels).astype(jnp.float32) + branch).astype(jnp.bfloat16).reshape(shape)

def section_backward(x_tile, g_tile, w_space, w_time):
    shape = x_tile.shape
    channels = shape[-1]
    p_space = space_patches(x_tile)
    pre_act = jnp.dot(p_space, w_space, preferred_element_type=jnp.float32)
    hidden = jax.nn.silu(pre_act).astype(jnp.bfloat16)
    p_time = time_patches(hidden.reshape(shape))
    g_out = g_tile.reshape(-1, channels)
    g_ptime = against_rows(g_out, w_time)
    g_hidden = jnp.zeros(shape, jnp.float32)
    for index, shift_by in enumerate((-1, 0, 1)):
        piece = g_ptime[:, index * channels:(index + 1) * channels].reshape(shape)
        g_hidden = g_hidden + offset_cells(piece, 0, -shift_by)
    sigma = jax.nn.sigmoid(pre_act)
    g_pre = (g_hidden.reshape(-1, channels) * sigma * (1.0 + pre_act * (1.0 - sigma))).astype(jnp.bfloat16)
    g_pspace = against_rows(g_pre, w_space)
    g_conv = jnp.zeros(shape, jnp.float32)
    index = 0
    for row_off in (-1, 0, 1):
        for col_off in (-1, 0, 1):
            piece = g_pspace[:, index * channels:(index + 1) * channels].reshape(shape)
            g_conv = g_conv + offset_cells(offset_cells(piece, 1, -row_off), 2, -col_off)
            index = index + 1
    g_in = (g_tile.astype(jnp.float32) + g_conv).astype(jnp.bfloat16)
    return (g_in, p_space, p_time, g_pre, g_out)

def reference(clips, cotangent, spatial_kernel, temporal_kernel):
    layers = spatial_kernel.shape[0]
    channels = spatial_kernel.shape[2]
    scale = 1.0 / math.sqrt(CLIPS * FRAMES * HEIGHT * WIDTH)

    def per_clip(carry, item):
        sum_space, sum_time = carry
        x_tile, g_tile = item
        inputs = []
        current = x_tile
        for layer in range(layers):
            inputs.append(current)
            current = section_forward(current, spatial_kernel[layer], temporal_kernel[layer])
        g_now = g_tile
        for layer in range(layers - 1, -1, -1):
            g_in, p_space, p_time, g_pre, g_out = section_backward(inputs[layer], g_now, spatial_kernel[layer], temporal_kernel[layer])
            sum_space = sum_space.at[layer].add(contract_rows(p_space, g_pre))
            sum_time = sum_time.at[layer].add(contract_rows(p_time, g_out))
            g_now = g_in
        return ((sum_space, sum_time), None)
    start = (jnp.zeros((layers, 9 * channels, channels), jnp.float32), jnp.zeros((layers, 3 * channels, channels), jnp.float32))
    totals, unused = lax.scan(per_clip, start, (clips, cotangent))
    return (totals[0] * scale, totals[1] * scale)
```

```python
import functools
import math

import jax
import jax.numpy as jnp
from jax import lax
from jax.experimental import pallas as pl
from jax.experimental.pallas import tpu as pltpu
from jax.sharding import PartitionSpec as P

MESH = pl.DeviceIdType.MESH
F32 = jnp.float32
BF16 = jnp.bfloat16
C = 256
ROWS = 128
HALF = 64
SPACE = 9 * C
TIME = 3 * C


def by_height(v):
    v = v.astype(F32).reshape(8, 2, 8, C)
    return jnp.concatenate([v[:, 0].reshape(HALF, C), v[:, 1].reshape(HALF, C)], axis=0)


def columns(v):
    w = lax.broadcasted_iota(jnp.int32, v.shape, 0) & 7
    before = jnp.where(w == 0, 0.0, pltpu.roll(v, 1, 0))
    after = jnp.where(w == 7, 0.0, pltpu.roll(v, ROWS - 1, 0))
    return before, after


def frames(v):
    zero = jnp.zeros((8, C), F32)
    before = jnp.concatenate([zero, v[0:56], zero, v[64:120]], axis=0)
    after = jnp.concatenate([v[8:64], zero, v[72:128], zero], axis=0)
    return before, after


def nn(a, b):
    return jnp.dot(a, b, preferred_element_type=F32)


def nt(a, b):
    return lax.dot_general(a, b, (((1,), (1,)), ((), ())), preferred_element_type=F32)


def tn(a, b):
    return lax.dot_general(a, b, (((0,), (0,)), ((), ())), preferred_element_type=F32)


def wide_space(v):
    before, after = columns(v)
    return jnp.concatenate([before, v, after], axis=1).astype(BF16)


def wide_time(v):
    before, after = frames(v)
    return jnp.concatenate([before, v, after], axis=1).astype(BF16)


def space_forward(wide, w):
    same = nn(wide, w[768:1536, :])
    top = nn(wide[HALF:], w[1536:2304, :])
    bottom = nn(wide[:HALF], w[0:768, :])
    return same + jnp.concatenate([top, bottom], axis=0)


def activate(pre):
    sigma = jax.nn.sigmoid(pre)
    hidden = (pre * sigma).astype(BF16).astype(F32)
    return hidden, sigma * (1.0 + pre * (1.0 - sigma))


def g_hidden_of(g, w):
    before, after = frames(g)
    out = nt(after.astype(BF16), w[0:256, :])
    out = out + nt(g.astype(BF16), w[256:512, :])
    return out + nt(before.astype(BF16), w[512:768, :])


def space_backward(g_pre, w):
    before, after = columns(g_pre)
    same = top = bottom = None
    for q, v in enumerate((after, g_pre, before)):
        v = v.astype(BF16)
        a = nt(v, w[768 + 256 * q : 1024 + 256 * q, :])
        t = nt(v[HALF:], w[256 * q : 256 * q + 256, :])
        b = nt(v[:HALF], w[1536 + 256 * q : 1792 + 256 * q, :])
        same, top, bottom = (a, t, b) if same is None else (same + a, top + t, bottom + b)
    return same + jnp.concatenate([top, bottom], axis=0)


def kernel(
    scale,
    clips_ref, cot_ref, ws_ref, wt_ref,
    out_s, out_t,
    wsv, wtv, cl, ct, xin, yout, bx, bg, gin,
    act, bact, xc, hc, gp, gb, dw, part, r1, s1, r2, s2, r3, fin,
    loc, wg_send, wg_recv, wf_send,
    x_send, x_recv, bx_send, bx_recv, ct_send, ct_recv,
    go_send, gin_recv, bg_send, bg_recv,
    r1_sem, r2_send, r2_recv, r3_send, r3_recv, r4_sem,
):
    S = lax.axis_index("section")
    D = lax.axis_index("dp")
    half = S // 4
    x = S % 4
    y = D // 16
    z = (D // 2) % 8
    k = D % 2
    far = D + 8 - 16 * (z // 4)
    sibling = D + 1 - 2 * k
    end = jnp.logical_or(x == 0, x == 3)
    mine = jnp.where(x == 0, 1, 0)
    base = half * 4

    def copy(src, dst, send, recv, section, dp):
        return pltpu.make_async_remote_copy(
            src_ref=src, dst_ref=dst, send_sem=send, recv_sem=recv,
            device_id={"section": section, "dp": dp}, device_id_type=MESH,
        )

    local = [
        pltpu.make_async_copy(clips_ref, cl, loc.at[0]),
        pltpu.make_async_copy(ws_ref, wsv.at[x], loc.at[1]),
        pltpu.make_async_copy(wt_ref, wtv.at[x], loc.at[2]),
    ]
    for c in local:
        c.start()

    barrier = pltpu.get_barrier_semaphore()

    def hello(section, dp):
        pl.semaphore_signal(
            barrier, inc=1, device_id={"section": section, "dp": dp}, device_id_type=MESH
        )

    hello(S, sibling)
    for i in range(1, 4):
        hello(S, lax.rem(y + i, 4) * 16 + lax.rem(D, 16))
        hello(base + lax.rem(x + i, 4), D)
    for i in range(1, 8):
        hello(S, y * 16 + lax.rem(z + i, 8) * 2 + k)

    @pl.when(S == 0)
    def _():
        hello(4, far)

    @pl.when(S == 3)
    def _():
        hello(4, far)
        hello(7, far)

    @pl.when(S == 4)
    def _():
        hello(0, far)
        hello(3, far)

    @pl.when(S == 7)
    def _():
        hello(3, far)

    crossings = jnp.where(end, 1, 0) + jnp.where(jnp.logical_or(S == 3, S == 4), 1, 0)
    pl.semaphore_wait(barrier, 14 + crossings)

    def weight_copies(j, target, slot):
        rows_s = pl.ds(pl.multiple_of(k * 1152, 128), 1152)
        rows_t = pl.ds(pl.multiple_of(k * 384, 128), 384)
        return (
            copy(ws_ref.at[rows_s], wsv.at[j, rows_s], wg_send.at[slot, 0], wg_recv.at[j, k, 0], base + target, D),
            copy(wt_ref.at[rows_t], wtv.at[j, rows_t], wg_send.at[slot, 1], wg_recv.at[j, k, 1], base + target, D),
        )

    def share_copies(j, core):
        rows_s = pl.ds(pl.multiple_of(core * 1152, 128), 1152)
        rows_t = pl.ds(pl.multiple_of(core * 384, 128), 384)
        return (
            copy(wsv.at[j, rows_s], wsv.at[j, rows_s], wf_send.at[j, 0], wg_recv.at[j, core, 0], S, sibling),
            copy(wtv.at[j, rows_t], wtv.at[j, rows_t], wf_send.at[j, 1], wg_recv.at[j, core, 1], S, sibling),
        )

    for slot, target in enumerate((0, 3)):
        @pl.when(x != target)
        def _():
            for c in weight_copies(x, target, slot):
                c.start()

    cot_copy = copy(cot_ref.at[mine], ct, ct_send, ct_recv, S, far)

    @pl.when(jnp.logical_or(S == 4, S == 7))
    def _():
        cot_copy.start()

    for c in local:
        c.wait()

    def rows_of(c, h):
        return pl.ds(pl.multiple_of(h * 128 + c * HALF, HALF), HALF)

    def keep(ref, c, value):
        ref[rows_of(c, 0), :] = value[:HALF]
        ref[rows_of(c, 1), :] = value[HALF:]

    def y_copy(c):
        return copy(yout.at[c], xin.at[c], x_send.at[c], x_recv.at[c], lax.rem(S + 1, 8), D)

    def y_cross(c):
        return copy(yout.at[c], bx.at[0], x_send.at[c], bx_recv, jnp.where(c == 0, 7, 4), far)

    def owner_hidden(c):
        wide = wide_space(xin[c].astype(F32))
        keep(xc, c, wide)
        hidden, slope = activate(space_forward(wide, wsv.at[x]))
        act[c] = slope
        wide = wide_time(hidden)
        keep(hc, c, wide)
        return wide

    @pl.when(half == 0)
    def _():
        def clip(c, carry):
            @pl.when(x == 0)
            def _():
                xin[c] = by_height(cl[c]).astype(BF16)

            @pl.when(x > 0)
            def _():
                y_copy(c).wait_recv()

            wide = owner_hidden(c)
            out = xin[c].astype(F32) + nn(wide, wtv[x])
            yout[c] = out.astype(BF16)

            @pl.when(x < 3)
            def _():
                y_copy(c).start()

            @pl.when(x == 3)
            def _():
                y_cross(c).start()

            return carry

        lax.fori_loop(0, 2, clip, 0)

    def x_copy(j):
        return copy(bx.at[j], xin.at[mine], bx_send.at[j], x_recv.at[mine], base + j, D)

    def g_copy(j):
        return copy(bg.at[j + 1], gin.at[mine], go_send.at[j], gin_recv.at[mine], base + j, D)

    back_copy = copy(bg.at[0], bg.at[4], bg_send, bg_recv, lax.rem(S + 4, 8), far)

    @pl.when(end)
    def _():
        for i in range(1, 4):
            j = lax.rem(x + i, 4)
            for c in weight_copies(j, 0, 0):
                c.wait_recv()
            for c in share_copies(j, k):
                c.start()
        for i in range(1, 4):
            j = lax.rem(x + i, 4)
            for c in share_copies(j, 1 - k):
                c.wait_recv()

        @pl.when(half == 0)
        def _():
            bx[0] = by_height(cl[mine]).astype(BF16)

        @pl.when(half == 1)
        def _():
            y_cross(0).wait_recv()

        def layer(j, carry):
            @pl.when(half == 1)
            def _():
                @pl.when(j == x)
                def _():
                    xin[mine] = bx[j]

                @pl.when(j != x)
                def _():
                    x_copy(j).start()

            v = bx[j].astype(F32)
            hidden, slope = activate(space_forward(wide_space(v), wsv.at[j]))
            bact[j] = slope

            @pl.when(j < 3)
            def _():
                out = v + nn(wide_time(hidden), wtv[j])
                bx[j + 1] = out.astype(BF16)

            return carry

        lax.fori_loop(0, 4, layer, 0)

        @pl.when(half == 0)
        def _():
            back_copy.wait_recv()

        @pl.when(half == 1)
        def _():
            cot_copy.wait_recv()
            bg[4] = by_height(ct[...]).astype(BF16)

        def layer_back(i, carry):
            j = 3 - i

            @pl.when(j == x)
            def _():
                gin[mine] = bg[j + 1]

            @pl.when(j != x)
            def _():
                g_copy(j).start()

            @pl.when(j + half > 0)
            def _():
                g = bg[j + 1].astype(F32)
                g_pre = (g_hidden_of(g, wtv.at[j]) * bact[j]).astype(BF16).astype(F32)
                bg[j] = (g + space_backward(g_pre, wsv.at[j])).astype(BF16)

            return carry

        lax.fori_loop(0, 4, layer_back, 0)

        @pl.when(half == 1)
        def _():
            back_copy.start()

    @pl.when(half == 1)
    def _():
        def clip(c, carry):
            @pl.when(jnp.logical_not(jnp.logical_and(end, c == mine)))
            def _():
                y_copy(c).wait_recv()

            owner_hidden(c)
            return carry

        lax.fori_loop(0, 2, clip, 0)

    def clip_back(i, carry):
        c = jnp.where(i == 0, mine, 1 - mine)

        @pl.when(jnp.logical_not(jnp.logical_and(end, c == mine)))
        def _():
            copy(gin.at[c], gin.at[c], go_send.at[0], gin_recv.at[c], S, D).wait_recv()

        keep(gb, c, gin[c])
        g = gin[c].astype(F32)
        keep(gp, c, (g_hidden_of(g, wtv.at[x]) * act[c]).astype(BF16))
        return carry

    lax.fori_loop(0, 2, clip_back, 0)

    for q in range(3):
        lanes = slice(256 * q, 256 * q + 256)
        dw[SPACE + 256 * q : SPACE + 256 * q + 256, :] = tn(hc[:, lanes], gb[...])
        dw[256 * q : 256 * q + 256, :] = tn(xc[0:128, lanes], gp[128:256, :])
        dw[768 + 256 * q : 1024 + 256 * q, :] = tn(xc[:, lanes], gp[...])
        dw[1536 + 256 * q : 1792 + 256 * q, :] = tn(xc[128:256, lanes], gp[0:128, :])

    def pack(b, carry):
        top = dw[pl.ds(pl.multiple_of(b * 72, 8), 72), :]
        low = dw[pl.ds(pl.multiple_of(SPACE + b * 24, 8), 24), :]
        block = jnp.concatenate([top, low], axis=0).astype(BF16)
        part[0, b // 8, b % 8] = block[:, 0:128]
        part[1, b // 8, b % 8] = block[:, 128:256]
        return carry

    lax.fori_loop(0, 32, pack, 0)

    first = copy(part.at[1 - k], r1, r1_sem.at[0], r1_sem.at[1], S, sibling)
    first.start()
    first.wait_recv()

    def add_cores(b, carry):
        s1[b // 8, b % 8] = (part[k, b // 8, b % 8].astype(F32) + r1[b // 8, b % 8].astype(F32)).astype(BF16)
        return carry

    lax.fori_loop(0, 32, add_cores, 0)

    def y_step(i):
        to = lax.rem(y + i, 4)
        return copy(s1.at[to], r2.at[i - 1], r2_send.at[i - 1], r2_recv.at[i - 1], S, to * 16 + lax.rem(D, 16))

    for i in range(1, 4):
        y_step(i).start()
    for i in range(1, 4):
        y_step(i).wait_recv()

    def add_y(b, carry):
        total = s1[y, b].astype(F32) + r2[0, b].astype(F32) + r2[1, b].astype(F32) + r2[2, b].astype(F32)
        s2[b] = total.astype(BF16)
        return carry

    lax.fori_loop(0, 8, add_y, 0)

    def z_step(i):
        to = lax.rem(z + i, 8)
        return copy(s2.at[to], r3.at[i - 1], r3_send.at[i - 1], r3_recv.at[i - 1], S, y * 16 + to * 2 + k)

    for i in range(1, 8):
        z_step(i).start()
    for i in range(1, 8):
        z_step(i).wait_recv()

    total = s2[z].astype(F32)
    for i in range(7):
        total = total + r3[i].astype(F32)
    fin[k] = total * scale

    final = copy(fin.at[k], fin.at[k], r4_sem.at[0], r4_sem.at[1], S, sibling)
    final.start()
    final.wait_send()
    copy(fin.at[1 - k], fin.at[1 - k], r4_sem.at[0], r4_sem.at[1], S, sibling).wait_recv()

    for core in range(2):
        @pl.when(k == core)
        def _():
            for side in range(2):
                lanes = slice(128 * side, 128 * side + 128)
                out_s[:, lanes] = fin[side, 36 * core : 36 * core + 36, :]
                out_t[:, lanes] = fin[side, 72 + 12 * core : 84 + 12 * core, :]

    first.wait_send()
    for i in range(1, 4):
        y_step(i).wait_send()
    for i in range(1, 8):
        z_step(i).wait_send()
    for slot, target in enumerate((0, 3)):
        @pl.when(x != target)
        def _():
            for c in weight_copies(x, target, slot):
                c.wait_send()

    @pl.when(jnp.logical_or(S == 4, S == 7))
    def _():
        cot_copy.wait_send()

    @pl.when(half == 0)
    def _():
        for c in range(2):
            y_copy(c).wait_send()

    @pl.when(end)
    def _():
        for i in range(1, 4):
            j = lax.rem(x + i, 4)
            for c in share_copies(j, k):
                c.wait_send()
            g_copy(j).wait_send()

            @pl.when(half == 1)
            def _():
                x_copy(j).wait_send()

        @pl.when(half == 1)
        def _():
            back_copy.wait_send()


def body(clips, cotangent, spatial_kernel, temporal_kernel):
    micro = clips.shape[0]
    tile = clips.shape[1:]
    cells = tile[0] * tile[1] * tile[2]
    scale = 1.0 / math.sqrt(micro * lax.axis_size("dp") * cells)
    sem = pltpu.SemaphoreType.DMA
    vmem = pltpu.VMEM
    out_s, out_t = pl.pallas_call(
        functools.partial(kernel, scale),
        out_shape=(jax.ShapeDtypeStruct((36, C), F32), jax.ShapeDtypeStruct((12, C), F32)),
        in_specs=[pl.BlockSpec(memory_space=pl.ANY)] * 4,
        out_specs=(pl.BlockSpec(memory_space=pltpu.VMEM),) * 2,
        scratch_shapes=[
            vmem((4, SPACE, C), BF16),
            vmem((4, TIME, C), BF16),
            vmem((2, ROWS, C), BF16),
            vmem((ROWS, C), BF16),
            vmem((2, ROWS, C), BF16),
            vmem((2, ROWS, C), BF16),
            vmem((4, ROWS, C), BF16),
            vmem((5, ROWS, C), BF16),
            vmem((2, ROWS, C), BF16),
            vmem((2, ROWS, C), F32),
            vmem((4, ROWS, C), F32),
            vmem((2 * ROWS, 3 * C), BF16),
            vmem((2 * ROWS, 3 * C), BF16),
            vmem((2 * ROWS, C), BF16),
            vmem((2 * ROWS, C), BF16),
            vmem((SPACE + TIME, C), F32),
            vmem((2, 4, 8, 96, 128), BF16),
            vmem((4, 8, 96, 128), BF16),
            vmem((4, 8, 96, 128), BF16),
            vmem((3, 8, 96, 128), BF16),
            vmem((8, 96, 128), BF16),
            vmem((7, 96, 128), BF16),
            vmem((2, 96, 128), F32),
            sem((3,)),
            sem((2, 2)),
            sem((4, 2, 2)),
            sem((4, 2)),
            sem((2,)),
            sem((2,)),
            sem((4,)),
            sem,
            sem,
            sem,
            sem((4,)),
            sem((2,)),
            sem,
            sem,
            sem((2,)),
            sem((3,)),
            sem((3,)),
            sem((7,)),
            sem((7,)),
            sem((2,)),
        ],
        compiler_params=pltpu.CompilerParams(
            collective_id=0, has_side_effects=True, vmem_limit_bytes=40 << 20
        ),
        name="window",
    )(
        clips.reshape(micro, cells, tile[3]),
        cotangent.reshape(micro, cells, tile[3]),
        spatial_kernel[0],
        temporal_kernel[0],
    )
    return (out_s[None], out_t[None])


def solution(mesh):
    return jax.shard_map(
        body,
        mesh=mesh,
        in_specs=(
            P("dp", None, None, None, None),
            P("dp", None, None, None, None),
            P("section", None, None),
            P("section", None, None),
        ),
        out_specs=(P("section", "dp", None), P("section", "dp", None)),
        check_vma=False,
    )
```

```python
import functools
import math

import jax
import jax.numpy as jnp
from jax import lax
from jax.experimental import pallas as pl
from jax.experimental.pallas import tpu as pltpu
from jax.sharding import PartitionSpec as P

MESH = pl.DeviceIdType.MESH
F32 = jnp.float32
BF16 = jnp.bfloat16
C = 256
ROWS = 128
HALF = 64
SPACE = 9 * C
TIME = 3 * C


def by_height(v):
    v = v.astype(F32).reshape(8, 2, 8, C)
    return jnp.concatenate([v[:, 0].reshape(HALF, C), v[:, 1].reshape(HALF, C)], axis=0)


def columns(v):
    w = lax.broadcasted_iota(jnp.int32, v.shape, 0) & 7
    before = jnp.where(w == 0, 0.0, pltpu.roll(v, 1, 0))
    after = jnp.where(w == 7, 0.0, pltpu.roll(v, ROWS - 1, 0))
    return before, after


def frames(v):
    zero = jnp.zeros((8, C), F32)
    before = jnp.concatenate([zero, v[0:56], zero, v[64:120]], axis=0)
    after = jnp.concatenate([v[8:64], zero, v[72:128], zero], axis=0)
    return before, after


def nn(a, b):
    return jnp.dot(a, b, preferred_element_type=F32)


def nt(a, b):
    return lax.dot_general(a, b, (((1,), (1,)), ((), ())), preferred_element_type=F32)


def tn(a, b):
    return lax.dot_general(a, b, (((0,), (0,)), ((), ())), preferred_element_type=F32)


def wide_space(v):
    before, after = columns(v)
    return jnp.concatenate([before, v, after], axis=1).astype(BF16)


def wide_time(v):
    before, after = frames(v)
    return jnp.concatenate([before, v, after], axis=1).astype(BF16)


def space_forward(wide, w):
    same = nn(wide, w[768:1536, :])
    top = nn(wide[HALF:], w[1536:2304, :])
    bottom = nn(wide[:HALF], w[0:768, :])
    return same + jnp.concatenate([top, bottom], axis=0)


def activate(pre):
    sigma = jax.nn.sigmoid(pre)
    hidden = (pre * sigma).astype(BF16).astype(F32)
    return hidden, sigma * (1.0 + pre * (1.0 - sigma))


def g_hidden_of(g, w):
    before, after = frames(g)
    out = nt(after.astype(BF16), w[0:256, :])
    out = out + nt(g.astype(BF16), w[256:512, :])
    return out + nt(before.astype(BF16), w[512:768, :])


def space_backward(g_pre, w):
    before, after = columns(g_pre)
    same = top = bottom = None
    for q, v in enumerate((after, g_pre, before)):
        v = v.astype(BF16)
        a = nt(v, w[768 + 256 * q : 1024 + 256 * q, :])
        t = nt(v[HALF:], w[256 * q : 256 * q + 256, :])
        b = nt(v[:HALF], w[1536 + 256 * q : 1792 + 256 * q, :])
        same, top, bottom = (a, t, b) if same is None else (same + a, top + t, bottom + b)
    return same + jnp.concatenate([top, bottom], axis=0)


def kernel(
    scale,
    clips_ref, cot_ref, ws_ref, wt_ref,
    out_s, out_t,
    wsv, wtv, cl, ct, xin, yout, bx, bg, gin,
    act, bact, xc, hc, gp, gb, dw, part, r1, s1, r2, s2, r3, fin,
    loc, wg_send, wg_recv, ws_send, ws_recv, wy_send, wy_recv,
    x_send, x_recv, bx_send, bx_recv, ct_send, ct_recv,
    go_send, gin_recv, bg_send, bg_recv,
    r1_send, r1_recv, r2_send, r2_recv, r3_send, r3_recv, r4_sem,
):
    S = lax.axis_index("section")
    D = lax.axis_index("dp")
    half = S // 4
    x = S % 4
    y = D // 16
    z = (D // 2) % 8
    k = D % 2
    far = D + 8 - 16 * (z // 4)
    sibling = D + 1 - 2 * k
    end = jnp.logical_or(x == 0, x == 3)
    mine = jnp.where(x == 0, 1, 0)
    base = half * 4
    odd = y % 2
    lane = lax.rem(D, 16)
    above = lax.rem(y + 1, 4) * 16 + lane
    below = lax.rem(y + 3, 4) * 16 + lane

    def copy(src, dst, send, recv, section, dp):
        return pltpu.make_async_remote_copy(
            src_ref=src, dst_ref=dst, send_sem=send, recv_sem=recv,
            device_id={"section": section, "dp": dp}, device_id_type=MESH,
        )

    local = [
        pltpu.make_async_copy(clips_ref, cl, loc.at[0]),
        pltpu.make_async_copy(ws_ref, wsv.at[x], loc.at[1]),
        pltpu.make_async_copy(wt_ref, wtv.at[x], loc.at[2]),
    ]
    for c in local:
        c.start()

    barrier = pltpu.get_barrier_semaphore()

    def hello(section, dp):
        pl.semaphore_signal(
            barrier, inc=1, device_id={"section": section, "dp": dp}, device_id_type=MESH
        )

    hello(S, sibling)
    for i in range(1, 4):
        hello(S, lax.rem(y + i, 4) * 16 + lax.rem(D, 16))
        hello(base + lax.rem(x + i, 4), D)
    for i in range(1, 8):
        hello(S, y * 16 + lax.rem(z + i, 8) * 2 + k)

    @pl.when(S == 0)
    def _():
        hello(4, far)

    @pl.when(S == 3)
    def _():
        hello(4, far)
        hello(7, far)

    @pl.when(S == 4)
    def _():
        hello(0, far)
        hello(3, far)

    @pl.when(S == 7)
    def _():
        hello(3, far)

    crossings = jnp.where(end, 1, 0) + jnp.where(jnp.logical_or(S == 3, S == 4), 1, 0)
    pl.semaphore_wait(barrier, 14 + crossings)

    near = jnp.where(x % 2 == 1, 0, 3)

    def both(j, eighth, eighths, send, recv, section, dp, source=None):
        copies = []
        for i, (out, held) in enumerate(((ws_ref, wsv), (wt_ref, wtv))):
            step = held.shape[1] // 8
            rows = pl.ds(pl.multiple_of(eighth * step, 32), eighths * step)
            src = held.at[j, rows] if source is None else out.at[rows]
            copies.append(copy(src, held.at[j, rows], send.at[i], recv.at[i], section, dp))
        return copies

    def weight_copies(j, target, slot):
        return both(j, 4 * odd + 2 * k, 2, wg_send.at[slot], wg_recv.at[j], base + target, D, "out")

    def share_copies(j, i, core):
        if i == 0:
            return both(j, 4 * odd + 2 * core, 2, ws_send.at[j, 0], ws_recv.at[j, 0], S, sibling)
        return both(j, 4 - 4 * odd + 2 * core + i - 1, 1, ws_send.at[j, i], ws_recv.at[j, i], S, sibling)

    def y_copies(j, i, parity):
        return both(
            j, 4 * parity + 2 * k + i, 1, wy_send.at[j, i], wy_recv.at[j, i], S, above if i else below
        )

    def send_weights():
        for c in weight_copies(x, near, 0):
            c.start()

        @pl.when(jnp.logical_not(end))
        def _():
            for c in weight_copies(x, 3 - near, 1):
                c.start()

    @pl.when(half == 1)
    def _():
        send_weights()

    cot_copy = copy(cot_ref.at[mine], ct, ct_send, ct_recv, S, far)

    @pl.when(jnp.logical_or(S == 4, S == 7))
    def _():
        cot_copy.start()

    for c in local:
        c.wait()

    def rows_of(c, h):
        return pl.ds(pl.multiple_of(h * 128 + c * HALF, HALF), HALF)

    def keep(ref, c, value):
        ref[rows_of(c, 0), :] = value[:HALF]
        ref[rows_of(c, 1), :] = value[HALF:]

    def y_copy(c):
        return copy(yout.at[c], xin.at[c], x_send.at[c], x_recv.at[c], lax.rem(S + 1, 8), D)

    def y_cross(c):
        return copy(yout.at[c], bx.at[0], x_send.at[c], bx_recv, jnp.where(c == 0, 7, 4), far)

    def owner_hidden(c):
        wide = wide_space(xin[c].astype(F32))
        keep(xc, c, wide)
        hidden, slope = activate(space_forward(wide, wsv.at[x]))
        act[c] = slope
        wide = wide_time(hidden)
        keep(hc, c, wide)
        return wide

    @pl.when(half == 0)
    def _():
        def clip(c, carry):
            @pl.when(x == 0)
            def _():
                xin[c] = by_height(cl[c]).astype(BF16)

            @pl.when(x > 0)
            def _():
                y_copy(c).wait_recv()

            wide = owner_hidden(c)
            out = xin[c].astype(F32) + nn(wide, wtv[x])
            yout[c] = out.astype(BF16)

            @pl.when(x < 3)
            def _():
                y_copy(c).start()

            @pl.when(x == 3)
            def _():
                y_cross(c).start()

            return carry

        lax.fori_loop(0, 2, clip, 0)
        send_weights()

    def x_copy(j):
        return copy(bx.at[j], xin.at[mine], bx_send.at[j], x_recv.at[mine], base + j, D)

    def g_copy(j):
        return copy(bg.at[j + 1], gin.at[mine], go_send.at[j], gin_recv.at[mine], base + j, D)

    back_copy = copy(bg.at[0], bg.at[4], bg_send, bg_recv, lax.rem(S + 4, 8), far)

    @pl.when(end)
    def _():
        others = [jnp.where(x == 0, a, b) for a, b in ((1, 2), (3, 0), (2, 1))]
        for j in others:
            for c in weight_copies(j, 0, 0):
                c.wait_recv()
            for c in y_copies(j, 0, odd) + y_copies(j, 1, odd) + share_copies(j, 0, k):
                c.start()
        for j in others:
            for i in range(2):
                for c in y_copies(j, i, 1 - odd):
                    c.wait_recv()
                for c in share_copies(j, i + 1, k):
                    c.start()
        for j in others:
            for i in range(3):
                for c in share_copies(j, i, 1 - k):
                    c.wait_recv()

        @pl.when(half == 0)
        def _():
            bx[0] = by_height(cl[mine]).astype(BF16)

        @pl.when(half == 1)
        def _():
            y_cross(0).wait_recv()

        def layer(j, carry):
            @pl.when(half == 1)
            def _():
                @pl.when(j == x)
                def _():
                    xin[mine] = bx[j]

                @pl.when(j != x)
                def _():
                    x_copy(j).start()

            v = bx[j].astype(F32)
            hidden, slope = activate(space_forward(wide_space(v), wsv.at[j]))
            bact[j] = slope

            @pl.when(j < 3)
            def _():
                out = v + nn(wide_time(hidden), wtv[j])
                bx[j + 1] = out.astype(BF16)

            return carry

        lax.fori_loop(0, 4, layer, 0)

        @pl.when(half == 0)
        def _():
            back_copy.wait_recv()

        @pl.when(half == 1)
        def _():
            cot_copy.wait_recv()
            bg[4] = by_height(ct[...]).astype(BF16)

        def layer_back(i, carry):
            j = 3 - i

            @pl.when(j == x)
            def _():
                gin[mine] = bg[j + 1]

            @pl.when(j != x)
            def _():
                g_copy(j).start()

            @pl.when(j + half > 0)
            def _():
                g = bg[j + 1].astype(F32)
                g_pre = (g_hidden_of(g, wtv.at[j]) * bact[j]).astype(BF16).astype(F32)
                bg[j] = (g + space_backward(g_pre, wsv.at[j])).astype(BF16)

            return carry

        lax.fori_loop(0, 4, layer_back, 0)

        @pl.when(half == 1)
        def _():
            back_copy.start()

    @pl.when(half == 1)
    def _():
        def clip(c, carry):
            @pl.when(jnp.logical_not(jnp.logical_and(end, c == mine)))
            def _():
                y_copy(c).wait_recv()

            owner_hidden(c)
            return carry

        lax.fori_loop(0, 2, clip, 0)

    def clip_back(i, carry):
        c = jnp.where(i == 0, mine, 1 - mine)

        @pl.when(jnp.logical_not(jnp.logical_and(end, c == mine)))
        def _():
            copy(gin.at[c], gin.at[c], go_send.at[0], gin_recv.at[c], S, D).wait_recv()

        keep(gb, c, gin[c])
        g = gin[c].astype(F32)
        keep(gp, c, (g_hidden_of(g, wtv.at[x]) * act[c]).astype(BF16))
        return carry

    lax.fori_loop(0, 2, clip_back, 0)

    for q in range(3):
        lanes = slice(256 * q, 256 * q + 256)
        dw[SPACE + 256 * q : SPACE + 256 * q + 256, :] = tn(hc[:, lanes], gb[...])
        dw[256 * q : 256 * q + 256, :] = tn(xc[0:128, lanes], gp[128:256, :])
        dw[768 + 256 * q : 1024 + 256 * q, :] = tn(xc[:, lanes], gp[...])
        dw[1536 + 256 * q : 1792 + 256 * q, :] = tn(xc[128:256, lanes], gp[0:128, :])

    ahead = jnp.where(odd == k, 1, 3)
    blocks = [lax.rem(y + i, 4) for i in (2, 1, 3, 0)]
    forth = lax.rem(y + ahead, 4)
    back = lax.rem(y + 4 - ahead, 4)

    def core_step(i, column):
        yb = blocks[i]
        return copy(part.at[column, yb], r1.at[yb], r1_send.at[i], r1_recv.at[i], S, sibling)

    for i in range(4):
        def pack(b, carry):
            n = blocks[i] * 8 + b
            top = dw[pl.ds(pl.multiple_of(n * 72, 8), 72), :]
            low = dw[pl.ds(pl.multiple_of(SPACE + n * 24, 8), 24), :]
            block = jnp.concatenate([top, low], axis=0).astype(BF16)
            part[0, blocks[i], b] = block[:, 0:128]
            part[1, blocks[i], b] = block[:, 128:256]
            return carry

        lax.fori_loop(0, 8, pack, 0)
        core_step(i, 1 - k).start()

    def add_cores(yb):
        def one(b, carry):
            s1[yb, b] = (part[k, yb, b].astype(F32) + r1[yb, b].astype(F32)).astype(BF16)
            return carry

        lax.fori_loop(0, 8, one, 0)

    def y_step(i):
        return copy(
            s1.at[(blocks[0], forth, back)[i]], r2.at[i], r2_send.at[i], r2_recv.at[i],
            S, (forth, forth, back)[i] * 16 + lane,
        )

    core_step(0, k).wait_recv()
    add_cores(blocks[0])
    y_step(0).start()
    core_step(1, k).wait_recv()
    core_step(2, k).wait_recv()
    add_cores(forth)
    y_step(1).start()
    y_step(0).wait_recv()

    def add_relayed(b, carry):
        total = part[k, back, b].astype(F32) + r1[back, b].astype(F32) + r2[0, b].astype(F32)
        s1[back, b] = total.astype(BF16)
        return carry

    lax.fori_loop(0, 8, add_relayed, 0)
    y_step(2).start()
    core_step(3, k).wait_recv()
    y_step(1).wait_recv()
    y_step(2).wait_recv()
    def add_y(b, carry):
        total = part[k, y, b].astype(F32) + r1[y, b].astype(F32) + r2[1, b].astype(F32) + r2[2, b].astype(F32)
        s2[b] = total.astype(BF16)
        return carry

    lax.fori_loop(0, 8, add_y, 0)

    def z_step(i):
        to = lax.rem(z + i, 8)
        return copy(s2.at[to], r3.at[i - 1], r3_send.at[i - 1], r3_recv.at[i - 1], S, y * 16 + to * 2 + k)

    for i in range(1, 8):
        z_step(i).start()
    for i in range(1, 8):
        z_step(i).wait_recv()

    total = s2[z].astype(F32)
    for i in range(7):
        total = total + r3[i].astype(F32)
    fin[k] = total * scale

    final = copy(fin.at[k], fin.at[k], r4_sem.at[0], r4_sem.at[1], S, sibling)
    final.start()
    final.wait_send()
    copy(fin.at[1 - k], fin.at[1 - k], r4_sem.at[0], r4_sem.at[1], S, sibling).wait_recv()

    for core in range(2):
        @pl.when(k == core)
        def _():
            for side in range(2):
                lanes = slice(128 * side, 128 * side + 128)
                out_s[:, lanes] = fin[side, 36 * core : 36 * core + 36, :]
                out_t[:, lanes] = fin[side, 72 + 12 * core : 84 + 12 * core, :]

    for i in range(4):
        core_step(i, 1 - k).wait_send()
    for i in range(3):
        y_step(i).wait_send()
    for i in range(1, 8):
        z_step(i).wait_send()
    for c in weight_copies(x, near, 0):
        c.wait_send()

    @pl.when(jnp.logical_not(end))
    def _():
        for c in weight_copies(x, 3 - near, 1):
            c.wait_send()

    @pl.when(jnp.logical_or(S == 4, S == 7))
    def _():
        cot_copy.wait_send()

    @pl.when(half == 0)
    def _():
        for c in range(2):
            y_copy(c).wait_send()

    @pl.when(end)
    def _():
        for i in range(1, 4):
            j = lax.rem(x + i, 4)
            for c in y_copies(j, 0, odd) + y_copies(j, 1, odd):
                c.wait_send()
            for n in range(3):
                for c in share_copies(j, n, k):
                    c.wait_send()
            g_copy(j).wait_send()

            @pl.when(half == 1)
            def _():
                x_copy(j).wait_send()

        @pl.when(half == 1)
        def _():
            back_copy.wait_send()


def body(clips, cotangent, spatial_kernel, temporal_kernel):
    micro = clips.shape[0]
    tile = clips.shape[1:]
    cells = tile[0] * tile[1] * tile[2]
    scale = 1.0 / math.sqrt(micro * lax.axis_size("dp") * cells)
    sem = pltpu.SemaphoreType.DMA
    vmem = pltpu.VMEM
    out_s, out_t = pl.pallas_call(
        functools.partial(kernel, scale),
        out_shape=(jax.ShapeDtypeStruct((36, C), F32), jax.ShapeDtypeStruct((12, C), F32)),
        in_specs=[pl.BlockSpec(memory_space=pltpu.HBM)] * 4,
        out_specs=(pl.BlockSpec(memory_space=pltpu.VMEM),) * 2,
        scratch_shapes=[
            vmem((4, SPACE, C), BF16),
            vmem((4, TIME, C), BF16),
            vmem((2, ROWS, C), BF16),
            vmem((ROWS, C), BF16),
            vmem((2, ROWS, C), BF16),
            vmem((2, ROWS, C), BF16),
            vmem((4, ROWS, C), BF16),
            vmem((5, ROWS, C), BF16),
            vmem((2, ROWS, C), BF16),
            vmem((2, ROWS, C), F32),
            vmem((4, ROWS, C), F32),
            vmem((2 * ROWS, 3 * C), BF16),
            vmem((2 * ROWS, 3 * C), BF16),
            vmem((2 * ROWS, C), BF16),
            vmem((2 * ROWS, C), BF16),
            vmem((SPACE + TIME, C), F32),
            vmem((2, 4, 8, 96, 128), BF16),
            vmem((4, 8, 96, 128), BF16),
            vmem((4, 8, 96, 128), BF16),
            vmem((3, 8, 96, 128), BF16),
            vmem((8, 96, 128), BF16),
            vmem((7, 96, 128), BF16),
            vmem((2, 96, 128), F32),
            sem((3,)),
            sem((2, 2)),
            sem((4, 2)),
            sem((4, 3, 2)),
            sem((4, 3, 2)),
            sem((4, 2, 2)),
            sem((4, 2, 2)),
            sem((2,)),
            sem((2,)),
            sem((4,)),
            sem,
            sem,
            sem,
            sem((4,)),
            sem((2,)),
            sem,
            sem,
            sem((4,)),
            sem((4,)),
            sem((3,)),
            sem((3,)),
            sem((7,)),
            sem((7,)),
            sem((2,)),
        ],
        compiler_params=pltpu.CompilerParams(
            collective_id=0, has_side_effects=True, vmem_limit_bytes=66_900_000
        ),
        name="window",
    )(
        clips.reshape(micro, cells, tile[3]),
        cotangent.reshape(micro, cells, tile[3]),
        spatial_kernel[0],
        temporal_kernel[0],
    )
    return (out_s[None], out_t[None])


def solution(mesh):
    return jax.shard_map(
        body,
        mesh=mesh,
        in_specs=(
            P("dp", None, None, None, None),
            P("dp", None, None, None, None),
            P("section", None, None),
            P("section", None, None),
        ),
        out_specs=(P("section", "dp", None), P("section", "dp", None)),
        check_vma=False,
    )
```

```python
import functools
import math

import jax
import jax.numpy as jnp
from jax import lax
from jax.experimental import pallas as pl
from jax.experimental.pallas import tpu as pltpu
from jax.sharding import PartitionSpec as P

MESH = pl.DeviceIdType.MESH
F32 = jnp.float32
BF16 = jnp.bfloat16
C = 256
ROWS = 128
HALF = 64
SPACE = 9 * C
TIME = 3 * C


def by_height(v):
    v = v.astype(F32).reshape(8, 2, 8, C)
    return jnp.concatenate([v[:, 0].reshape(HALF, C), v[:, 1].reshape(HALF, C)], axis=0)


def columns(v):
    w = lax.broadcasted_iota(jnp.int32, v.shape, 0) & 7
    before = jnp.where(w == 0, 0.0, pltpu.roll(v, 1, 0))
    after = jnp.where(w == 7, 0.0, pltpu.roll(v, ROWS - 1, 0))
    return before, after


def frames(v):
    zero = jnp.zeros((8, C), F32)
    before = jnp.concatenate([zero, v[0:56], zero, v[64:120]], axis=0)
    after = jnp.concatenate([v[8:64], zero, v[72:128], zero], axis=0)
    return before, after


def nn(a, b):
    return jnp.dot(a, b, preferred_element_type=F32)


def nt(a, b):
    return lax.dot_general(a, b, (((1,), (1,)), ((), ())), preferred_element_type=F32)


def tn(a, b):
    return lax.dot_general(a, b, (((0,), (0,)), ((), ())), preferred_element_type=F32)


def wide_space(v):
    before, after = columns(v)
    return jnp.concatenate([before, v, after], axis=1).astype(BF16)


def wide_time(v):
    before, after = frames(v)
    return jnp.concatenate([before, v, after], axis=1).astype(BF16)


def space_forward(wide, w):
    same = nn(wide, w[768:1536, :])
    top = nn(wide[HALF:], w[1536:2304, :])
    bottom = nn(wide[:HALF], w[0:768, :])
    return same + jnp.concatenate([top, bottom], axis=0)


def activate(pre):
    sigma = jax.nn.sigmoid(pre)
    hidden = (pre * sigma).astype(BF16).astype(F32)
    return hidden, sigma * (1.0 + pre * (1.0 - sigma))


def g_hidden_of(g, w):
    before, after = frames(g)
    out = nt(after.astype(BF16), w[0:256, :])
    out = out + nt(g.astype(BF16), w[256:512, :])
    return out + nt(before.astype(BF16), w[512:768, :])


def space_backward(g_pre, w):
    before, after = columns(g_pre)
    same = top = bottom = None
    for q, v in enumerate((after, g_pre, before)):
        v = v.astype(BF16)
        a = nt(v, w[768 + 256 * q : 1024 + 256 * q, :])
        t = nt(v[HALF:], w[256 * q : 256 * q + 256, :])
        b = nt(v[:HALF], w[1536 + 256 * q : 1792 + 256 * q, :])
        same, top, bottom = (a, t, b) if same is None else (same + a, top + t, bottom + b)
    return same + jnp.concatenate([top, bottom], axis=0)


def kernel(
    scale,
    clips_ref, cot_ref, ws_ref, wt_ref,
    out_s, out_t,
    wsv, wtv, cl, ct, xin, yout, bx, bg, gin,
    act, bact, xc, hc, gp, gb, dw, part, r1, s1, r2, s2, r3, fin,
    loc, wg_send, wg_recv, ws_send, ws_recv, wy_send, wy_recv,
    x_send, x_recv, bx_send, bx_recv, ct_send, ct_recv,
    go_send, gin_recv, bg_send, bg_recv,
    r1_send, r1_recv, r2_send, r2_recv, r3_send, r3_recv, r4_sem,
):
    S = lax.axis_index("section")
    D = lax.axis_index("dp")
    half = S // 4
    x = S % 4
    y = D // 16
    z = (D // 2) % 8
    k = D % 2
    far = D + 8 - 16 * (z // 4)
    sibling = D + 1 - 2 * k
    end = jnp.logical_or(x == 0, x == 3)
    mine = jnp.where(x == 0, 1, 0)
    base = half * 4
    odd = y % 2
    lane = lax.rem(D, 16)
    above = lax.rem(y + 1, 4) * 16 + lane
    below = lax.rem(y + 3, 4) * 16 + lane

    def copy(src, dst, send, recv, section, dp):
        return pltpu.make_async_remote_copy(
            src_ref=src, dst_ref=dst, send_sem=send, recv_sem=recv,
            device_id={"section": section, "dp": dp}, device_id_type=MESH,
        )

    local = [
        pltpu.make_async_copy(clips_ref, cl, loc.at[0]),
        pltpu.make_async_copy(ws_ref, wsv.at[x], loc.at[1]),
        pltpu.make_async_copy(wt_ref, wtv.at[x], loc.at[2]),
    ]
    for c in local:
        c.start()

    barrier = pltpu.get_barrier_semaphore()

    def hello(section, dp):
        pl.semaphore_signal(
            barrier, inc=1, device_id={"section": section, "dp": dp}, device_id_type=MESH
        )

    hello(S, sibling)
    for i in range(1, 4):
        hello(S, lax.rem(y + i, 4) * 16 + lax.rem(D, 16))
        hello(base + lax.rem(x + i, 4), D)
    for i in range(1, 8):
        hello(S, y * 16 + lax.rem(z + i, 8) * 2 + k)

    @pl.when(S == 0)
    def _():
        hello(4, far)

    @pl.when(S == 3)
    def _():
        hello(4, far)
        hello(7, far)

    @pl.when(S == 4)
    def _():
        hello(0, far)
        hello(3, far)

    @pl.when(S == 7)
    def _():
        hello(3, far)

    crossings = jnp.where(end, 1, 0) + jnp.where(jnp.logical_or(S == 3, S == 4), 1, 0)
    pl.semaphore_wait(barrier, 14 + crossings)

    near = jnp.where(x % 2 == 1, 0, 3)

    def both(j, eighth, eighths, send, recv, section, dp, source=None):
        copies = []
        for i, (out, held) in enumerate(((ws_ref, wsv), (wt_ref, wtv))):
            step = held.shape[1] // 8
            rows = pl.ds(pl.multiple_of(eighth * step, 32), eighths * step)
            src = held.at[j, rows] if source is None else out.at[rows]
            copies.append(copy(src, held.at[j, rows], send.at[i], recv.at[i], section, dp))
        return copies

    def weight_copies(j, target, slot):
        return both(j, 4 * odd + 2 * k, 2, wg_send.at[slot], wg_recv.at[j], base + target, D, "out")

    def share_copies(j, i, core):
        if i == 0:
            return both(j, 4 * odd + 2 * core, 2, ws_send.at[j, 0], ws_recv.at[j, 0], S, sibling)
        return both(j, 4 - 4 * odd + 2 * core + i - 1, 1, ws_send.at[j, i], ws_recv.at[j, i], S, sibling)

    def y_copies(j, i, parity):
        return both(
            j, 4 * parity + 2 * k + i, 1, wy_send.at[j, i], wy_recv.at[j, i], S, above if i else below
        )

    passed = jnp.where(x % 2 == 0, 1, 2)
    passes = jnp.where(end, k == 0, k == 1)
    middle = jnp.logical_and(jnp.logical_not(end), k == 1)

    def pass_copies():
        return both(passed, 4 * odd + 2 * k, 2, wg_send.at[2], wg_recv.at[passed], base + near, D)

    def send_near():
        for c in weight_copies(x, near, 0):
            c.start()

    def pass_middle():
        @pl.when(middle)
        def _():
            for c in weight_copies(passed, near, 0):
                c.wait_recv()
            for c in pass_copies():
                c.start()

    @pl.when(S != 2)
    def _():
        send_near()

    @pl.when(middle)
    def _():
        for c in weight_copies(x, 3 - x, 1):
            c.start()

    @pl.when(half == 1)
    def _():
        pass_middle()

    cot_copy = copy(cot_ref.at[mine], ct, ct_send, ct_recv, S, far)

    @pl.when(jnp.logical_or(S == 4, S == 7))
    def _():
        cot_copy.start()

    for c in local:
        c.wait()

    def rows_of(c, h):
        return pl.ds(pl.multiple_of(h * 128 + c * HALF, HALF), HALF)

    def keep(ref, c, value):
        ref[rows_of(c, 0), :] = value[:HALF]
        ref[rows_of(c, 1), :] = value[HALF:]

    def y_copy(c):
        return copy(yout.at[c], xin.at[c], x_send.at[c], x_recv.at[c], lax.rem(S + 1, 8), D)

    def y_cross(c):
        return copy(yout.at[c], bx.at[0], x_send.at[c], bx_recv, jnp.where(c == 0, 7, 4), far)

    def owner_hidden(c):
        wide = wide_space(xin[c].astype(F32))
        keep(xc, c, wide)
        hidden, slope = activate(space_forward(wide, wsv.at[x]))
        act[c] = slope
        wide = wide_time(hidden)
        keep(hc, c, wide)
        return wide

    @pl.when(half == 0)
    def _():
        def clip(c, carry):
            @pl.when(x == 0)
            def _():
                xin[c] = by_height(cl[c]).astype(BF16)

            @pl.when(x > 0)
            def _():
                y_copy(c).wait_recv()

            wide = owner_hidden(c)
            out = xin[c].astype(F32) + nn(wide, wtv[x])
            yout[c] = out.astype(BF16)

            @pl.when(x < 3)
            def _():
                y_copy(c).start()

            @pl.when(x == 3)
            def _():
                y_cross(c).start()

            return carry

        lax.fori_loop(0, 2, clip, 0)

        @pl.when(x == 2)
        def _():
            send_near()

        pass_middle()

    def x_copy(j):
        return copy(bx.at[j], xin.at[mine], bx_send.at[j], x_recv.at[mine], base + j, D)

    def g_copy(j):
        return copy(bg.at[j + 1], gin.at[mine], go_send.at[j], gin_recv.at[mine], base + j, D)

    back_copy = copy(bg.at[0], bg.at[4], bg_send, bg_recv, lax.rem(S + 4, 8), far)

    @pl.when(end)
    def _():
        others = [jnp.where(x == 0, a, b) for a, b in ((1, 0), (3, 2), (2, 1))]
        for j in others:
            for c in weight_copies(j, 0, 0):
                c.wait_recv()
            for c in y_copies(j, 0, odd) + y_copies(j, 1, odd) + share_copies(j, 0, k):
                c.start()

            @pl.when(jnp.logical_and(j == passed, k == 0))
            def _():
                for c in pass_copies():
                    c.start()

        for j in others:
            for i in range(2):
                for c in y_copies(j, i, 1 - odd):
                    c.wait_recv()
                for c in share_copies(j, i + 1, k):
                    c.start()
        for j in others:
            for i in range(3):
                for c in share_copies(j, i, 1 - k):
                    c.wait_recv()

        @pl.when(half == 0)
        def _():
            bx[0] = by_height(cl[mine]).astype(BF16)

        @pl.when(half == 1)
        def _():
            y_cross(0).wait_recv()

        def layer(j, carry):
            @pl.when(half == 1)
            def _():
                @pl.when(j == x)
                def _():
                    xin[mine] = bx[j]

                @pl.when(j != x)
                def _():
                    x_copy(j).start()

            v = bx[j].astype(F32)
            hidden, slope = activate(space_forward(wide_space(v), wsv.at[j]))
            bact[j] = slope

            @pl.when(j < 3)
            def _():
                out = v + nn(wide_time(hidden), wtv[j])
                bx[j + 1] = out.astype(BF16)

            return carry

        lax.fori_loop(0, 4, layer, 0)

        @pl.when(half == 0)
        def _():
            back_copy.wait_recv()

        @pl.when(half == 1)
        def _():
            cot_copy.wait_recv()
            bg[4] = by_height(ct[...]).astype(BF16)

        def layer_back(i, carry):
            j = 3 - i

            @pl.when(j == x)
            def _():
                gin[mine] = bg[j + 1]

            @pl.when(j != x)
            def _():
                g_copy(j).start()

            @pl.when(j + half > 0)
            def _():
                g = bg[j + 1].astype(F32)
                g_pre = (g_hidden_of(g, wtv.at[j]) * bact[j]).astype(BF16).astype(F32)
                bg[j] = (g + space_backward(g_pre, wsv.at[j])).astype(BF16)

            return carry

        lax.fori_loop(0, 4, layer_back, 0)

        @pl.when(half == 1)
        def _():
            back_copy.start()

    @pl.when(half == 1)
    def _():
        def clip(c, carry):
            @pl.when(jnp.logical_not(jnp.logical_and(end, c == mine)))
            def _():
                y_copy(c).wait_recv()

            owner_hidden(c)
            return carry

        lax.fori_loop(0, 2, clip, 0)

    def clip_back(i, carry):
        c = jnp.where(i == 0, mine, 1 - mine)

        @pl.when(jnp.logical_not(jnp.logical_and(end, c == mine)))
        def _():
            copy(gin.at[c], gin.at[c], go_send.at[0], gin_recv.at[c], S, D).wait_recv()

        keep(gb, c, gin[c])
        g = gin[c].astype(F32)
        keep(gp, c, (g_hidden_of(g, wtv.at[x]) * act[c]).astype(BF16))
        return carry

    lax.fori_loop(0, 2, clip_back, 0)

    for q in range(3):
        lanes = slice(256 * q, 256 * q + 256)
        dw[SPACE + 256 * q : SPACE + 256 * q + 256, :] = tn(hc[:, lanes], gb[...])
        dw[256 * q : 256 * q + 256, :] = tn(xc[0:128, lanes], gp[128:256, :])
        dw[768 + 256 * q : 1024 + 256 * q, :] = tn(xc[:, lanes], gp[...])
        dw[1536 + 256 * q : 1792 + 256 * q, :] = tn(xc[128:256, lanes], gp[0:128, :])

    ahead = jnp.where(odd == k, 1, 3)
    blocks = [lax.rem(y + i, 4) for i in (2, 1, 3, 0)]
    forth = lax.rem(y + ahead, 4)
    back = lax.rem(y + 4 - ahead, 4)

    def core_step(i, column):
        yb = blocks[i]
        return copy(part.at[column, yb], r1.at[yb], r1_send.at[i], r1_recv.at[i], S, sibling)

    for i in range(4):
        def pack(b, carry):
            n = blocks[i] * 8 + b
            top = dw[pl.ds(pl.multiple_of(n * 72, 8), 72), :]
            low = dw[pl.ds(pl.multiple_of(SPACE + n * 24, 8), 24), :]
            block = jnp.concatenate([top, low], axis=0).astype(BF16)
            part[0, blocks[i], b] = block[:, 0:128]
            part[1, blocks[i], b] = block[:, 128:256]
            return carry

        lax.fori_loop(0, 8, pack, 0)
        core_step(i, 1 - k).start()

    def add_cores(yb):
        def one(b, carry):
            s1[yb, b] = (part[k, yb, b].astype(F32) + r1[yb, b].astype(F32)).astype(BF16)
            return carry

        lax.fori_loop(0, 8, one, 0)

    def y_step(i):
        return copy(
            s1.at[(blocks[0], forth, back)[i]], r2.at[i], r2_send.at[i], r2_recv.at[i],
            S, (forth, forth, back)[i] * 16 + lane,
        )

    core_step(0, k).wait_recv()
    add_cores(blocks[0])
    y_step(0).start()
    core_step(1, k).wait_recv()
    core_step(2, k).wait_recv()
    add_cores(forth)
    y_step(1).start()
    y_step(0).wait_recv()

    def add_relayed(b, carry):
        total = part[k, back, b].astype(F32) + r1[back, b].astype(F32) + r2[0, b].astype(F32)
        s1[back, b] = total.astype(BF16)
        return carry

    lax.fori_loop(0, 8, add_relayed, 0)
    y_step(2).start()
    core_step(3, k).wait_recv()
    y_step(1).wait_recv()
    y_step(2).wait_recv()
    def add_y(b, carry):
        total = part[k, y, b].astype(F32) + r1[y, b].astype(F32) + r2[1, b].astype(F32) + r2[2, b].astype(F32)
        s2[b] = total.astype(BF16)
        return carry

    lax.fori_loop(0, 8, add_y, 0)

    def z_step(i):
        to = lax.rem(z + i, 8)
        return copy(s2.at[to], r3.at[i - 1], r3_send.at[i - 1], r3_recv.at[i - 1], S, y * 16 + to * 2 + k)

    for i in range(1, 8):
        z_step(i).start()
    for i in range(1, 8):
        z_step(i).wait_recv()

    total = s2[z].astype(F32)
    for i in range(7):
        total = total + r3[i].astype(F32)
    fin[k] = total * scale

    final = copy(fin.at[k], fin.at[k], r4_sem.at[0], r4_sem.at[1], S, sibling)
    final.start()
    final.wait_send()
    copy(fin.at[1 - k], fin.at[1 - k], r4_sem.at[0], r4_sem.at[1], S, sibling).wait_recv()

    for core in range(2):
        @pl.when(k == core)
        def _():
            for side in range(2):
                lanes = slice(128 * side, 128 * side + 128)
                out_s[:, lanes] = fin[side, 36 * core : 36 * core + 36, :]
                out_t[:, lanes] = fin[side, 72 + 12 * core : 84 + 12 * core, :]

    for i in range(4):
        core_step(i, 1 - k).wait_send()
    for i in range(3):
        y_step(i).wait_send()
    for i in range(1, 8):
        z_step(i).wait_send()
    for c in weight_copies(x, near, 0):
        c.wait_send()

    @pl.when(middle)
    def _():
        for c in weight_copies(x, 3 - x, 1):
            c.wait_send()

    @pl.when(passes)
    def _():
        for c in pass_copies():
            c.wait_send()

    @pl.when(jnp.logical_or(S == 4, S == 7))
    def _():
        cot_copy.wait_send()

    @pl.when(half == 0)
    def _():
        for c in range(2):
            y_copy(c).wait_send()

    @pl.when(end)
    def _():
        for i in range(1, 4):
            j = lax.rem(x + i, 4)
            for c in y_copies(j, 0, odd) + y_copies(j, 1, odd):
                c.wait_send()
            for n in range(3):
                for c in share_copies(j, n, k):
                    c.wait_send()
            g_copy(j).wait_send()

            @pl.when(half == 1)
            def _():
                x_copy(j).wait_send()

        @pl.when(half == 1)
        def _():
            back_copy.wait_send()


def body(clips, cotangent, spatial_kernel, temporal_kernel):
    micro = clips.shape[0]
    tile = clips.shape[1:]
    cells = tile[0] * tile[1] * tile[2]
    scale = 1.0 / math.sqrt(micro * lax.axis_size("dp") * cells)
    sem = pltpu.SemaphoreType.DMA
    vmem = pltpu.VMEM
    out_s, out_t = pl.pallas_call(
        functools.partial(kernel, scale),
        out_shape=(jax.ShapeDtypeStruct((36, C), F32), jax.ShapeDtypeStruct((12, C), F32)),
        in_specs=[pl.BlockSpec(memory_space=pltpu.HBM)] * 4,
        out_specs=(pl.BlockSpec(memory_space=pltpu.VMEM),) * 2,
        scratch_shapes=[
            vmem((4, SPACE, C), BF16),
            vmem((4, TIME, C), BF16),
            vmem((2, ROWS, C), BF16),
            vmem((ROWS, C), BF16),
            vmem((2, ROWS, C), BF16),
            vmem((2, ROWS, C), BF16),
            vmem((4, ROWS, C), BF16),
            vmem((5, ROWS, C), BF16),
            vmem((2, ROWS, C), BF16),
            vmem((2, ROWS, C), F32),
            vmem((4, ROWS, C), F32),
            vmem((2 * ROWS, 3 * C), BF16),
            vmem((2 * ROWS, 3 * C), BF16),
            vmem((2 * ROWS, C), BF16),
            vmem((2 * ROWS, C), BF16),
            vmem((SPACE + TIME, C), F32),
            vmem((2, 4, 8, 96, 128), BF16),
            vmem((4, 8, 96, 128), BF16),
            vmem((4, 8, 96, 128), BF16),
            vmem((3, 8, 96, 128), BF16),
            vmem((8, 96, 128), BF16),
            vmem((7, 96, 128), BF16),
            vmem((2, 96, 128), F32),
            sem((3,)),
            sem((3, 2)),
            sem((4, 2)),
            sem((4, 3, 2)),
            sem((4, 3, 2)),
            sem((4, 2, 2)),
            sem((4, 2, 2)),
            sem((2,)),
            sem((2,)),
            sem((4,)),
            sem,
            sem,
            sem,
            sem((4,)),
            sem((2,)),
            sem,
            sem,
            sem((4,)),
            sem((4,)),
            sem((3,)),
            sem((3,)),
            sem((7,)),
            sem((7,)),
            sem((2,)),
        ],
        compiler_params=pltpu.CompilerParams(
            collective_id=0, has_side_effects=True, vmem_limit_bytes=66_900_000
        ),
        name="window",
    )(
        clips.reshape(micro, cells, tile[3]),
        cotangent.reshape(micro, cells, tile[3]),
        spatial_kernel[0],
        temporal_kernel[0],
    )
    return (out_s[None], out_t[None])


def solution(mesh):
    return jax.shard_map(
        body,
        mesh=mesh,
        in_specs=(
            P("dp", None, None, None, None),
            P("dp", None, None, None, None),
            P("section", None, None),
            P("section", None, None),
        ),
        out_specs=(P("section", "dp", None), P("section", "dp", None)),
        check_vma=False,
    )
```

```python
import functools
import math

import jax
import jax.numpy as jnp
from jax import lax
from jax.experimental import pallas as pl
from jax.experimental.pallas import tpu as pltpu
from jax.sharding import PartitionSpec as P

MESH = pl.DeviceIdType.MESH
F32 = jnp.float32
BF16 = jnp.bfloat16
C = 256
ROWS = 128
HALF = 64
SPACE = 9 * C
TIME = 3 * C


def by_height(v):
    v = v.astype(F32).reshape(8, 2, 8, C)
    return jnp.concatenate([v[:, 0].reshape(HALF, C), v[:, 1].reshape(HALF, C)], axis=0)


def columns(v):
    w = lax.broadcasted_iota(jnp.int32, v.shape, 0) & 7
    before = jnp.where(w == 0, 0.0, pltpu.roll(v, 1, 0))
    after = jnp.where(w == 7, 0.0, pltpu.roll(v, ROWS - 1, 0))
    return before, after


def frames(v):
    zero = jnp.zeros((8, C), F32)
    before = jnp.concatenate([zero, v[0:56], zero, v[64:120]], axis=0)
    after = jnp.concatenate([v[8:64], zero, v[72:128], zero], axis=0)
    return before, after


def nn(a, b):
    return jnp.dot(a, b, preferred_element_type=F32)


def nt(a, b):
    return lax.dot_general(a, b, (((1,), (1,)), ((), ())), preferred_element_type=F32)


def tn(a, b):
    return lax.dot_general(a, b, (((0,), (0,)), ((), ())), preferred_element_type=F32)


def wide_space(v):
    before, after = columns(v)
    return jnp.concatenate([before, v, after], axis=1).astype(BF16)


def wide_time(v):
    before, after = frames(v)
    return jnp.concatenate([before, v, after], axis=1).astype(BF16)


def space_forward(wide, w):
    same = nn(wide, w[768:1536, :])
    top = nn(wide[HALF:], w[1536:2304, :])
    bottom = nn(wide[:HALF], w[0:768, :])
    return same + jnp.concatenate([top, bottom], axis=0)


def activate(pre):
    sigma = jax.nn.sigmoid(pre)
    hidden = (pre * sigma).astype(BF16).astype(F32)
    return hidden, sigma * (1.0 + pre * (1.0 - sigma))


def g_hidden_of(g, w):
    before, after = frames(g)
    out = nt(after.astype(BF16), w[SPACE : SPACE + 256, :])
    out = out + nt(g.astype(BF16), w[SPACE + 256 : SPACE + 512, :])
    return out + nt(before.astype(BF16), w[SPACE + 512 : SPACE + 768, :])


def space_backward(g_pre, w):
    before, after = columns(g_pre)
    same = top = bottom = None
    for q, v in enumerate((after, g_pre, before)):
        v = v.astype(BF16)
        a = nt(v, w[768 + 256 * q : 1024 + 256 * q, :])
        t = nt(v[HALF:], w[256 * q : 256 * q + 256, :])
        b = nt(v[:HALF], w[1536 + 256 * q : 1792 + 256 * q, :])
        same, top, bottom = (a, t, b) if same is None else (same + a, top + t, bottom + b)
    return same + jnp.concatenate([top, bottom], axis=0)


def kernel(
    scale,
    clips_ref, cot_ref, ws_ref, wt_ref,
    out_s, out_t,
    wv, cl, ct, xin, yout, bx, bg, gin,
    act, bact, xc, hc, gp, gb, dw, part, r1, s1, r2, s2, r3, fin,
    loc, wg_send, wg_recv, ws_send, ws_recv, wy_send, wy_recv,
    x_send, x_recv, bx_send, bx_recv, ct_send, ct_recv,
    go_send, gin_recv, bg_send, bg_recv,
    r1_send, r1_recv, r2_send, r2_recv, r3_send, r3_recv, r4_sem,
):
    S = lax.axis_index("section")
    D = lax.axis_index("dp")
    half = S // 4
    x = S % 4
    y = D // 16
    z = (D // 2) % 8
    k = D % 2
    far = D + 8 - 16 * (z // 4)
    sibling = D + 1 - 2 * k
    end = jnp.logical_or(x == 0, x == 3)
    mine = jnp.where(x == 0, 1, 0)
    base = half * 4
    odd = y % 2
    lane = lax.rem(D, 16)
    above = lax.rem(y + 1, 4) * 16 + lane
    below = lax.rem(y + 3, 4) * 16 + lane

    def copy(src, dst, send, recv, section, dp):
        return pltpu.make_async_remote_copy(
            src_ref=src, dst_ref=dst, send_sem=send, recv_sem=recv,
            device_id={"section": section, "dp": dp}, device_id_type=MESH,
        )

    local = [
        pltpu.make_async_copy(clips_ref, cl, loc.at[0]),
        pltpu.make_async_copy(ws_ref, wv.at[x, 0:SPACE], loc.at[1]),
        pltpu.make_async_copy(wt_ref, wv.at[x, SPACE : SPACE + TIME], loc.at[2]),
    ]
    for c in local:
        c.start()

    barrier = pltpu.get_barrier_semaphore()

    def hello(section, dp):
        pl.semaphore_signal(
            barrier, inc=1, device_id={"section": section, "dp": dp}, device_id_type=MESH
        )

    hello(S, sibling)
    for i in range(1, 4):
        hello(S, lax.rem(y + i, 4) * 16 + lax.rem(D, 16))
        hello(base + lax.rem(x + i, 4), D)
    for i in range(1, 8):
        hello(S, y * 16 + lax.rem(z + i, 8) * 2 + k)

    @pl.when(S == 0)
    def _():
        hello(4, far)

    @pl.when(S == 3)
    def _():
        hello(4, far)
        hello(7, far)

    @pl.when(S == 4)
    def _():
        hello(0, far)
        hello(3, far)

    @pl.when(S == 7)
    def _():
        hello(3, far)

    crossings = jnp.where(end, 1, 0) + jnp.where(jnp.logical_or(S == 3, S == 4), 1, 0)
    pl.semaphore_wait(barrier, 14 + crossings)

    for c in local:
        c.wait()

    near = jnp.where(x % 2 == 1, 0, 3)
    passed = jnp.where(x % 2 == 0, 1, 2)
    other = jnp.where(x == 0, 3, 0)
    distant = jnp.where(x == 0, 2, 1)
    middle = jnp.logical_and(jnp.logical_not(end), k == 1)
    passes = jnp.logical_or(middle, jnp.logical_and(end, k == 0))

    def chunk_copy(j, c, parity, core, send, recv, section, dp):
        n = 8 * parity + 4 * core + 2 * (c % 2) + c // 2
        rows = pl.ds(pl.multiple_of(n * 192, 192), 192)
        return copy(wv.at[j, rows], wv.at[j, rows], send, recv, section, dp)

    def x_chunk(j, c, target, slot):
        return chunk_copy(j, c, odd, k, wg_send.at[slot, c], wg_recv.at[j, c], base + target, D)

    def y_chunk(j, c, parity):
        dp = jnp.where(c % 2 == 1, above, below)
        return chunk_copy(j, c, parity, k, wy_send.at[j, c], wy_recv.at[j, c], S, dp)

    def core_chunk(j, c, far_rows, core):
        parity = 1 - odd if far_rows else odd
        at = 4 * far_rows + c
        return chunk_copy(j, c, parity, core, ws_send.at[j, at], ws_recv.at[j, at], S, sibling)

    def each(body):
        def step(c, carry):
            body(c)
            return carry

        lax.fori_loop(0, 4, step, 0)

    def take_x(j, c):
        x_chunk(j, c, 0, 0).wait_recv()
        y_chunk(j, c, odd).start()

        @pl.when(jnp.logical_and(j == passed, k == 0))
        def _():
            x_chunk(j, c, near, 2).start()

        core_chunk(j, c, 0, k).start()

    def take_y(j, c):
        y_chunk(j, c, 1 - odd).wait_recv()
        core_chunk(j, c, 1, k).start()

    def pass_middle():
        @pl.when(middle)
        def _():
            @each
            def _(c):
                x_chunk(passed, c, 0, 0).wait_recv()
                x_chunk(passed, c, near, 2).start()

    @each
    def _(c):
        x_chunk(x, c, near, 0).start()

        @pl.when(middle)
        def _():
            x_chunk(x, c, 3 - x, 1).start()

    cot_copy = copy(cot_ref.at[mine], ct, ct_send, ct_recv, S, far)

    @pl.when(jnp.logical_or(S == 4, S == 7))
    def _():
        cot_copy.start()

    @pl.when(half == 1)
    def _():
        pass_middle()

    def rows_of(c, h):
        return pl.ds(pl.multiple_of(h * 128 + c * HALF, HALF), HALF)

    def keep(ref, c, value):
        ref[rows_of(c, 0), :] = value[:HALF]
        ref[rows_of(c, 1), :] = value[HALF:]

    def y_copy(c):
        return copy(yout.at[c], xin.at[c], x_send.at[c], x_recv.at[c], lax.rem(S + 1, 8), D)

    def y_cross(c):
        return copy(yout.at[c], bx.at[0], x_send.at[c], bx_recv, jnp.where(c == 0, 7, 4), far)

    def owner_hidden(c):
        wide = wide_space(xin[c].astype(F32))
        keep(xc, c, wide)
        hidden, slope = activate(space_forward(wide, wv.at[x]))
        act[c] = slope
        wide = wide_time(hidden)
        keep(hc, c, wide)
        return wide

    def forward(first):
        def clip(c, carry):
            if first:
                xin[c] = by_height(cl[c]).astype(BF16)
            else:
                y_copy(c).wait_recv()
            wide = owner_hidden(c)
            out = xin[c].astype(F32) + nn(wide, wv[x, SPACE : SPACE + TIME, :])
            yout[c] = out.astype(BF16)
            if first:
                y_copy(c).start()
            else:
                @pl.when(x < 3)
                def _():
                    y_copy(c).start()

                @pl.when(x == 3)
                def _():
                    y_cross(c).start()

            return carry

        lax.fori_loop(0, 2, clip, 0)

    @pl.when(S == 0)
    def _():
        forward(True)

    @pl.when(end)
    def _():
        @each
        def _(c):
            take_x(passed, c)
            take_x(other, c)

    @pl.when(jnp.logical_and(half == 0, x > 0))
    def _():
        forward(False)
        pass_middle()

    def x_copy(j):
        return copy(bx.at[j], xin.at[mine], bx_send.at[j], x_recv.at[mine], base + j, D)

    def g_copy(j):
        return copy(bg.at[j + 1], gin.at[mine], go_send.at[j], gin_recv.at[mine], base + j, D)

    back_copy = copy(bg.at[0], bg.at[4], bg_send, bg_recv, lax.rem(S + 4, 8), far)

    @pl.when(end)
    def _():
        @each
        def _(c):
            take_x(distant, c)
            take_y(passed, c)
            take_y(other, c)
        @each
        def _(c):
            take_y(distant, c)
        @each
        def _(c):
            for j in (passed, other, distant):
                core_chunk(j, c, 0, 1 - k).wait_recv()
                core_chunk(j, c, 1, 1 - k).wait_recv()

        @pl.when(half == 0)
        def _():
            bx[0] = by_height(cl[mine]).astype(BF16)

        @pl.when(half == 1)
        def _():
            y_cross(0).wait_recv()

        def layer(j, carry):
            @pl.when(half == 1)
            def _():
                @pl.when(j == x)
                def _():
                    xin[mine] = bx[j]

                @pl.when(j != x)
                def _():
                    x_copy(j).start()

            v = bx[j].astype(F32)
            hidden, slope = activate(space_forward(wide_space(v), wv.at[j]))
            bact[j] = slope

            @pl.when(j < 3)
            def _():
                out = v + nn(wide_time(hidden), wv[j, SPACE : SPACE + TIME, :])
                bx[j + 1] = out.astype(BF16)

            return carry

        lax.fori_loop(0, 4, layer, 0)

        @pl.when(half == 0)
        def _():
            back_copy.wait_recv()

        @pl.when(half == 1)
        def _():
            cot_copy.wait_recv()
            bg[4] = by_height(ct[...]).astype(BF16)

        def layer_back(i, carry):
            j = 3 - i

            @pl.when(j == x)
            def _():
                gin[mine] = bg[j + 1]

            @pl.when(j != x)
            def _():
                g_copy(j).start()

            @pl.when(j + half > 0)
            def _():
                g = bg[j + 1].astype(F32)
                g_pre = (g_hidden_of(g, wv.at[j]) * bact[j]).astype(BF16).astype(F32)
                bg[j] = (g + space_backward(g_pre, wv.at[j])).astype(BF16)

            return carry

        lax.fori_loop(0, 4, layer_back, 0)

        @pl.when(half == 1)
        def _():
            back_copy.start()

    @pl.when(half == 1)
    def _():
        def clip(c, carry):
            @pl.when(jnp.logical_not(jnp.logical_and(end, c == mine)))
            def _():
                y_copy(c).wait_recv()

            owner_hidden(c)
            return carry

        lax.fori_loop(0, 2, clip, 0)

    def clip_back(i, carry):
        c = jnp.where(i == 0, mine, 1 - mine)

        @pl.when(jnp.logical_not(jnp.logical_and(end, c == mine)))
        def _():
            copy(gin.at[c], gin.at[c], go_send.at[0], gin_recv.at[c], S, D).wait_recv()

        keep(gb, c, gin[c])
        g = gin[c].astype(F32)
        keep(gp, c, (g_hidden_of(g, wv.at[x]) * act[c]).astype(BF16))
        return carry

    lax.fori_loop(0, 2, clip_back, 0)

    for q in range(3):
        lanes = slice(256 * q, 256 * q + 256)
        dw[SPACE + 256 * q : SPACE + 256 * q + 256, :] = tn(hc[:, lanes], gb[...])
        dw[256 * q : 256 * q + 256, :] = tn(xc[0:128, lanes], gp[128:256, :])
        dw[768 + 256 * q : 1024 + 256 * q, :] = tn(xc[:, lanes], gp[...])
        dw[1536 + 256 * q : 1792 + 256 * q, :] = tn(xc[128:256, lanes], gp[0:128, :])

    ahead = jnp.where(odd == k, 1, 3)
    blocks = [lax.rem(y + i, 4) for i in (2, 1, 3, 0)]
    forth = lax.rem(y + ahead, 4)
    back = lax.rem(y + 4 - ahead, 4)

    def core_step(i, column):
        yb = blocks[i]
        return copy(part.at[column, yb], r1.at[yb], r1_send.at[i], r1_recv.at[i], S, sibling)

    for i in range(4):
        def pack(b, carry):
            n = blocks[i] * 8 + b
            top = dw[pl.ds(pl.multiple_of(n * 72, 8), 72), :]
            low = dw[pl.ds(pl.multiple_of(SPACE + n * 24, 8), 24), :]
            block = jnp.concatenate([top, low], axis=0).astype(BF16)
            part[0, blocks[i], b] = block[:, 0:128]
            part[1, blocks[i], b] = block[:, 128:256]
            return carry

        lax.fori_loop(0, 8, pack, 0)
        core_step(i, 1 - k).start()

    def add_cores(yb):
        def one(b, carry):
            s1[yb, b] = (part[k, yb, b].astype(F32) + r1[yb, b].astype(F32)).astype(BF16)
            return carry

        lax.fori_loop(0, 8, one, 0)

    def y_step(i):
        return copy(
            s1.at[(blocks[0], forth, back)[i]], r2.at[i], r2_send.at[i], r2_recv.at[i],
            S, (forth, forth, back)[i] * 16 + lane,
        )

    core_step(0, k).wait_recv()
    add_cores(blocks[0])
    y_step(0).start()
    core_step(1, k).wait_recv()
    core_step(2, k).wait_recv()
    add_cores(forth)
    y_step(1).start()
    y_step(0).wait_recv()

    def add_relayed(b, carry):
        total = part[k, back, b].astype(F32) + r1[back, b].astype(F32) + r2[0, b].astype(F32)
        s1[back, b] = total.astype(BF16)
        return carry

    lax.fori_loop(0, 8, add_relayed, 0)
    y_step(2).start()
    core_step(3, k).wait_recv()
    y_step(1).wait_recv()
    y_step(2).wait_recv()
    def add_y(b, carry):
        total = part[k, y, b].astype(F32) + r1[y, b].astype(F32) + r2[1, b].astype(F32) + r2[2, b].astype(F32)
        s2[b] = total.astype(BF16)
        return carry

    lax.fori_loop(0, 8, add_y, 0)

    def z_step(i):
        to = lax.rem(z + i, 8)
        return copy(s2.at[to], r3.at[i - 1], r3_send.at[i - 1], r3_recv.at[i - 1], S, y * 16 + to * 2 + k)

    for i in range(1, 8):
        z_step(i).start()
    for i in range(1, 8):
        z_step(i).wait_recv()

    total = s2[z].astype(F32)
    for i in range(7):
        total = total + r3[i].astype(F32)
    fin[k] = total * scale

    final = copy(fin.at[k], fin.at[k], r4_sem.at[0], r4_sem.at[1], S, sibling)
    final.start()
    final.wait_send()
    copy(fin.at[1 - k], fin.at[1 - k], r4_sem.at[0], r4_sem.at[1], S, sibling).wait_recv()

    for core in range(2):
        @pl.when(k == core)
        def _():
            for side in range(2):
                lanes = slice(128 * side, 128 * side + 128)
                out_s[:, lanes] = fin[side, 36 * core : 36 * core + 36, :]
                out_t[:, lanes] = fin[side, 72 + 12 * core : 84 + 12 * core, :]

    for i in range(4):
        core_step(i, 1 - k).wait_send()
    for i in range(3):
        y_step(i).wait_send()
    for i in range(1, 8):
        z_step(i).wait_send()
    @each
    def _(c):
        x_chunk(x, c, near, 0).wait_send()

        @pl.when(middle)
        def _():
            x_chunk(x, c, 3 - x, 1).wait_send()

        @pl.when(passes)
        def _():
            x_chunk(passed, c, near, 2).wait_send()

        @pl.when(end)
        def _():
            for j in (passed, other, distant):
                y_chunk(j, c, odd).wait_send()
                core_chunk(j, c, 0, k).wait_send()
                core_chunk(j, c, 1, k).wait_send()

    @pl.when(jnp.logical_or(S == 4, S == 7))
    def _():
        cot_copy.wait_send()

    @pl.when(half == 0)
    def _():
        for c in range(2):
            y_copy(c).wait_send()

    @pl.when(end)
    def _():
        for i in range(1, 4):
            j = lax.rem(x + i, 4)
            g_copy(j).wait_send()

            @pl.when(half == 1)
            def _():
                x_copy(j).wait_send()

        @pl.when(half == 1)
        def _():
            back_copy.wait_send()


def body(clips, cotangent, spatial_kernel, temporal_kernel):
    micro = clips.shape[0]
    tile = clips.shape[1:]
    cells = tile[0] * tile[1] * tile[2]
    scale = 1.0 / math.sqrt(micro * lax.axis_size("dp") * cells)
    sem = pltpu.SemaphoreType.DMA
    vmem = pltpu.VMEM
    out_s, out_t = pl.pallas_call(
        functools.partial(kernel, scale),
        out_shape=(jax.ShapeDtypeStruct((36, C), F32), jax.ShapeDtypeStruct((12, C), F32)),
        in_specs=[pl.BlockSpec(memory_space=pltpu.HBM)] * 4,
        out_specs=(pl.BlockSpec(memory_space=pltpu.VMEM),) * 2,
        scratch_shapes=[
            vmem((4, SPACE + TIME, C), BF16),
            vmem((2, ROWS, C), BF16),
            vmem((ROWS, C), BF16),
            vmem((2, ROWS, C), BF16),
            vmem((2, ROWS, C), BF16),
            vmem((4, ROWS, C), BF16),
            vmem((5, ROWS, C), BF16),
            vmem((2, ROWS, C), BF16),
            vmem((2, ROWS, C), F32),
            vmem((4, ROWS, C), F32),
            vmem((2 * ROWS, 3 * C), BF16),
            vmem((2 * ROWS, 3 * C), BF16),
            vmem((2 * ROWS, C), BF16),
            vmem((2 * ROWS, C), BF16),
            vmem((SPACE + TIME, C), F32),
            vmem((2, 4, 8, 96, 128), BF16),
            vmem((4, 8, 96, 128), BF16),
            vmem((4, 8, 96, 128), BF16),
            vmem((3, 8, 96, 128), BF16),
            vmem((8, 96, 128), BF16),
            vmem((7, 96, 128), BF16),
            vmem((2, 96, 128), F32),
            sem((3,)),
            sem((3, 4)),
            sem((4, 4)),
            sem((4, 8)),
            sem((4, 8)),
            sem((4, 4)),
            sem((4, 4)),
            sem((2,)),
            sem((2,)),
            sem((4,)),
            sem,
            sem,
            sem,
            sem((4,)),
            sem((2,)),
            sem,
            sem,
            sem((4,)),
            sem((4,)),
            sem((3,)),
            sem((3,)),
            sem((7,)),
            sem((7,)),
            sem((2,)),
        ],
        compiler_params=pltpu.CompilerParams(
            collective_id=0, has_side_effects=True, vmem_limit_bytes=66_900_000
        ),
        name="window",
    )(
        clips.reshape(micro, cells, tile[3]),
        cotangent.reshape(micro, cells, tile[3]),
        spatial_kernel[0],
        temporal_kernel[0],
    )
    return (out_s[None], out_t[None])


def solution(mesh):
    return jax.shard_map(
        body,
        mesh=mesh,
        in_specs=(
            P("dp", None, None, None, None),
            P("dp", None, None, None, None),
            P("section", None, None),
            P("section", None, None),
        ),
        out_specs=(P("section", "dp", None), P("section", "dp", None)),
        check_vma=False,
    )
```

```python
import functools
import math

import jax
import jax.numpy as jnp
from jax import lax
from jax.experimental import pallas as pl
from jax.experimental.pallas import tpu as pltpu
from jax.sharding import PartitionSpec as P

MESH = pl.DeviceIdType.MESH
F32 = jnp.float32
BF16 = jnp.bfloat16
C = 256
ROWS = 128
HALF = 64
SPACE = 9 * C
TIME = 3 * C


def by_height(v):
    v = v.astype(F32).reshape(8, 2, 8, C)
    return jnp.concatenate([v[:, 0].reshape(HALF, C), v[:, 1].reshape(HALF, C)], axis=0)


def columns(v):
    w = lax.broadcasted_iota(jnp.int32, v.shape, 0) & 7
    before = jnp.where(w == 0, 0.0, pltpu.roll(v, 1, 0))
    after = jnp.where(w == 7, 0.0, pltpu.roll(v, ROWS - 1, 0))
    return before, after


def frames(v):
    zero = jnp.zeros((8, C), F32)
    before = jnp.concatenate([zero, v[0:56], zero, v[64:120]], axis=0)
    after = jnp.concatenate([v[8:64], zero, v[72:128], zero], axis=0)
    return before, after


def nn(a, b):
    return jnp.dot(a, b, preferred_element_type=F32)


def nt(a, b):
    return lax.dot_general(a, b, (((1,), (1,)), ((), ())), preferred_element_type=F32)


def tn(a, b):
    return lax.dot_general(a, b, (((0,), (0,)), ((), ())), preferred_element_type=F32)


def wide_space(v):
    before, after = columns(v)
    return jnp.concatenate([before, v, after], axis=1).astype(BF16)


def wide_time(v):
    before, after = frames(v)
    return jnp.concatenate([before, v, after], axis=1).astype(BF16)


def space_forward(wide, w):
    same = nn(wide, w[768:1536, :])
    top = nn(wide[HALF:], w[1536:2304, :])
    bottom = nn(wide[:HALF], w[0:768, :])
    return same + jnp.concatenate([top, bottom], axis=0)


def activate(pre):
    sigma = jax.nn.sigmoid(pre)
    hidden = (pre * sigma).astype(BF16).astype(F32)
    return hidden, sigma * (1.0 + pre * (1.0 - sigma))


def g_hidden_of(g, w):
    before, after = frames(g)
    out = nt(after.astype(BF16), w[SPACE : SPACE + 256, :])
    out = out + nt(g.astype(BF16), w[SPACE + 256 : SPACE + 512, :])
    return out + nt(before.astype(BF16), w[SPACE + 512 : SPACE + 768, :])


def space_backward(g_pre, w):
    before, after = columns(g_pre)
    same = top = bottom = None
    for q, v in enumerate((after, g_pre, before)):
        v = v.astype(BF16)
        a = nt(v, w[768 + 256 * q : 1024 + 256 * q, :])
        t = nt(v[HALF:], w[256 * q : 256 * q + 256, :])
        b = nt(v[:HALF], w[1536 + 256 * q : 1792 + 256 * q, :])
        same, top, bottom = (a, t, b) if same is None else (same + a, top + t, bottom + b)
    return same + jnp.concatenate([top, bottom], axis=0)


def kernel(
    scale,
    clips_ref, cot_ref, ws_ref, wt_ref,
    out_s, out_t,
    wv, cl, ct, xin, yout, bx, bg, gin,
    act, bact, xc, hc, gp, gb, dw, part, r1, s1, r2, s2, r3, fin,
    loc, wg_send, wg_recv, ws_send, ws_recv, wy_send, wy_recv,
    x_send, x_recv, bx_send, bx_recv, ct_send, ct_recv,
    go_send, gin_recv, bg_send, bg_recv,
    r1_send, r1_recv, r2_send, r2_recv, r3_send, r3_recv, r4_sem, up, down,
):
    S = lax.axis_index("section")
    D = lax.axis_index("dp")
    half = S // 4
    x = S % 4
    y = D // 16
    z = (D // 2) % 8
    k = D % 2
    far = D + 8 - 16 * (z // 4)
    sibling = D + 1 - 2 * k
    end = jnp.logical_or(x == 0, x == 3)
    mine = jnp.where(x == 0, 1, 0)
    base = half * 4
    odd = y % 2
    lane = lax.rem(D, 16)
    above = lax.rem(y + 1, 4) * 16 + lane
    below = lax.rem(y + 3, 4) * 16 + lane

    def copy(src, dst, send, recv, section, dp):
        return pltpu.make_async_remote_copy(
            src_ref=src, dst_ref=dst, send_sem=send, recv_sem=recv,
            device_id={"section": section, "dp": dp}, device_id_type=MESH,
        )

    local = [
        pltpu.make_async_copy(clips_ref, cl, loc.at[0]),
        pltpu.make_async_copy(ws_ref, wv.at[x, 0:SPACE], loc.at[1]),
        pltpu.make_async_copy(wt_ref, wv.at[x, SPACE : SPACE + TIME], loc.at[2]),
    ]
    for c in local:
        c.start()

    barrier = pltpu.get_barrier_semaphore()

    def hello(section, dp):
        pl.semaphore_signal(
            barrier, inc=1, device_id={"section": section, "dp": dp}, device_id_type=MESH
        )

    hello(S, sibling)
    hello(S, above)
    hello(S, below)
    hello(base + lax.rem(x + 1, 4), D)
    hello(base + lax.rem(x + 3, 4), D)

    @pl.when(z > 0)
    def _():
        hello(S, D - 2)

    @pl.when(z < 7)
    def _():
        hello(S, D + 2)

    @pl.when(S == 0)
    def _():
        hello(4, far)

    @pl.when(S == 3)
    def _():
        hello(7, far)

    @pl.when(jnp.logical_or(S == 4, S == 7))
    def _():
        hello(3, far)

    inner = jnp.logical_and(z > 0, z < 7)
    crossings = jnp.where(S == 3, 2, jnp.where(jnp.logical_or(S == 4, S == 7), 1, 0))
    pl.semaphore_wait(barrier, 6 + jnp.where(inner, 1, 0) + crossings)

    def sweep(sem, step, first, last):
        @pl.when(z != first)
        def _():
            pl.semaphore_wait(sem, 1)

        @pl.when(z != last)
        def _():
            pl.semaphore_signal(
                sem, inc=1, device_id={"section": S, "dp": D + 2 * step}, device_id_type=MESH
            )

    def meet_line():
        @pl.when(z < 4)
        def _():
            sweep(up, 1, 0, 7)
            sweep(down, -1, 7, 0)

        @pl.when(z >= 4)
        def _():
            sweep(down, -1, 7, 0)
            sweep(up, 1, 0, 7)

    for c in local:
        c.wait()

    near = jnp.where(x % 2 == 1, 0, 3)
    passed = jnp.where(x % 2 == 0, 1, 2)
    other = jnp.where(x == 0, 3, 0)
    distant = jnp.where(x == 0, 2, 1)
    middle = jnp.logical_and(jnp.logical_not(end), k == 1)
    passes = jnp.logical_or(middle, jnp.logical_and(end, k == 0))

    def chunk_copy(j, c, parity, core, send, recv, section, dp):
        n = 8 * parity + 4 * core + 2 * (c % 2) + c // 2
        rows = pl.ds(pl.multiple_of(n * 192, 192), 192)
        return copy(wv.at[j, rows], wv.at[j, rows], send, recv, section, dp)

    def x_chunk(j, c, target, slot):
        return chunk_copy(j, c, odd, k, wg_send.at[slot, c], wg_recv.at[j, c], base + target, D)

    def y_chunk(j, c, parity):
        dp = jnp.where(c % 2 == 1, above, below)
        return chunk_copy(j, c, parity, k, wy_send.at[j, c], wy_recv.at[j, c], S, dp)

    def core_chunk(j, c, far_rows, core):
        parity = 1 - odd if far_rows else odd
        at = 4 * far_rows + c
        return chunk_copy(j, c, parity, core, ws_send.at[j, at], ws_recv.at[j, at], S, sibling)

    def each(body):
        def step(c, carry):
            body(c)
            return carry

        lax.fori_loop(0, 4, step, 0)

    def take_x(j, c):
        x_chunk(j, c, 0, 0).wait_recv()
        y_chunk(j, c, odd).start()

        @pl.when(jnp.logical_and(j == passed, k == 0))
        def _():
            x_chunk(j, c, near, 2).start()

        core_chunk(j, c, 0, k).start()

    def take_y(j, c):
        y_chunk(j, c, 1 - odd).wait_recv()
        core_chunk(j, c, 1, k).start()

    def pass_middle():
        @pl.when(middle)
        def _():
            @each
            def _(c):
                x_chunk(passed, c, 0, 0).wait_recv()
                x_chunk(passed, c, near, 2).start()

    @each
    def _(c):
        x_chunk(x, c, near, 0).start()

        @pl.when(middle)
        def _():
            x_chunk(x, c, 3 - x, 1).start()

    def cot_copy(c):
        return copy(cot_ref.at[c], ct, ct_send.at[c], ct_recv, jnp.where(c == 0, 7, 4), far)

    @pl.when(S == 3)
    def _():
        for c in range(2):
            cot_copy(c).start()

    @pl.when(half == 1)
    def _():
        pass_middle()

        @pl.when(jnp.logical_not(end))
        def _():
            meet_line()

    def rows_of(c, h):
        return pl.ds(pl.multiple_of(h * 128 + c * HALF, HALF), HALF)

    def keep(ref, c, value):
        ref[rows_of(c, 0), :] = value[:HALF]
        ref[rows_of(c, 1), :] = value[HALF:]

    def y_copy(c):
        return copy(yout.at[c], xin.at[c], x_send.at[c], x_recv.at[c], lax.rem(S + 1, 8), D)

    def y_cross(c):
        return copy(yout.at[c], bx.at[0], x_send.at[c], bx_recv, jnp.where(c == 0, 7, 4), far)

    def owner_hidden(c):
        wide = wide_space(xin[c].astype(F32))
        keep(xc, c, wide)
        hidden, slope = activate(space_forward(wide, wv.at[x]))
        act[c] = slope
        wide = wide_time(hidden)
        keep(hc, c, wide)
        return wide

    def forward(first):
        def clip(c, carry):
            if first:
                xin[c] = by_height(cl[c]).astype(BF16)
            else:
                y_copy(c).wait_recv()
            wide = owner_hidden(c)
            out = xin[c].astype(F32) + nn(wide, wv[x, SPACE : SPACE + TIME, :])
            yout[c] = out.astype(BF16)
            if first:
                y_copy(c).start()
            else:
                @pl.when(x < 3)
                def _():
                    y_copy(c).start()

                @pl.when(x == 3)
                def _():
                    y_cross(c).start()

            return carry

        lax.fori_loop(0, 2, clip, 0)

    @pl.when(S == 0)
    def _():
        forward(True)

    @pl.when(end)
    def _():
        @each
        def _(c):
            take_x(passed, c)
            take_x(other, c)

    @pl.when(jnp.logical_and(half == 0, x > 0))
    def _():
        forward(False)
        pass_middle()

        @pl.when(x < 3)
        def _():
            meet_line()

    def x_copy(j):
        return copy(bx.at[j], xin.at[mine], bx_send.at[j], x_recv.at[mine], base + j, D)

    def g_copy(j):
        return copy(bg.at[j + 1], gin.at[mine], go_send.at[j], gin_recv.at[mine], base + j, D)

    back_copy = copy(bg.at[0], bg.at[4], bg_send, bg_recv, lax.rem(S + 4, 8), far)

    @pl.when(end)
    def _():
        @each
        def _(c):
            take_x(distant, c)
            take_y(passed, c)
            take_y(other, c)
        @each
        def _(c):
            take_y(distant, c)
        @each
        def _(c):
            for j in (passed, other, distant):
                core_chunk(j, c, 0, 1 - k).wait_recv()
                core_chunk(j, c, 1, 1 - k).wait_recv()

        @pl.when(half == 0)
        def _():
            bx[0] = by_height(cl[mine]).astype(BF16)

        @pl.when(half == 1)
        def _():
            y_cross(0).wait_recv()

        def layer(j, carry):
            @pl.when(half == 1)
            def _():
                @pl.when(j == x)
                def _():
                    xin[mine] = bx[j]

                @pl.when(j != x)
                def _():
                    x_copy(j).start()

            v = bx[j].astype(F32)
            hidden, slope = activate(space_forward(wide_space(v), wv.at[j]))
            bact[j] = slope

            @pl.when(j < 3)
            def _():
                out = v + nn(wide_time(hidden), wv[j, SPACE : SPACE + TIME, :])
                bx[j + 1] = out.astype(BF16)

            return carry

        lax.fori_loop(0, 4, layer, 0)

        @pl.when(half == 0)
        def _():
            meet_line()
            back_copy.wait_recv()

        @pl.when(half == 1)
        def _():
            cot_copy(0).wait_recv()
            bg[4] = by_height(ct[...]).astype(BF16)

        def layer_back(i, carry):
            j = 3 - i

            @pl.when(j == x)
            def _():
                gin[mine] = bg[j + 1]

            @pl.when(j != x)
            def _():
                g_copy(j).start()

            @pl.when(j + half > 0)
            def _():
                g = bg[j + 1].astype(F32)
                g_pre = (g_hidden_of(g, wv.at[j]) * bact[j]).astype(BF16).astype(F32)
                bg[j] = (g + space_backward(g_pre, wv.at[j])).astype(BF16)

            return carry

        lax.fori_loop(0, 4, layer_back, 0)

        @pl.when(half == 1)
        def _():
            back_copy.start()
            meet_line()

    @pl.when(half == 1)
    def _():
        def clip(c, carry):
            @pl.when(jnp.logical_not(jnp.logical_and(end, c == mine)))
            def _():
                y_copy(c).wait_recv()

            owner_hidden(c)
            return carry

        lax.fori_loop(0, 2, clip, 0)

    def clip_back(i, carry):
        c = jnp.where(i == 0, mine, 1 - mine)

        @pl.when(jnp.logical_not(jnp.logical_and(end, c == mine)))
        def _():
            copy(gin.at[c], gin.at[c], go_send.at[0], gin_recv.at[c], S, D).wait_recv()

        keep(gb, c, gin[c])
        g = gin[c].astype(F32)
        keep(gp, c, (g_hidden_of(g, wv.at[x]) * act[c]).astype(BF16))
        return carry

    lax.fori_loop(0, 2, clip_back, 0)

    for q in range(3):
        lanes = slice(256 * q, 256 * q + 256)
        dw[SPACE + 256 * q : SPACE + 256 * q + 256, :] = tn(hc[:, lanes], gb[...])
        dw[256 * q : 256 * q + 256, :] = tn(xc[0:128, lanes], gp[128:256, :])
        dw[768 + 256 * q : 1024 + 256 * q, :] = tn(xc[:, lanes], gp[...])
        dw[1536 + 256 * q : 1792 + 256 * q, :] = tn(xc[128:256, lanes], gp[0:128, :])

    ahead = jnp.where(odd == k, 1, 3)
    blocks = [lax.rem(y + i, 4) for i in (2, 1, 3, 0)]
    forth = lax.rem(y + ahead, 4)
    back = lax.rem(y + 4 - ahead, 4)

    def core_step(i, column):
        yb = blocks[i]
        return copy(part.at[column, yb], r1.at[yb], r1_send.at[i], r1_recv.at[i], S, sibling)

    for i in range(4):
        def pack(b, carry):
            n = blocks[i] * 8 + b
            top = dw[pl.ds(pl.multiple_of(n * 72, 8), 72), :]
            low = dw[pl.ds(pl.multiple_of(SPACE + n * 24, 8), 24), :]
            block = jnp.concatenate([top, low], axis=0).astype(BF16)
            part[0, blocks[i], b] = block[:, 0:128]
            part[1, blocks[i], b] = block[:, 128:256]
            return carry

        lax.fori_loop(0, 8, pack, 0)
        core_step(i, 1 - k).start()

    def add_cores(yb):
        def one(b, carry):
            s1[yb, b] = (part[k, yb, b].astype(F32) + r1[yb, b].astype(F32)).astype(BF16)
            return carry

        lax.fori_loop(0, 8, one, 0)

    def y_step(i):
        return copy(
            s1.at[(blocks[0], forth, back)[i]], r2.at[i], r2_send.at[i], r2_recv.at[i],
            S, (forth, forth, back)[i] * 16 + lane,
        )

    core_step(0, k).wait_recv()
    add_cores(blocks[0])
    y_step(0).start()
    core_step(1, k).wait_recv()
    core_step(2, k).wait_recv()
    add_cores(forth)
    y_step(1).start()
    y_step(0).wait_recv()

    def add_relayed(b, carry):
        total = part[k, back, b].astype(F32) + r1[back, b].astype(F32) + r2[0, b].astype(F32)
        s1[back, b] = total.astype(BF16)
        return carry

    lax.fori_loop(0, 8, add_relayed, 0)
    y_step(2).start()
    core_step(3, k).wait_recv()
    y_step(1).wait_recv()
    y_step(2).wait_recv()
    def add_y(b, carry):
        total = part[k, y, b].astype(F32) + r1[y, b].astype(F32) + r2[1, b].astype(F32) + r2[2, b].astype(F32)
        s2[b] = total.astype(BF16)
        return carry

    lax.fori_loop(0, 8, add_y, 0)

    def z_step(i):
        to = lax.rem(z + i, 8)
        return copy(s2.at[to], r3.at[i - 1], r3_send.at[i - 1], r3_recv.at[i - 1], S, y * 16 + to * 2 + k)

    for i in range(1, 8):
        z_step(i).start()
    for i in range(1, 8):
        z_step(i).wait_recv()

    total = s2[z].astype(F32)
    for i in range(7):
        total = total + r3[i].astype(F32)
    fin[k] = total * scale

    final = copy(fin.at[k], fin.at[k], r4_sem.at[0], r4_sem.at[1], S, sibling)
    final.start()
    final.wait_send()
    copy(fin.at[1 - k], fin.at[1 - k], r4_sem.at[0], r4_sem.at[1], S, sibling).wait_recv()

    for core in range(2):
        @pl.when(k == core)
        def _():
            for side in range(2):
                lanes = slice(128 * side, 128 * side + 128)
                out_s[:, lanes] = fin[side, 36 * core : 36 * core + 36, :]
                out_t[:, lanes] = fin[side, 72 + 12 * core : 84 + 12 * core, :]

    for i in range(4):
        core_step(i, 1 - k).wait_send()
    for i in range(3):
        y_step(i).wait_send()
    for i in range(1, 8):
        z_step(i).wait_send()
    @each
    def _(c):
        x_chunk(x, c, near, 0).wait_send()

        @pl.when(middle)
        def _():
            x_chunk(x, c, 3 - x, 1).wait_send()

        @pl.when(passes)
        def _():
            x_chunk(passed, c, near, 2).wait_send()

        @pl.when(end)
        def _():
            for j in (passed, other, distant):
                y_chunk(j, c, odd).wait_send()
                core_chunk(j, c, 0, k).wait_send()
                core_chunk(j, c, 1, k).wait_send()

    @pl.when(S == 3)
    def _():
        for c in range(2):
            cot_copy(c).wait_send()

    @pl.when(half == 0)
    def _():
        for c in range(2):
            y_copy(c).wait_send()

    @pl.when(end)
    def _():
        for i in range(1, 4):
            j = lax.rem(x + i, 4)
            g_copy(j).wait_send()

            @pl.when(half == 1)
            def _():
                x_copy(j).wait_send()

        @pl.when(half == 1)
        def _():
            back_copy.wait_send()


def body(clips, cotangent, spatial_kernel, temporal_kernel):
    micro = clips.shape[0]
    tile = clips.shape[1:]
    cells = tile[0] * tile[1] * tile[2]
    scale = 1.0 / math.sqrt(micro * lax.axis_size("dp") * cells)
    sem = pltpu.SemaphoreType.DMA
    vmem = pltpu.VMEM
    out_s, out_t = pl.pallas_call(
        functools.partial(kernel, scale),
        out_shape=(jax.ShapeDtypeStruct((36, C), F32), jax.ShapeDtypeStruct((12, C), F32)),
        in_specs=[pl.BlockSpec(memory_space=pltpu.HBM)] * 4,
        out_specs=(pl.BlockSpec(memory_space=pltpu.VMEM),) * 2,
        scratch_shapes=[
            vmem((4, SPACE + TIME, C), BF16),
            vmem((2, ROWS, C), BF16),
            vmem((ROWS, C), BF16),
            vmem((2, ROWS, C), BF16),
            vmem((2, ROWS, C), BF16),
            vmem((4, ROWS, C), BF16),
            vmem((5, ROWS, C), BF16),
            vmem((2, ROWS, C), BF16),
            vmem((2, ROWS, C), F32),
            vmem((4, ROWS, C), F32),
            vmem((2 * ROWS, 3 * C), BF16),
            vmem((2 * ROWS, 3 * C), BF16),
            vmem((2 * ROWS, C), BF16),
            vmem((2 * ROWS, C), BF16),
            vmem((SPACE + TIME, C), F32),
            vmem((2, 4, 8, 96, 128), BF16),
            vmem((4, 8, 96, 128), BF16),
            vmem((4, 8, 96, 128), BF16),
            vmem((3, 8, 96, 128), BF16),
            vmem((8, 96, 128), BF16),
            vmem((7, 96, 128), BF16),
            vmem((2, 96, 128), F32),
            sem((3,)),
            sem((3, 4)),
            sem((4, 4)),
            sem((4, 8)),
            sem((4, 8)),
            sem((4, 4)),
            sem((4, 4)),
            sem((2,)),
            sem((2,)),
            sem((4,)),
            sem,
            sem((2,)),
            sem,
            sem((4,)),
            sem((2,)),
            sem,
            sem,
            sem((4,)),
            sem((4,)),
            sem((3,)),
            sem((3,)),
            sem((7,)),
            sem((7,)),
            sem((2,)),
            pltpu.SemaphoreType.REGULAR,
            pltpu.SemaphoreType.REGULAR,
        ],
        compiler_params=pltpu.CompilerParams(
            collective_id=0, has_side_effects=True, vmem_limit_bytes=66_900_000
        ),
        name="window",
    )(
        clips.reshape(micro, cells, tile[3]),
        cotangent.reshape(micro, cells, tile[3]),
        spatial_kernel[0],
        temporal_kernel[0],
    )
    return (out_s[None], out_t[None])


def solution(mesh):
    return jax.shard_map(
        body,
        mesh=mesh,
        in_specs=(
            P("dp", None, None, None, None),
            P("dp", None, None, None, None),
            P("section", None, None),
            P("section", None, None),
        ),
        out_specs=(P("section", "dp", None), P("section", "dp", None)),
        check_vma=False,
    )
```

```python
import functools
import math

import jax
import jax.numpy as jnp
from jax import lax
from jax.experimental import pallas as pl
from jax.experimental.pallas import tpu as pltpu
from jax.sharding import PartitionSpec as P

MESH = pl.DeviceIdType.MESH
F32 = jnp.float32
BF16 = jnp.bfloat16
C = 256
ROWS = 128
HALF = 64
SPACE = 9 * C
TIME = 3 * C


def by_height(v):
    v = v.astype(F32).reshape(8, 2, 8, C)
    return jnp.concatenate([v[:, 0].reshape(HALF, C), v[:, 1].reshape(HALF, C)], axis=0)


def columns(v):
    w = lax.broadcasted_iota(jnp.int32, v.shape, 0) & 7
    before = jnp.where(w == 0, 0.0, pltpu.roll(v, 1, 0))
    after = jnp.where(w == 7, 0.0, pltpu.roll(v, ROWS - 1, 0))
    return before, after


def frames(v):
    zero = jnp.zeros((8, C), F32)
    before = jnp.concatenate([zero, v[0:56], zero, v[64:120]], axis=0)
    after = jnp.concatenate([v[8:64], zero, v[72:128], zero], axis=0)
    return before, after


def nn(a, b):
    return jnp.dot(a, b, preferred_element_type=F32)


def nt(a, b):
    return lax.dot_general(a, b, (((1,), (1,)), ((), ())), preferred_element_type=F32)


def tn(a, b):
    return lax.dot_general(a, b, (((0,), (0,)), ((), ())), preferred_element_type=F32)


def wide_space(v):
    before, after = columns(v)
    return jnp.concatenate([before, v, after], axis=1).astype(BF16)


def wide_time(v):
    before, after = frames(v)
    return jnp.concatenate([before, v, after], axis=1).astype(BF16)


def space_forward(wide, w):
    same = nn(wide, w[768:1536, :])
    top = nn(wide[HALF:], w[1536:2304, :])
    bottom = nn(wide[:HALF], w[0:768, :])
    return same + jnp.concatenate([top, bottom], axis=0)


def activate(pre):
    sigma = jax.nn.sigmoid(pre)
    hidden = (pre * sigma).astype(BF16).astype(F32)
    return hidden, sigma * (1.0 + pre * (1.0 - sigma))


def g_hidden_of(g, w):
    before, after = frames(g)
    out = nt(after.astype(BF16), w[SPACE : SPACE + 256, :])
    out = out + nt(g.astype(BF16), w[SPACE + 256 : SPACE + 512, :])
    return out + nt(before.astype(BF16), w[SPACE + 512 : SPACE + 768, :])


def space_backward(g_pre, w):
    before, after = columns(g_pre)
    same = top = bottom = None
    for q, v in enumerate((after, g_pre, before)):
        v = v.astype(BF16)
        a = nt(v, w[768 + 256 * q : 1024 + 256 * q, :])
        t = nt(v[HALF:], w[256 * q : 256 * q + 256, :])
        b = nt(v[:HALF], w[1536 + 256 * q : 1792 + 256 * q, :])
        same, top, bottom = (a, t, b) if same is None else (same + a, top + t, bottom + b)
    return same + jnp.concatenate([top, bottom], axis=0)


def kernel(
    scale,
    clips_ref, cot_ref, ws_ref, wt_ref,
    out_s, out_t,
    wv, cl, ct, xin, yout, bx, bg, gin,
    act, bact, xc, hc, gp, gb, dw, part, r1, s1, r2, s2, r3, fin,
    loc, wg_send, wg_recv, ws_send, ws_recv, wy_send, wy_recv,
    x_send, x_recv, bx_send, bx_recv, ct_send, ct_recv,
    go_send, gin_recv, bg_send, bg_recv,
    r1_send, r1_recv, r2_send, r2_recv, r3_send, r3_recv, r4_sem, up, down,
):
    S = lax.axis_index("section")
    D = lax.axis_index("dp")
    half = S // 4
    x = S % 4
    y = D // 16
    z = (D // 2) % 8
    k = D % 2
    far = D + 8 - 16 * (z // 4)
    sibling = D + 1 - 2 * k
    end = jnp.logical_or(x == 0, x == 3)
    mine = jnp.where(x == 0, 1, 0)
    base = half * 4
    odd = y % 2
    lane = lax.rem(D, 16)
    above = lax.rem(y + 1, 4) * 16 + lane
    below = lax.rem(y + 3, 4) * 16 + lane

    def copy(src, dst, send, recv, section, dp):
        return pltpu.make_async_remote_copy(
            src_ref=src, dst_ref=dst, send_sem=send, recv_sem=recv,
            device_id={"section": section, "dp": dp}, device_id_type=MESH,
        )

    local = [
        pltpu.make_async_copy(clips_ref, cl, loc.at[0]),
        pltpu.make_async_copy(ws_ref, wv.at[x, 0:SPACE], loc.at[1]),
        pltpu.make_async_copy(wt_ref, wv.at[x, SPACE : SPACE + TIME], loc.at[2]),
    ]
    for c in local:
        c.start()

    barrier = pltpu.get_barrier_semaphore()

    def hello(section, dp):
        pl.semaphore_signal(
            barrier, inc=1, device_id={"section": section, "dp": dp}, device_id_type=MESH
        )

    hello(S, sibling)
    hello(S, above)
    hello(S, below)
    hello(base + lax.rem(x + 1, 4), D)
    hello(base + lax.rem(x + 3, 4), D)

    @pl.when(z > 0)
    def _():
        hello(S, D - 2)

    @pl.when(z < 7)
    def _():
        hello(S, D + 2)

    @pl.when(S == 0)
    def _():
        hello(4, far)

    @pl.when(S == 3)
    def _():
        hello(7, far)

    @pl.when(jnp.logical_or(S == 4, S == 7))
    def _():
        hello(3, far)
        hello(S, far)

    inner = jnp.logical_and(z > 0, z < 7)
    crossings = jnp.where(jnp.logical_or(S == 3, jnp.logical_or(S == 4, S == 7)), 2, 0)
    pl.semaphore_wait(barrier, 6 + jnp.where(inner, 1, 0) + crossings)

    def sweep(sem, step, first, last):
        @pl.when(z != first)
        def _():
            pl.semaphore_wait(sem, 1)

        @pl.when(z != last)
        def _():
            pl.semaphore_signal(
                sem, inc=1, device_id={"section": S, "dp": D + 2 * step}, device_id_type=MESH
            )

    def meet_line():
        @pl.when(z < 4)
        def _():
            sweep(up, 1, 0, 7)
            sweep(down, -1, 7, 0)

        @pl.when(z >= 4)
        def _():
            sweep(down, -1, 7, 0)
            sweep(up, 1, 0, 7)

    for c in local:
        c.wait()

    near = jnp.where(x % 2 == 1, 0, 3)
    passed = jnp.where(x % 2 == 0, 1, 2)
    other = jnp.where(x == 0, 3, 0)
    distant = jnp.where(x == 0, 2, 1)
    middle = jnp.logical_not(end)

    def chunk_copy(j, c, parity, core, send, recv, section, dp):
        n = 8 * parity + 4 * core + 2 * (c % 2) + c // 2
        rows = pl.ds(pl.multiple_of(n * 192, 192), 192)
        return copy(wv.at[j, rows], wv.at[j, rows], send, recv, section, dp)

    def x_chunk(j, c, target, slot):
        return chunk_copy(j, c, odd, k, wg_send.at[slot, c], wg_recv.at[j, c], base + target, D)

    def y_chunk(j, c, parity):
        dp = jnp.where(c % 2 == 1, above, below)
        return chunk_copy(j, c, parity, k, wy_send.at[j, c], wy_recv.at[j, c], S, dp)

    def core_chunk(j, c, far_rows, core):
        parity = 1 - odd if far_rows else odd
        at = 4 * far_rows + c
        return chunk_copy(j, c, parity, core, ws_send.at[j, at], ws_recv.at[j, at], S, sibling)

    def each(body):
        def step(c, carry):
            body(c)
            return carry

        lax.fori_loop(0, 4, step, 0)

    def take_x(j, c):
        x_chunk(j, c, 0, 0).wait_recv()
        y_chunk(j, c, odd).start()

        @pl.when(jnp.logical_and(j == passed, c < 2))
        def _():
            x_chunk(j, c, near, 2).start()

        core_chunk(j, c, 0, k).start()

    def take_y(j, c):
        y_chunk(j, c, 1 - odd).wait_recv()
        core_chunk(j, c, 1, k).start()

    def pass_middle():
        @pl.when(middle)
        def _():
            for c in (2, 3):
                x_chunk(passed, c, 0, 0).wait_recv()
                x_chunk(passed, c, near, 2).start()

    @each
    def _(c):
        x_chunk(x, c, near, 0).start()

        @pl.when(jnp.logical_and(middle, c >= 2))
        def _():
            x_chunk(x, c, 3 - x, 1).start()

    cot_copy = copy(cot_ref.at[mine], ct, ct_send, ct_recv, S, far)

    @pl.when(jnp.logical_or(S == 4, S == 7))
    def _():
        cot_copy.start()

    @pl.when(half == 1)
    def _():
        pass_middle()

        @pl.when(jnp.logical_not(end))
        def _():
            meet_line()

    def rows_of(c, h):
        return pl.ds(pl.multiple_of(h * 128 + c * HALF, HALF), HALF)

    def keep(ref, c, value):
        ref[rows_of(c, 0), :] = value[:HALF]
        ref[rows_of(c, 1), :] = value[HALF:]

    def y_copy(c):
        return copy(yout.at[c], xin.at[c], x_send.at[c], x_recv.at[c], lax.rem(S + 1, 8), D)

    cross_copy = copy(yout.at[0], bx.at[0], x_send.at[0], bx_recv, 7, far)
    hand_copy = copy(yout.at[1], ct, x_send.at[1], ct_recv, 0, D)
    relay_copy = copy(ct, bx.at[0], ct_send, bx_recv, 4, far)

    def owner_hidden(c):
        wide = wide_space(xin[c].astype(F32))
        keep(xc, c, wide)
        hidden, slope = activate(space_forward(wide, wv.at[x]))
        act[c] = slope
        wide = wide_time(hidden)
        keep(hc, c, wide)
        return wide

    def forward(first):
        def clip(c, carry):
            if first:
                xin[c] = by_height(cl[c]).astype(BF16)
            else:
                y_copy(c).wait_recv()
            wide = owner_hidden(c)
            out = xin[c].astype(F32) + nn(wide, wv[x, SPACE : SPACE + TIME, :])
            yout[c] = out.astype(BF16)
            if first:
                y_copy(c).start()
            else:
                @pl.when(x < 3)
                def _():
                    y_copy(c).start()

                @pl.when(jnp.logical_and(x == 3, c == 0))
                def _():
                    cross_copy.start()

                @pl.when(jnp.logical_and(x == 3, c == 1))
                def _():
                    hand_copy.start()

            return carry

        lax.fori_loop(0, 2, clip, 0)

    @pl.when(S == 0)
    def _():
        forward(True)

    @pl.when(end)
    def _():
        @each
        def _(c):
            take_x(passed, c)
            take_x(other, c)

    @pl.when(S == 0)
    def _():
        hand_copy.wait_recv()
        relay_copy.start()

    @pl.when(jnp.logical_and(half == 0, x > 0))
    def _():
        forward(False)
        pass_middle()

        @pl.when(x < 3)
        def _():
            meet_line()

    def x_copy(j):
        return copy(bx.at[j], xin.at[mine], bx_send.at[j], x_recv.at[mine], base + j, D)

    def g_copy(j):
        return copy(bg.at[j + 1], gin.at[mine], go_send.at[j], gin_recv.at[mine], base + j, D)

    back_copy = copy(bg.at[0], bg.at[4], bg_send, bg_recv, lax.rem(S + 4, 8), far)

    @pl.when(end)
    def _():
        @each
        def _(c):
            take_x(distant, c)
            take_y(passed, c)
            take_y(other, c)
        @each
        def _(c):
            take_y(distant, c)
        @each
        def _(c):
            for j in (passed, other, distant):
                core_chunk(j, c, 0, 1 - k).wait_recv()
                core_chunk(j, c, 1, 1 - k).wait_recv()

        @pl.when(half == 0)
        def _():
            bx[0] = by_height(cl[mine]).astype(BF16)

        @pl.when(half == 1)
        def _():
            cross_copy.wait_recv()

        def layer(j, carry):
            @pl.when(half == 1)
            def _():
                @pl.when(j == x)
                def _():
                    xin[mine] = bx[j]

                @pl.when(j != x)
                def _():
                    x_copy(j).start()

            v = bx[j].astype(F32)
            hidden, slope = activate(space_forward(wide_space(v), wv.at[j]))
            bact[j] = slope

            @pl.when(j < 3)
            def _():
                out = v + nn(wide_time(hidden), wv[j, SPACE : SPACE + TIME, :])
                bx[j + 1] = out.astype(BF16)

            return carry

        lax.fori_loop(0, 4, layer, 0)

        @pl.when(half == 0)
        def _():
            meet_line()
            back_copy.wait_recv()

        @pl.when(half == 1)
        def _():
            cot_copy.wait_recv()
            bg[4] = by_height(ct[...]).astype(BF16)

        def layer_back(i, carry):
            j = 3 - i

            @pl.when(j == x)
            def _():
                gin[mine] = bg[j + 1]

            @pl.when(j != x)
            def _():
                g_copy(j).start()

            @pl.when(j + half > 0)
            def _():
                g = bg[j + 1].astype(F32)
                g_pre = (g_hidden_of(g, wv.at[j]) * bact[j]).astype(BF16).astype(F32)
                bg[j] = (g + space_backward(g_pre, wv.at[j])).astype(BF16)

            return carry

        lax.fori_loop(0, 4, layer_back, 0)

        @pl.when(half == 1)
        def _():
            back_copy.start()
            meet_line()

    @pl.when(half == 1)
    def _():
        def clip(c, carry):
            @pl.when(jnp.logical_not(jnp.logical_and(end, c == mine)))
            def _():
                y_copy(c).wait_recv()

            owner_hidden(c)
            return carry

        lax.fori_loop(0, 2, clip, 0)

    def clip_back(i, carry):
        c = jnp.where(i == 0, mine, 1 - mine)

        @pl.when(jnp.logical_not(jnp.logical_and(end, c == mine)))
        def _():
            copy(gin.at[c], gin.at[c], go_send.at[0], gin_recv.at[c], S, D).wait_recv()

        keep(gb, c, gin[c])
        g = gin[c].astype(F32)
        keep(gp, c, (g_hidden_of(g, wv.at[x]) * act[c]).astype(BF16))
        return carry

    lax.fori_loop(0, 2, clip_back, 0)

    for q in range(3):
        lanes = slice(256 * q, 256 * q + 256)
        dw[SPACE + 256 * q : SPACE + 256 * q + 256, :] = tn(hc[:, lanes], gb[...])
        dw[256 * q : 256 * q + 256, :] = tn(xc[0:128, lanes], gp[128:256, :])
        dw[768 + 256 * q : 1024 + 256 * q, :] = tn(xc[:, lanes], gp[...])
        dw[1536 + 256 * q : 1792 + 256 * q, :] = tn(xc[128:256, lanes], gp[0:128, :])

    blocks = [lax.rem(y + i, 4) for i in (2, 1, 3, 0)]
    sides = (lax.rem(y + 1, 4), lax.rem(y + 3, 4))

    def core_step(i, column):
        yb = blocks[i]
        return copy(part.at[column, yb], r1.at[yb], r1_send.at[i], r1_recv.at[i], S, sibling)

    for i in range(4):
        def pack(b, carry):
            n = blocks[i] * 8 + b
            top = dw[pl.ds(pl.multiple_of(n * 72, 8), 72), :]
            low = dw[pl.ds(pl.multiple_of(SPACE + n * 24, 8), 24), :]
            block = jnp.concatenate([top, low], axis=0).astype(BF16)
            part[0, blocks[i], b] = block[:, 0:128]
            part[1, blocks[i], b] = block[:, 128:256]
            return carry

        lax.fori_loop(0, 8, pack, 0)
        core_step(i, 1 - k).start()

    def add_cores(yb, start, stop):
        def one(b, carry):
            s1[yb, b] = (part[k, yb, b].astype(F32) + r1[yb, b].astype(F32)).astype(BF16)
            return carry

        lax.fori_loop(start, stop, one, 0)

    def y_step(i, side):
        forth, back = sides[side], sides[1 - side]
        to = (forth, back, forth)[i]
        some = pl.ds(4 * side, 4)
        return copy(
            s1.at[blocks[0] if i == 0 else to, some], r2.at[i, some],
            r2_send.at[i, side], r2_recv.at[i, side], S, to * 16 + lane,
        )

    core_step(0, k).wait_recv()
    add_cores(blocks[0], 0, 8)
    y_step(0, 0).start()
    y_step(0, 1).start()
    for side in (1, 0):
        core_step(2 - side, k).wait_recv()
        add_cores(sides[1 - side], 4 * side, 4 * side + 4)
        y_step(1, side).start()
    for side in range(2):
        forth = sides[side]
        y_step(0, side).wait_recv()

        def add_relayed(b, carry):
            total = part[k, forth, b].astype(F32) + r1[forth, b].astype(F32) + r2[0, b].astype(F32)
            s1[forth, b] = total.astype(BF16)
            return carry

        lax.fori_loop(4 * side, 4 * side + 4, add_relayed, 0)
        y_step(2, side).start()
    core_step(3, k).wait_recv()
    for i in (1, 2):
        for side in range(2):
            y_step(i, side).wait_recv()
    def add_y(b, carry):
        total = part[k, y, b].astype(F32) + r1[y, b].astype(F32) + r2[1, b].astype(F32) + r2[2, b].astype(F32)
        s2[b] = total.astype(BF16)
        return carry

    lax.fori_loop(0, 8, add_y, 0)

    def z_step(i):
        to = lax.rem(z + i, 8)
        return copy(s2.at[to], r3.at[i - 1], r3_send.at[i - 1], r3_recv.at[i - 1], S, y * 16 + to * 2 + k)

    for i in range(1, 8):
        z_step(i).start()
    for i in range(1, 8):
        z_step(i).wait_recv()

    total = s2[z].astype(F32)
    for i in range(7):
        total = total + r3[i].astype(F32)
    fin[k] = total * scale

    final = copy(fin.at[k], fin.at[k], r4_sem.at[0], r4_sem.at[1], S, sibling)
    final.start()
    final.wait_send()
    copy(fin.at[1 - k], fin.at[1 - k], r4_sem.at[0], r4_sem.at[1], S, sibling).wait_recv()

    for core in range(2):
        @pl.when(k == core)
        def _():
            for side in range(2):
                lanes = slice(128 * side, 128 * side + 128)
                out_s[:, lanes] = fin[side, 36 * core : 36 * core + 36, :]
                out_t[:, lanes] = fin[side, 72 + 12 * core : 84 + 12 * core, :]

    for i in range(4):
        core_step(i, 1 - k).wait_send()
    for i in range(3):
        for side in range(2):
            y_step(i, side).wait_send()
    for i in range(1, 8):
        z_step(i).wait_send()
    @each
    def _(c):
        x_chunk(x, c, near, 0).wait_send()

        @pl.when(jnp.logical_and(middle, c >= 2))
        def _():
            x_chunk(x, c, 3 - x, 1).wait_send()

        @pl.when(middle == (c >= 2))
        def _():
            x_chunk(passed, c, near, 2).wait_send()

        @pl.when(end)
        def _():
            for j in (passed, other, distant):
                y_chunk(j, c, odd).wait_send()
                core_chunk(j, c, 0, k).wait_send()
                core_chunk(j, c, 1, k).wait_send()

    @pl.when(jnp.logical_or(S == 4, S == 7))
    def _():
        cot_copy.wait_send()

    @pl.when(S == 0)
    def _():
        relay_copy.wait_send()

    @pl.when(half == 0)
    def _():
        for c in range(2):
            y_copy(c).wait_send()

    @pl.when(end)
    def _():
        for i in range(1, 4):
            j = lax.rem(x + i, 4)
            g_copy(j).wait_send()

            @pl.when(half == 1)
            def _():
                x_copy(j).wait_send()

        @pl.when(half == 1)
        def _():
            back_copy.wait_send()


def body(clips, cotangent, spatial_kernel, temporal_kernel):
    micro = clips.shape[0]
    tile = clips.shape[1:]
    cells = tile[0] * tile[1] * tile[2]
    scale = 1.0 / math.sqrt(micro * lax.axis_size("dp") * cells)
    sem = pltpu.SemaphoreType.DMA
    vmem = pltpu.VMEM
    out_s, out_t = pl.pallas_call(
        functools.partial(kernel, scale),
        out_shape=(jax.ShapeDtypeStruct((36, C), F32), jax.ShapeDtypeStruct((12, C), F32)),
        in_specs=[pl.BlockSpec(memory_space=pltpu.HBM)] * 4,
        out_specs=(pl.BlockSpec(memory_space=pltpu.VMEM),) * 2,
        scratch_shapes=[
            vmem((4, SPACE + TIME, C), BF16),
            vmem((2, ROWS, C), BF16),
            vmem((ROWS, C), BF16),
            vmem((2, ROWS, C), BF16),
            vmem((2, ROWS, C), BF16),
            vmem((4, ROWS, C), BF16),
            vmem((5, ROWS, C), BF16),
            vmem((2, ROWS, C), BF16),
            vmem((2, ROWS, C), F32),
            vmem((4, ROWS, C), F32),
            vmem((2 * ROWS, 3 * C), BF16),
            vmem((2 * ROWS, 3 * C), BF16),
            vmem((2 * ROWS, C), BF16),
            vmem((2 * ROWS, C), BF16),
            vmem((SPACE + TIME, C), F32),
            vmem((2, 4, 8, 96, 128), BF16),
            vmem((4, 8, 96, 128), BF16),
            vmem((4, 8, 96, 128), BF16),
            vmem((3, 8, 96, 128), BF16),
            vmem((8, 96, 128), BF16),
            vmem((7, 96, 128), BF16),
            vmem((2, 96, 128), F32),
            sem((3,)),
            sem((3, 4)),
            sem((4, 4)),
            sem((4, 8)),
            sem((4, 8)),
            sem((4, 4)),
            sem((4, 4)),
            sem((2,)),
            sem((2,)),
            sem((4,)),
            sem,
            sem,
            sem,
            sem((4,)),
            sem((2,)),
            sem,
            sem,
            sem((4,)),
            sem((4,)),
            sem((3, 2)),
            sem((3, 2)),
            sem((7,)),
            sem((7,)),
            sem((2,)),
            pltpu.SemaphoreType.REGULAR,
            pltpu.SemaphoreType.REGULAR,
        ],
        compiler_params=pltpu.CompilerParams(
            collective_id=0, has_side_effects=True, vmem_limit_bytes=66_900_000
        ),
        name="window",
    )(
        clips.reshape(micro, cells, tile[3]),
        cotangent.reshape(micro, cells, tile[3]),
        spatial_kernel[0],
        temporal_kernel[0],
    )
    return (out_s[None], out_t[None])


def solution(mesh):
    return jax.shard_map(
        body,
        mesh=mesh,
        in_specs=(
            P("dp", None, None, None, None),
            P("dp", None, None, None, None),
            P("section", None, None),
            P("section", None, None),
        ),
        out_specs=(P("section", "dp", None), P("section", "dp", None)),
        check_vma=False,
    )
```

```python
import functools
import math

import jax
import jax.numpy as jnp
from jax import lax
from jax.experimental import pallas as pl
from jax.experimental.pallas import tpu as pltpu
from jax.sharding import PartitionSpec as P

MESH = pl.DeviceIdType.MESH
F32 = jnp.float32
BF16 = jnp.bfloat16
C = 256
ROWS = 128
HALF = 64
SPACE = 9 * C
TIME = 3 * C


def by_height(v):
    v = v.astype(F32).reshape(8, 2, 8, C)
    return jnp.concatenate([v[:, 0].reshape(HALF, C), v[:, 1].reshape(HALF, C)], axis=0)


def columns(v):
    w = lax.broadcasted_iota(jnp.int32, v.shape, 0) & 7
    before = jnp.where(w == 0, 0.0, pltpu.roll(v, 1, 0))
    after = jnp.where(w == 7, 0.0, pltpu.roll(v, ROWS - 1, 0))
    return before, after


def frames(v):
    zero = jnp.zeros((8, C), F32)
    before = jnp.concatenate([zero, v[0:56], zero, v[64:120]], axis=0)
    after = jnp.concatenate([v[8:64], zero, v[72:128], zero], axis=0)
    return before, after


def nn(a, b):
    return jnp.dot(a, b, preferred_element_type=F32)


def nt(a, b):
    return lax.dot_general(a, b, (((1,), (1,)), ((), ())), preferred_element_type=F32)


def tn(a, b):
    return lax.dot_general(a, b, (((0,), (0,)), ((), ())), preferred_element_type=F32)


def wide_space(v):
    before, after = columns(v)
    return jnp.concatenate([before, v, after], axis=1).astype(BF16)


def wide_time(v):
    before, after = frames(v)
    return jnp.concatenate([before, v, after], axis=1).astype(BF16)


def space_forward(wide, w):
    same = nn(wide, w[768:1536, :])
    top = nn(wide[HALF:], w[1536:2304, :])
    bottom = nn(wide[:HALF], w[0:768, :])
    return same + jnp.concatenate([top, bottom], axis=0)


def activate(pre):
    sigma = jax.nn.sigmoid(pre)
    hidden = (pre * sigma).astype(BF16).astype(F32)
    return hidden, sigma * (1.0 + pre * (1.0 - sigma))


def g_hidden_of(g, w):
    before, after = frames(g)
    out = nt(after.astype(BF16), w[SPACE : SPACE + 256, :])
    out = out + nt(g.astype(BF16), w[SPACE + 256 : SPACE + 512, :])
    return out + nt(before.astype(BF16), w[SPACE + 512 : SPACE + 768, :])


def space_backward(g_pre, w):
    before, after = columns(g_pre)
    same = top = bottom = None
    for q, v in enumerate((after, g_pre, before)):
        v = v.astype(BF16)
        a = nt(v, w[768 + 256 * q : 1024 + 256 * q, :])
        t = nt(v[HALF:], w[256 * q : 256 * q + 256, :])
        b = nt(v[:HALF], w[1536 + 256 * q : 1792 + 256 * q, :])
        same, top, bottom = (a, t, b) if same is None else (same + a, top + t, bottom + b)
    return same + jnp.concatenate([top, bottom], axis=0)


def kernel(
    scale,
    clips_ref, cot_ref, ws_ref, wt_ref,
    out_s, out_t,
    wv, cl, ct, xin, yout, bx, bg, gin,
    act, bact, xc, hc, gp, gb, dw, part, r1, s1, r2, s2, r3, fin,
    loc, wg_send, wg_recv, ws_send, ws_recv, wy_send, wy_recv,
    x_send, x_recv, bx_send, bx_recv, ct_send, ct_recv,
    go_send, gin_recv, bg_send, bg_recv,
    r1_send, r1_recv, r2_send, r2_recv, r3_send, r3_recv, r4_sem, up, down, answer,
):
    S = lax.axis_index("section")
    D = lax.axis_index("dp")
    half = S // 4
    x = S % 4
    y = D // 16
    z = (D // 2) % 8
    k = D % 2
    far = D + 8 - 16 * (z // 4)
    sibling = D + 1 - 2 * k
    end = jnp.logical_or(x == 0, x == 3)
    mine = jnp.where(x == 0, 1, 0)
    base = half * 4
    odd = y % 2
    lane = lax.rem(D, 16)
    above = lax.rem(y + 1, 4) * 16 + lane
    below = lax.rem(y + 3, 4) * 16 + lane

    def copy(src, dst, send, recv, section, dp):
        return pltpu.make_async_remote_copy(
            src_ref=src, dst_ref=dst, send_sem=send, recv_sem=recv,
            device_id={"section": section, "dp": dp}, device_id_type=MESH,
        )

    local = [
        pltpu.make_async_copy(clips_ref, cl, loc.at[0]),
        pltpu.make_async_copy(ws_ref, wv.at[x, 0:SPACE], loc.at[1]),
        pltpu.make_async_copy(wt_ref, wv.at[x, SPACE : SPACE + TIME], loc.at[2]),
    ]
    for c in local:
        c.start()

    barrier = pltpu.get_barrier_semaphore()

    def hello(section, dp):
        pl.semaphore_signal(
            barrier, inc=1, device_id={"section": section, "dp": dp}, device_id_type=MESH
        )

    hello(S, sibling)
    hello(S, above)
    hello(S, below)
    hello(base + lax.rem(x + 1, 4), D)
    hello(base + lax.rem(x + 3, 4), D)

    @pl.when(z > 0)
    def _():
        hello(S, D - 2)

    @pl.when(z < 7)
    def _():
        hello(S, D + 2)

    @pl.when(S == 0)
    def _():
        hello(4, far)

    @pl.when(S == 3)
    def _():
        hello(7, far)

    @pl.when(jnp.logical_or(S == 4, S == 7))
    def _():
        hello(S, far)

    inner = jnp.logical_and(z > 0, z < 7)
    crossings = jnp.where(jnp.logical_or(S == 4, S == 7), 2, 0)
    pl.semaphore_wait(barrier, 6 + jnp.where(inner, 1, 0) + crossings)

    @pl.when(jnp.logical_or(S == 4, S == 7))
    def _():
        pl.semaphore_signal(
            answer, inc=1, device_id={"section": lax.rem(S + 4, 8), "dp": far}, device_id_type=MESH
        )

    def sweep(sem, step, first, last):
        @pl.when(z != first)
        def _():
            pl.semaphore_wait(sem, 1)

        @pl.when(z != last)
        def _():
            pl.semaphore_signal(
                sem, inc=1, device_id={"section": S, "dp": D + 2 * step}, device_id_type=MESH
            )

    def meet_line():
        @pl.when(z < 4)
        def _():
            sweep(up, 1, 0, 7)
            sweep(down, -1, 7, 0)

        @pl.when(z >= 4)
        def _():
            sweep(down, -1, 7, 0)
            sweep(up, 1, 0, 7)

    for c in local:
        c.wait()

    near = jnp.where(x % 2 == 1, 0, 3)
    passed = jnp.where(x % 2 == 0, 1, 2)
    other = jnp.where(x == 0, 3, 0)
    distant = jnp.where(x == 0, 2, 1)
    middle = jnp.logical_not(end)

    def chunk_copy(j, c, parity, core, send, recv, section, dp):
        n = 8 * parity + 4 * core + 2 * (c % 2) + c // 2
        rows = pl.ds(pl.multiple_of(n * 192, 192), 192)
        return copy(wv.at[j, rows], wv.at[j, rows], send, recv, section, dp)

    def x_chunk(j, c, target, slot):
        return chunk_copy(j, c, odd, k, wg_send.at[slot, c], wg_recv.at[j, c], base + target, D)

    def y_chunk(j, c, parity):
        dp = jnp.where(c % 2 == 1, above, below)
        return chunk_copy(j, c, parity, k, wy_send.at[j, c], wy_recv.at[j, c], S, dp)

    def core_chunk(j, c, far_rows, core):
        parity = 1 - odd if far_rows else odd
        at = 4 * far_rows + c
        return chunk_copy(j, c, parity, core, ws_send.at[j, at], ws_recv.at[j, at], S, sibling)

    def each(body):
        def step(c, carry):
            body(c)
            return carry

        lax.fori_loop(0, 4, step, 0)

    def take_x(j, c):
        x_chunk(j, c, 0, 0).wait_recv()
        y_chunk(j, c, odd).start()

        if c in (0, 3):
            @pl.when(j == passed)
            def _():
                x_chunk(j, c, near, 2).start()

        core_chunk(j, c, 0, k).start()

    def take_y(j, c):
        y_chunk(j, c, 1 - odd).wait_recv()
        core_chunk(j, c, 1, k).start()

    def pass_middle():
        @pl.when(middle)
        def _():
            for c in (1, 2):
                x_chunk(passed, c, 0, 0).wait_recv()
                x_chunk(passed, c, near, 2).start()
                x_chunk(x, c + 1, near, 0).start()

    for c in (0, 1):
        x_chunk(x, c, near, 0).start()

    @pl.when(middle)
    def _():
        for c in (1, 2):
            x_chunk(x, c, 3 - x, 1).start()

    cot_copy = copy(cot_ref.at[mine], ct, ct_send, ct_recv, S, far)

    @pl.when(jnp.logical_or(S == 4, S == 7))
    def _():
        cot_copy.start()

    @pl.when(half == 1)
    def _():
        pass_middle()

        @pl.when(jnp.logical_not(end))
        def _():
            meet_line()

    def rows_of(c, h):
        return pl.ds(pl.multiple_of(h * 128 + c * HALF, HALF), HALF)

    def keep(ref, c, value):
        ref[rows_of(c, 0), :] = value[:HALF]
        ref[rows_of(c, 1), :] = value[HALF:]

    def y_copy(c):
        return copy(yout.at[c], xin.at[c], x_send.at[c], x_recv.at[c], lax.rem(S + 1, 8), D)

    cross_copy = copy(yout.at[0], bx.at[0], x_send.at[0], bx_recv, 7, far)
    hand_copy = copy(yout.at[1], ct, x_send.at[1], ct_recv, 0, D)
    relay_copy = copy(ct, bx.at[0], ct_send, bx_recv, 4, far)

    def owner_hidden(c):
        wide = wide_space(xin[c].astype(F32))
        keep(xc, c, wide)
        hidden, slope = activate(space_forward(wide, wv.at[x]))
        act[c] = slope
        wide = wide_time(hidden)
        keep(hc, c, wide)
        return wide

    def forward(first):
        def clip(c, carry):
            if first:
                xin[c] = by_height(cl[c]).astype(BF16)
            else:
                y_copy(c).wait_recv()
            wide = owner_hidden(c)
            out = xin[c].astype(F32) + nn(wide, wv[x, SPACE : SPACE + TIME, :])
            yout[c] = out.astype(BF16)
            if first:
                y_copy(c).start()
            else:
                @pl.when(x < 3)
                def _():
                    y_copy(c).start()

                @pl.when(jnp.logical_and(x == 3, c == 0))
                def _():
                    pl.semaphore_wait(answer, 1)
                    cross_copy.start()

                @pl.when(jnp.logical_and(x == 3, c == 1))
                def _():
                    hand_copy.start()

            return carry

        lax.fori_loop(0, 2, clip, 0)

    @pl.when(S == 0)
    def _():
        forward(True)

    @pl.when(end)
    def _():
        for c in (0, 1):
            take_x(passed, c)
            take_x(other, c)
            x_chunk(x, c + 2, near, 0).start()

    @pl.when(S == 0)
    def _():
        hand_copy.wait_recv()
        pl.semaphore_wait(answer, 1)
        relay_copy.start()

    @pl.when(jnp.logical_and(half == 0, x > 0))
    def _():
        forward(False)
        pass_middle()

        @pl.when(x < 3)
        def _():
            meet_line()

    def x_copy(j):
        return copy(bx.at[j], xin.at[mine], bx_send.at[j], x_recv.at[mine], base + j, D)

    def g_copy(j):
        return copy(bg.at[j + 1], gin.at[mine], go_send.at[j], gin_recv.at[mine], base + j, D)

    back_copy = copy(bg.at[0], bg.at[4], bg_send, bg_recv, lax.rem(S + 4, 8), far)

    @pl.when(end)
    def _():
        def take_ys(*pairs):
            for j, c in pairs:
                take_y(j, c)

        take_x(distant, 0)
        take_x(distant, 1)
        take_ys((passed, 0), (other, 0))
        take_x(passed, 2)
        take_x(other, 2)
        take_ys((passed, 1), (other, 1))
        take_x(distant, 2)
        take_ys((distant, 0), (distant, 1))
        take_x(passed, 3)
        take_x(other, 3)
        take_ys((passed, 2), (other, 2))
        take_x(distant, 3)
        take_ys((distant, 2), (passed, 3), (other, 3), (distant, 3))
        @each
        def _(c):
            for j in (passed, other, distant):
                core_chunk(j, c, 0, 1 - k).wait_recv()
                core_chunk(j, c, 1, 1 - k).wait_recv()

        @pl.when(half == 0)
        def _():
            bx[0] = by_height(cl[mine]).astype(BF16)

        @pl.when(half == 1)
        def _():
            cross_copy.wait_recv()

        def layer(j, carry):
            @pl.when(half == 1)
            def _():
                @pl.when(j == x)
                def _():
                    xin[mine] = bx[j]

                @pl.when(j != x)
                def _():
                    x_copy(j).start()

            v = bx[j].astype(F32)
            hidden, slope = activate(space_forward(wide_space(v), wv.at[j]))
            bact[j] = slope

            @pl.when(j < 3)
            def _():
                out = v + nn(wide_time(hidden), wv[j, SPACE : SPACE + TIME, :])
                bx[j + 1] = out.astype(BF16)

            return carry

        lax.fori_loop(0, 4, layer, 0)

        @pl.when(half == 0)
        def _():
            meet_line()
            back_copy.wait_recv()

        @pl.when(half == 1)
        def _():
            cot_copy.wait_recv()
            bg[4] = by_height(ct[...]).astype(BF16)

        def layer_back(i, carry):
            j = 3 - i

            @pl.when(j == x)
            def _():
                gin[mine] = bg[j + 1]

            @pl.when(j != x)
            def _():
                g_copy(j).start()

            @pl.when(j + half > 0)
            def _():
                g = bg[j + 1].astype(F32)
                g_pre = (g_hidden_of(g, wv.at[j]) * bact[j]).astype(BF16).astype(F32)
                bg[j] = (g + space_backward(g_pre, wv.at[j])).astype(BF16)

            return carry

        lax.fori_loop(0, 4, layer_back, 0)

        @pl.when(half == 1)
        def _():
            back_copy.start()
            meet_line()

    @pl.when(half == 1)
    def _():
        def clip(c, carry):
            @pl.when(jnp.logical_not(jnp.logical_and(end, c == mine)))
            def _():
                y_copy(c).wait_recv()

            owner_hidden(c)
            return carry

        lax.fori_loop(0, 2, clip, 0)

    def clip_back(i, carry):
        c = jnp.where(i == 0, mine, 1 - mine)

        @pl.when(jnp.logical_not(jnp.logical_and(end, c == mine)))
        def _():
            copy(gin.at[c], gin.at[c], go_send.at[0], gin_recv.at[c], S, D).wait_recv()

        keep(gb, c, gin[c])
        g = gin[c].astype(F32)
        keep(gp, c, (g_hidden_of(g, wv.at[x]) * act[c]).astype(BF16))
        return carry

    lax.fori_loop(0, 2, clip_back, 0)

    for q in range(3):
        lanes = slice(256 * q, 256 * q + 256)
        dw[SPACE + 256 * q : SPACE + 256 * q + 256, :] = tn(hc[:, lanes], gb[...])
        dw[256 * q : 256 * q + 256, :] = tn(xc[0:128, lanes], gp[128:256, :])
        dw[768 + 256 * q : 1024 + 256 * q, :] = tn(xc[:, lanes], gp[...])
        dw[1536 + 256 * q : 1792 + 256 * q, :] = tn(xc[128:256, lanes], gp[0:128, :])

    blocks = [lax.rem(y + i, 4) for i in (2, 1, 3, 0)]
    sides = (lax.rem(y + 1, 4), lax.rem(y + 3, 4))

    def core_step(i, column):
        yb = blocks[i]
        return copy(part.at[column, yb], r1.at[yb], r1_send.at[i], r1_recv.at[i], S, sibling)

    for i in range(4):
        def pack(b, carry):
            n = blocks[i] * 8 + b
            top = dw[pl.ds(pl.multiple_of(n * 72, 8), 72), :]
            low = dw[pl.ds(pl.multiple_of(SPACE + n * 24, 8), 24), :]
            block = jnp.concatenate([top, low], axis=0).astype(BF16)
            part[0, blocks[i], b] = block[:, 0:128]
            part[1, blocks[i], b] = block[:, 128:256]
            return carry

        lax.fori_loop(0, 8, pack, 0)
        core_step(i, 1 - k).start()

    def add_cores(yb, start, stop):
        def one(b, carry):
            s1[yb, b] = (part[k, yb, b].astype(F32) + r1[yb, b].astype(F32)).astype(BF16)
            return carry

        lax.fori_loop(start, stop, one, 0)

    def y_step(i, side):
        forth, back = sides[side], sides[1 - side]
        to = (forth, back, forth)[i]
        some = pl.ds(4 * side, 4)
        return copy(
            s1.at[blocks[0] if i == 0 else to, some], r2.at[i, some],
            r2_send.at[i, side], r2_recv.at[i, side], S, to * 16 + lane,
        )

    core_step(0, k).wait_recv()
    add_cores(blocks[0], 0, 8)
    y_step(0, 0).start()
    y_step(0, 1).start()
    for side in (1, 0):
        core_step(2 - side, k).wait_recv()
        add_cores(sides[1 - side], 4 * side, 4 * side + 4)
        y_step(1, side).start()
    for side in range(2):
        forth = sides[side]
        y_step(0, side).wait_recv()

        def add_relayed(b, carry):
            total = part[k, forth, b].astype(F32) + r1[forth, b].astype(F32) + r2[0, b].astype(F32)
            s1[forth, b] = total.astype(BF16)
            return carry

        lax.fori_loop(4 * side, 4 * side + 4, add_relayed, 0)
        y_step(2, side).start()
    core_step(3, k).wait_recv()
    for i in (1, 2):
        for side in range(2):
            y_step(i, side).wait_recv()
    def add_y(b, carry):
        total = part[k, y, b].astype(F32) + r1[y, b].astype(F32) + r2[1, b].astype(F32) + r2[2, b].astype(F32)
        s2[b] = total.astype(BF16)
        return carry

    lax.fori_loop(0, 8, add_y, 0)

    def z_step(i):
        to = lax.rem(z + i, 8)
        return copy(s2.at[to], r3.at[i - 1], r3_send.at[i - 1], r3_recv.at[i - 1], S, y * 16 + to * 2 + k)

    for i in range(1, 8):
        z_step(i).start()
    for i in range(1, 8):
        z_step(i).wait_recv()

    total = s2[z].astype(F32)
    for i in range(7):
        total = total + r3[i].astype(F32)
    fin[k] = total * scale

    final = copy(fin.at[k], fin.at[k], r4_sem.at[0], r4_sem.at[1], S, sibling)
    final.start()
    final.wait_send()
    copy(fin.at[1 - k], fin.at[1 - k], r4_sem.at[0], r4_sem.at[1], S, sibling).wait_recv()

    for core in range(2):
        @pl.when(k == core)
        def _():
            for side in range(2):
                lanes = slice(128 * side, 128 * side + 128)
                out_s[:, lanes] = fin[side, 36 * core : 36 * core + 36, :]
                out_t[:, lanes] = fin[side, 72 + 12 * core : 84 + 12 * core, :]

    for i in range(4):
        core_step(i, 1 - k).wait_send()
    for i in range(3):
        for side in range(2):
            y_step(i, side).wait_send()
    for i in range(1, 8):
        z_step(i).wait_send()
    @each
    def _(c):
        x_chunk(x, c, near, 0).wait_send()

        between = jnp.logical_or(c == 1, c == 2)

        @pl.when(jnp.logical_and(middle, between))
        def _():
            x_chunk(x, c, 3 - x, 1).wait_send()

        @pl.when(middle == between)
        def _():
            x_chunk(passed, c, near, 2).wait_send()

        @pl.when(end)
        def _():
            for j in (passed, other, distant):
                y_chunk(j, c, odd).wait_send()
                core_chunk(j, c, 0, k).wait_send()
                core_chunk(j, c, 1, k).wait_send()

    @pl.when(jnp.logical_or(S == 4, S == 7))
    def _():
        cot_copy.wait_send()

    @pl.when(S == 0)
    def _():
        relay_copy.wait_send()

    @pl.when(half == 0)
    def _():
        for c in range(2):
            y_copy(c).wait_send()

    @pl.when(end)
    def _():
        for i in range(1, 4):
            j = lax.rem(x + i, 4)
            g_copy(j).wait_send()

            @pl.when(half == 1)
            def _():
                x_copy(j).wait_send()

        @pl.when(half == 1)
        def _():
            back_copy.wait_send()


def body(clips, cotangent, spatial_kernel, temporal_kernel):
    micro = clips.shape[0]
    tile = clips.shape[1:]
    cells = tile[0] * tile[1] * tile[2]
    scale = 1.0 / math.sqrt(micro * lax.axis_size("dp") * cells)
    sem = pltpu.SemaphoreType.DMA
    vmem = pltpu.VMEM
    out_s, out_t = pl.pallas_call(
        functools.partial(kernel, scale),
        out_shape=(jax.ShapeDtypeStruct((36, C), F32), jax.ShapeDtypeStruct((12, C), F32)),
        in_specs=[pl.BlockSpec(memory_space=pltpu.HBM)] * 4,
        out_specs=(pl.BlockSpec(memory_space=pltpu.VMEM),) * 2,
        scratch_shapes=[
            vmem((4, SPACE + TIME, C), BF16),
            vmem((2, ROWS, C), BF16),
            vmem((ROWS, C), BF16),
            vmem((2, ROWS, C), BF16),
            vmem((2, ROWS, C), BF16),
            vmem((4, ROWS, C), BF16),
            vmem((5, ROWS, C), BF16),
            vmem((2, ROWS, C), BF16),
            vmem((2, ROWS, C), F32),
            vmem((4, ROWS, C), F32),
            vmem((2 * ROWS, 3 * C), BF16),
            vmem((2 * ROWS, 3 * C), BF16),
            vmem((2 * ROWS, C), BF16),
            vmem((2 * ROWS, C), BF16),
            vmem((SPACE + TIME, C), F32),
            vmem((2, 4, 8, 96, 128), BF16),
            vmem((4, 8, 96, 128), BF16),
            vmem((4, 8, 96, 128), BF16),
            vmem((3, 8, 96, 128), BF16),
            vmem((8, 96, 128), BF16),
            vmem((7, 96, 128), BF16),
            vmem((2, 96, 128), F32),
            sem((3,)),
            sem((3, 4)),
            sem((4, 4)),
            sem((4, 8)),
            sem((4, 8)),
            sem((4, 4)),
            sem((4, 4)),
            sem((2,)),
            sem((2,)),
            sem((4,)),
            sem,
            sem,
            sem,
            sem((4,)),
            sem((2,)),
            sem,
            sem,
            sem((4,)),
            sem((4,)),
            sem((3, 2)),
            sem((3, 2)),
            sem((7,)),
            sem((7,)),
            sem((2,)),
            pltpu.SemaphoreType.REGULAR,
            pltpu.SemaphoreType.REGULAR,
            pltpu.SemaphoreType.REGULAR,
        ],
        compiler_params=pltpu.CompilerParams(
            collective_id=0, has_side_effects=True, vmem_limit_bytes=66_900_000
        ),
        name="window",
    )(
        clips.reshape(micro, cells, tile[3]),
        cotangent.reshape(micro, cells, tile[3]),
        spatial_kernel[0],
        temporal_kernel[0],
    )
    return (out_s[None], out_t[None])


def solution(mesh):
    return jax.shard_map(
        body,
        mesh=mesh,
        in_specs=(
            P("dp", None, None, None, None),
            P("dp", None, None, None, None),
            P("section", None, None),
            P("section", None, None),
        ),
        out_specs=(P("section", "dp", None), P("section", "dp", None)),
        check_vma=False,
    )
```

```python
import functools
import math

import jax
import jax.numpy as jnp
from jax import lax
from jax.experimental import pallas as pl
from jax.experimental.pallas import tpu as pltpu
from jax.sharding import PartitionSpec as P

MESH = pl.DeviceIdType.MESH
F32 = jnp.float32
BF16 = jnp.bfloat16
C = 256
ROWS = 128
HALF = 64
SPACE = 9 * C
TIME = 3 * C


def by_height(v):
    v = v.astype(F32).reshape(8, 2, 8, C)
    return jnp.concatenate([v[:, 0].reshape(HALF, C), v[:, 1].reshape(HALF, C)], axis=0)


def columns(v):
    w = lax.broadcasted_iota(jnp.int32, v.shape, 0) & 7
    before = jnp.where(w == 0, 0.0, pltpu.roll(v, 1, 0))
    after = jnp.where(w == 7, 0.0, pltpu.roll(v, ROWS - 1, 0))
    return before, after


def frames(v):
    zero = jnp.zeros((8, C), F32)
    before = jnp.concatenate([zero, v[0:56], zero, v[64:120]], axis=0)
    after = jnp.concatenate([v[8:64], zero, v[72:128], zero], axis=0)
    return before, after


def nn(a, b):
    return jnp.dot(a, b, preferred_element_type=F32)


def nt(a, b):
    return lax.dot_general(a, b, (((1,), (1,)), ((), ())), preferred_element_type=F32)


def tn(a, b):
    return lax.dot_general(a, b, (((0,), (0,)), ((), ())), preferred_element_type=F32)


def wide_space(v):
    before, after = columns(v)
    return jnp.concatenate([before, v, after], axis=1).astype(BF16)


def wide_time(v):
    before, after = frames(v)
    return jnp.concatenate([before, v, after], axis=1).astype(BF16)


def space_forward(wide, w):
    same = nn(wide, w[768:1536, :])
    top = nn(wide[HALF:], w[1536:2304, :])
    bottom = nn(wide[:HALF], w[0:768, :])
    return same + jnp.concatenate([top, bottom], axis=0)


def activate(pre):
    sigma = jax.nn.sigmoid(pre)
    hidden = (pre * sigma).astype(BF16).astype(F32)
    return hidden, sigma * (1.0 + pre * (1.0 - sigma))


def g_hidden_of(g, w):
    before, after = frames(g)
    out = nt(after.astype(BF16), w[SPACE : SPACE + 256, :])
    out = out + nt(g.astype(BF16), w[SPACE + 256 : SPACE + 512, :])
    return out + nt(before.astype(BF16), w[SPACE + 512 : SPACE + 768, :])


def space_backward(g_pre, w):
    before, after = columns(g_pre)
    same = top = bottom = None
    for q, v in enumerate((after, g_pre, before)):
        v = v.astype(BF16)
        a = nt(v, w[768 + 256 * q : 1024 + 256 * q, :])
        t = nt(v[HALF:], w[256 * q : 256 * q + 256, :])
        b = nt(v[:HALF], w[1536 + 256 * q : 1792 + 256 * q, :])
        same, top, bottom = (a, t, b) if same is None else (same + a, top + t, bottom + b)
    return same + jnp.concatenate([top, bottom], axis=0)


def kernel(
    scale,
    clips_ref, cot_ref, ws_ref, wt_ref,
    out_s, out_t,
    wv, cl, ct, xin, yout, bx, bg, gin,
    act, bact, xc, hc, gp, gb, dw, part, r1, s1, r2, s2, r3, fin,
    loc, wg_send, wg_recv, ws_send, ws_recv, wy_send, wy_recv,
    x_send, x_recv, bx_send, bx_recv, ct_send, ct_recv,
    go_send, gin_recv, bg_send, bg_recv,
    r1_send, r1_recv, r2_send, r2_recv, r3_send, r3_recv, r4_sem, up, down, answer,
):
    S = lax.axis_index("section")
    D = lax.axis_index("dp")
    half = S // 4
    x = S % 4
    y = D // 16
    z = (D // 2) % 8
    k = D % 2
    far = D + 8 - 16 * (z // 4)
    sibling = D + 1 - 2 * k
    end = jnp.logical_or(x == 0, x == 3)
    mine = jnp.where(x == 0, 1, 0)
    base = half * 4
    odd = y % 2
    lane = lax.rem(D, 16)
    above = lax.rem(y + 1, 4) * 16 + lane
    below = lax.rem(y + 3, 4) * 16 + lane

    def copy(src, dst, send, recv, section, dp):
        return pltpu.make_async_remote_copy(
            src_ref=src, dst_ref=dst, send_sem=send, recv_sem=recv,
            device_id={"section": section, "dp": dp}, device_id_type=MESH,
        )

    local = [
        pltpu.make_async_copy(clips_ref, cl, loc.at[0]),
        pltpu.make_async_copy(ws_ref, wv.at[x, 0:SPACE], loc.at[1]),
        pltpu.make_async_copy(wt_ref, wv.at[x, SPACE : SPACE + TIME], loc.at[2]),
    ]
    for c in local:
        c.start()

    barrier = pltpu.get_barrier_semaphore()

    def hello(section, dp):
        pl.semaphore_signal(
            barrier, inc=1, device_id={"section": section, "dp": dp}, device_id_type=MESH
        )

    hello(S, sibling)
    hello(S, above)
    hello(S, below)
    hello(base + lax.rem(x + 1, 4), D)
    hello(base + lax.rem(x + 3, 4), D)

    @pl.when(z > 0)
    def _():
        hello(S, D - 2)

    @pl.when(z < 7)
    def _():
        hello(S, D + 2)

    @pl.when(S == 0)
    def _():
        hello(4, far)

    @pl.when(S == 3)
    def _():
        hello(7, far)

    @pl.when(jnp.logical_or(S == 4, S == 7))
    def _():
        hello(S, far)

    inner = jnp.logical_and(z > 0, z < 7)
    crossings = jnp.where(jnp.logical_or(S == 4, S == 7), 2, 0)
    pl.semaphore_wait(barrier, 6 + jnp.where(inner, 1, 0) + crossings)

    @pl.when(jnp.logical_or(S == 4, S == 7))
    def _():
        pl.semaphore_signal(
            answer, inc=1, device_id={"section": lax.rem(S + 4, 8), "dp": far}, device_id_type=MESH
        )

    def sweep(sem, step, first, last):
        @pl.when(z != first)
        def _():
            pl.semaphore_wait(sem, 1)

        @pl.when(z != last)
        def _():
            pl.semaphore_signal(
                sem, inc=1, device_id={"section": S, "dp": D + 2 * step}, device_id_type=MESH
            )

    def meet_line():
        @pl.when(z < 4)
        def _():
            sweep(up, 1, 0, 7)
            sweep(down, -1, 7, 0)

        @pl.when(z >= 4)
        def _():
            sweep(down, -1, 7, 0)
            sweep(up, 1, 0, 7)

    for c in local:
        c.wait()

    near = jnp.where(x % 2 == 1, 0, 3)
    passed = jnp.where(x % 2 == 0, 1, 2)
    other = jnp.where(x == 0, 3, 0)
    distant = jnp.where(x == 0, 2, 1)
    middle = jnp.logical_not(end)

    def between(c):
        return jnp.logical_or(c == 1, c == 2)

    def chunk_copy(j, c, parity, core, send, recv, section, dp):
        n = 8 * parity + 4 * core + 2 * (c % 2) + c // 2
        rows = pl.ds(pl.multiple_of(n * 192, 192), 192)
        return copy(wv.at[j, rows], wv.at[j, rows], send, recv, section, dp)

    def x_chunk(j, c, target, slot):
        return chunk_copy(j, c, odd, k, wg_send.at[slot, c], wg_recv.at[j, c], base + target, D)

    def y_chunk(j, c, parity):
        dp = jnp.where(c % 2 == 1, above, below)
        return chunk_copy(j, c, parity, k, wy_send.at[j, c], wy_recv.at[j, c], S, dp)

    def core_chunk(j, c, far_rows, core):
        parity = 1 - odd if far_rows else odd
        at = 4 * far_rows + c
        return chunk_copy(j, c, parity, core, ws_send.at[j, at], ws_recv.at[j, at], S, sibling)

    def each(body):
        def step(c, carry):
            body(c)
            return carry

        lax.fori_loop(0, 4, step, 0)

    def take_x(j, c):
        x_chunk(j, c, 0, 0).wait_recv()
        y_chunk(j, c, odd).start()

        @pl.when(jnp.logical_and(j == passed, jnp.logical_not(between(c))))
        def _():
            x_chunk(j, c, near, 2).start()

        core_chunk(j, c, 0, k).start()

    def take_y(j, c):
        y_chunk(j, c, 1 - odd).wait_recv()
        core_chunk(j, c, 1, k).start()

    def pass_middle():
        @pl.when(middle)
        def _():
            for c in (1, 2):
                x_chunk(passed, c, 0, 0).wait_recv()
                x_chunk(passed, c, near, 2).start()

    @each
    def _(c):
        x_chunk(x, c, near, 0).start()

        @pl.when(jnp.logical_and(middle, between(c)))
        def _():
            x_chunk(x, c, 3 - x, 1).start()

    cot_copy = copy(cot_ref.at[mine], ct, ct_send, ct_recv, S, far)

    @pl.when(jnp.logical_or(S == 4, S == 7))
    def _():
        cot_copy.start()

    @pl.when(half == 1)
    def _():
        pass_middle()

        @pl.when(jnp.logical_not(end))
        def _():
            meet_line()

    def rows_of(c, h):
        return pl.ds(pl.multiple_of(h * 128 + c * HALF, HALF), HALF)

    def keep(ref, c, value):
        ref[rows_of(c, 0), :] = value[:HALF]
        ref[rows_of(c, 1), :] = value[HALF:]

    def y_copy(c):
        return copy(yout.at[c], xin.at[c], x_send.at[c], x_recv.at[c], lax.rem(S + 1, 8), D)

    cross_copy = copy(yout.at[0], bx.at[0], x_send.at[0], bx_recv, 7, far)
    hand_copy = copy(yout.at[1], ct, x_send.at[1], ct_recv, 0, D)
    relay_copy = copy(ct, bx.at[0], ct_send, bx_recv, 4, far)

    def owner_hidden(c):
        wide = wide_space(xin[c].astype(F32))
        keep(xc, c, wide)
        hidden, slope = activate(space_forward(wide, wv.at[x]))
        act[c] = slope
        wide = wide_time(hidden)
        keep(hc, c, wide)
        return wide

    def forward(first):
        def clip(c, carry):
            if first:
                xin[c] = by_height(cl[c]).astype(BF16)
            else:
                y_copy(c).wait_recv()
            wide = owner_hidden(c)
            out = xin[c].astype(F32) + nn(wide, wv[x, SPACE : SPACE + TIME, :])
            yout[c] = out.astype(BF16)
            if first:
                y_copy(c).start()
            else:
                @pl.when(x < 3)
                def _():
                    y_copy(c).start()

                @pl.when(jnp.logical_and(x == 3, c == 0))
                def _():
                    pl.semaphore_wait(answer, 1)
                    cross_copy.start()

                @pl.when(jnp.logical_and(x == 3, c == 1))
                def _():
                    hand_copy.start()

            return carry

        lax.fori_loop(0, 2, clip, 0)

    @pl.when(S == 0)
    def _():
        forward(True)

    @pl.when(jnp.logical_or(S == 0, S == 3))
    def _():
        meet_line()

    @pl.when(end)
    def _():
        @each
        def _(c):
            take_x(passed, c)
            take_x(other, c)

    @pl.when(S == 0)
    def _():
        hand_copy.wait_recv()
        pl.semaphore_wait(answer, 1)
        relay_copy.start()

    @pl.when(jnp.logical_and(half == 0, x > 0))
    def _():
        forward(False)
        pass_middle()

        @pl.when(x < 3)
        def _():
            meet_line()

    def x_copy(j):
        return copy(bx.at[j], xin.at[mine], bx_send.at[j], x_recv.at[mine], base + j, D)

    def g_copy(j):
        return copy(bg.at[j + 1], gin.at[mine], go_send.at[j], gin_recv.at[mine], base + j, D)

    back_copy = copy(bg.at[0], bg.at[4], bg_send, bg_recv, lax.rem(S + 4, 8), far)

    @pl.when(end)
    def _():
        @each
        def _(c):
            take_x(distant, c)
            take_y(passed, c)
            take_y(other, c)
        @each
        def _(c):
            take_y(distant, c)
        @each
        def _(c):
            for j in (passed, other, distant):
                core_chunk(j, c, 0, 1 - k).wait_recv()
                core_chunk(j, c, 1, 1 - k).wait_recv()

        @pl.when(half == 0)
        def _():
            bx[0] = by_height(cl[mine]).astype(BF16)

        @pl.when(half == 1)
        def _():
            cross_copy.wait_recv()

        def layer(j, carry):
            @pl.when(half == 1)
            def _():
                @pl.when(j == x)
                def _():
                    xin[mine] = bx[j]

                @pl.when(j != x)
                def _():
                    x_copy(j).start()

            v = bx[j].astype(F32)
            hidden, slope = activate(space_forward(wide_space(v), wv.at[j]))
            bact[j] = slope

            @pl.when(j < 3)
            def _():
                out = v + nn(wide_time(hidden), wv[j, SPACE : SPACE + TIME, :])
                bx[j + 1] = out.astype(BF16)

            return carry

        lax.fori_loop(0, 4, layer, 0)

        @pl.when(half == 0)
        def _():
            back_copy.wait_recv()

        @pl.when(half == 1)
        def _():
            cot_copy.wait_recv()
            bg[4] = by_height(ct[...]).astype(BF16)

        def layer_back(i, carry):
            j = 3 - i

            @pl.when(j == x)
            def _():
                gin[mine] = bg[j + 1]

            @pl.when(j != x)
            def _():
                g_copy(j).start()

            @pl.when(j + half > 0)
            def _():
                g = bg[j + 1].astype(F32)
                g_pre = (g_hidden_of(g, wv.at[j]) * bact[j]).astype(BF16).astype(F32)
                bg[j] = (g + space_backward(g_pre, wv.at[j])).astype(BF16)

            return carry

        lax.fori_loop(0, 4, layer_back, 0)

        @pl.when(half == 1)
        def _():
            back_copy.start()
            meet_line()

    @pl.when(half == 1)
    def _():
        def clip(c, carry):
            @pl.when(jnp.logical_not(jnp.logical_and(end, c == mine)))
            def _():
                y_copy(c).wait_recv()

            owner_hidden(c)
            return carry

        lax.fori_loop(0, 2, clip, 0)

    def clip_back(i, carry):
        c = jnp.where(i == 0, mine, 1 - mine)

        @pl.when(jnp.logical_not(jnp.logical_and(end, c == mine)))
        def _():
            copy(gin.at[c], gin.at[c], go_send.at[0], gin_recv.at[c], S, D).wait_recv()

        keep(gb, c, gin[c])
        g = gin[c].astype(F32)
        keep(gp, c, (g_hidden_of(g, wv.at[x]) * act[c]).astype(BF16))
        return carry

    lax.fori_loop(0, 2, clip_back, 0)

    for q in range(3):
        lanes = slice(256 * q, 256 * q + 256)
        dw[SPACE + 256 * q : SPACE + 256 * q + 256, :] = tn(hc[:, lanes], gb[...])
        dw[256 * q : 256 * q + 256, :] = tn(xc[0:128, lanes], gp[128:256, :])
        dw[768 + 256 * q : 1024 + 256 * q, :] = tn(xc[:, lanes], gp[...])
        dw[1536 + 256 * q : 1792 + 256 * q, :] = tn(xc[128:256, lanes], gp[0:128, :])

    blocks = [lax.rem(y + i, 4) for i in (2, 1, 3, 0)]
    sides = (lax.rem(y + 1, 4), lax.rem(y + 3, 4))

    def core_step(i, column):
        yb = blocks[i]
        return copy(part.at[column, yb], r1.at[yb], r1_send.at[i], r1_recv.at[i], S, sibling)

    for i in range(4):
        def pack(b, carry):
            n = blocks[i] * 8 + b
            top = dw[pl.ds(pl.multiple_of(n * 72, 8), 72), :]
            low = dw[pl.ds(pl.multiple_of(SPACE + n * 24, 8), 24), :]
            block = jnp.concatenate([top, low], axis=0).astype(BF16)
            part[0, blocks[i], b] = block[:, 0:128]
            part[1, blocks[i], b] = block[:, 128:256]
            return carry

        lax.fori_loop(0, 8, pack, 0)
        core_step(i, 1 - k).start()

    def add_cores(yb, start, stop):
        def one(b, carry):
            s1[yb, b] = (part[k, yb, b].astype(F32) + r1[yb, b].astype(F32)).astype(BF16)
            return carry

        lax.fori_loop(start, stop, one, 0)

    def y_step(i, side):
        forth, back = sides[side], sides[1 - side]
        to = (forth, back, forth)[i]
        some = pl.ds(4 * side, 4)
        return copy(
            s1.at[blocks[0] if i == 0 else to, some], r2.at[i, some],
            r2_send.at[i, side], r2_recv.at[i, side], S, to * 16 + lane,
        )

    core_step(0, k).wait_recv()
    add_cores(blocks[0], 0, 8)
    y_step(0, 0).start()
    y_step(0, 1).start()
    for side in (1, 0):
        core_step(2 - side, k).wait_recv()
        add_cores(sides[1 - side], 4 * side, 4 * side + 4)
        y_step(1, side).start()
    for side in range(2):
        forth = sides[side]
        y_step(0, side).wait_recv()

        def add_relayed(b, carry):
            total = part[k, forth, b].astype(F32) + r1[forth, b].astype(F32) + r2[0, b].astype(F32)
            s1[forth, b] = total.astype(BF16)
            return carry

        lax.fori_loop(4 * side, 4 * side + 4, add_relayed, 0)
        y_step(2, side).start()
    core_step(3, k).wait_recv()
    for i in (1, 2):
        for side in range(2):
            y_step(i, side).wait_recv()
    def add_y(b, carry):
        total = part[k, y, b].astype(F32) + r1[y, b].astype(F32) + r2[1, b].astype(F32) + r2[2, b].astype(F32)
        s2[b] = total.astype(BF16)
        return carry

    lax.fori_loop(0, 8, add_y, 0)

    def z_step(i):
        to = lax.rem(z + i, 8)
        return copy(s2.at[to], r3.at[i - 1], r3_send.at[i - 1], r3_recv.at[i - 1], S, y * 16 + to * 2 + k)

    for i in range(1, 8):
        z_step(i).start()
    for i in range(1, 8):
        z_step(i).wait_recv()

    total = s2[z].astype(F32)
    for i in range(7):
        total = total + r3[i].astype(F32)
    fin[k] = total * scale

    final = copy(fin.at[k], fin.at[k], r4_sem.at[0], r4_sem.at[1], S, sibling)
    final.start()
    final.wait_send()
    copy(fin.at[1 - k], fin.at[1 - k], r4_sem.at[0], r4_sem.at[1], S, sibling).wait_recv()

    for core in range(2):
        @pl.when(k == core)
        def _():
            for side in range(2):
                lanes = slice(128 * side, 128 * side + 128)
                out_s[:, lanes] = fin[side, 36 * core : 36 * core + 36, :]
                out_t[:, lanes] = fin[side, 72 + 12 * core : 84 + 12 * core, :]

    for i in range(4):
        core_step(i, 1 - k).wait_send()
    for i in range(3):
        for side in range(2):
            y_step(i, side).wait_send()
    for i in range(1, 8):
        z_step(i).wait_send()
    @each
    def _(c):
        x_chunk(x, c, near, 0).wait_send()

        @pl.when(jnp.logical_and(middle, between(c)))
        def _():
            x_chunk(x, c, 3 - x, 1).wait_send()

        @pl.when(middle == between(c))
        def _():
            x_chunk(passed, c, near, 2).wait_send()

        @pl.when(end)
        def _():
            for j in (passed, other, distant):
                y_chunk(j, c, odd).wait_send()
                core_chunk(j, c, 0, k).wait_send()
                core_chunk(j, c, 1, k).wait_send()

    @pl.when(jnp.logical_or(S == 4, S == 7))
    def _():
        cot_copy.wait_send()

    @pl.when(S == 0)
    def _():
        relay_copy.wait_send()

    @pl.when(half == 0)
    def _():
        for c in range(2):
            y_copy(c).wait_send()

    @pl.when(end)
    def _():
        for i in range(1, 4):
            j = lax.rem(x + i, 4)
            g_copy(j).wait_send()

            @pl.when(half == 1)
            def _():
                x_copy(j).wait_send()

        @pl.when(half == 1)
        def _():
            back_copy.wait_send()


def body(clips, cotangent, spatial_kernel, temporal_kernel):
    micro = clips.shape[0]
    tile = clips.shape[1:]
    cells = tile[0] * tile[1] * tile[2]
    scale = 1.0 / math.sqrt(micro * lax.axis_size("dp") * cells)
    sem = pltpu.SemaphoreType.DMA
    vmem = pltpu.VMEM
    out_s, out_t = pl.pallas_call(
        functools.partial(kernel, scale),
        out_shape=(jax.ShapeDtypeStruct((36, C), F32), jax.ShapeDtypeStruct((12, C), F32)),
        in_specs=[pl.BlockSpec(memory_space=pltpu.HBM)] * 4,
        out_specs=(pl.BlockSpec(memory_space=pltpu.VMEM),) * 2,
        scratch_shapes=[
            vmem((4, SPACE + TIME, C), BF16),
            vmem((2, ROWS, C), BF16),
            vmem((ROWS, C), BF16),
            vmem((2, ROWS, C), BF16),
            vmem((2, ROWS, C), BF16),
            vmem((4, ROWS, C), BF16),
            vmem((5, ROWS, C), BF16),
            vmem((2, ROWS, C), BF16),
            vmem((2, ROWS, C), F32),
            vmem((4, ROWS, C), F32),
            vmem((2 * ROWS, 3 * C), BF16),
            vmem((2 * ROWS, 3 * C), BF16),
            vmem((2 * ROWS, C), BF16),
            vmem((2 * ROWS, C), BF16),
            vmem((SPACE + TIME, C), F32),
            vmem((2, 4, 8, 96, 128), BF16),
            vmem((4, 8, 96, 128), BF16),
            vmem((4, 8, 96, 128), BF16),
            vmem((3, 8, 96, 128), BF16),
            vmem((8, 96, 128), BF16),
            vmem((7, 96, 128), BF16),
            vmem((2, 96, 128), F32),
            sem((3,)),
            sem((3, 4)),
            sem((4, 4)),
            sem((4, 8)),
            sem((4, 8)),
            sem((4, 4)),
            sem((4, 4)),
            sem((2,)),
            sem((2,)),
            sem((4,)),
            sem,
            sem,
            sem,
            sem((4,)),
            sem((2,)),
            sem,
            sem,
            sem((4,)),
            sem((4,)),
            sem((3, 2)),
            sem((3, 2)),
            sem((7,)),
            sem((7,)),
            sem((2,)),
            pltpu.SemaphoreType.REGULAR,
            pltpu.SemaphoreType.REGULAR,
            pltpu.SemaphoreType.REGULAR,
        ],
        compiler_params=pltpu.CompilerParams(
            collective_id=0, has_side_effects=True, vmem_limit_bytes=66_900_000
        ),
        name="window",
    )(
        clips.reshape(micro, cells, tile[3]),
        cotangent.reshape(micro, cells, tile[3]),
        spatial_kernel[0],
        temporal_kernel[0],
    )
    return (out_s[None], out_t[None])


def solution(mesh):
    return jax.shard_map(
        body,
        mesh=mesh,
        in_specs=(
            P("dp", None, None, None, None),
            P("dp", None, None, None, None),
            P("section", None, None),
            P("section", None, None),
        ),
        out_specs=(P("section", "dp", None), P("section", "dp", None)),
        check_vma=False,
    )
```

```python
import functools
import math

import jax
import jax.numpy as jnp
from jax import lax
from jax.experimental import pallas as pl
from jax.experimental.pallas import tpu as pltpu
from jax.sharding import PartitionSpec as P

MESH = pl.DeviceIdType.MESH
F32 = jnp.float32
BF16 = jnp.bfloat16
C = 256
ROWS = 128
HALF = 64
SPACE = 9 * C
TIME = 3 * C


def by_height(v):
    v = v.astype(F32).reshape(8, 2, 8, C)
    return jnp.concatenate([v[:, 0].reshape(HALF, C), v[:, 1].reshape(HALF, C)], axis=0)


def columns(v):
    w = lax.broadcasted_iota(jnp.int32, v.shape, 0) & 7
    before = jnp.where(w == 0, 0.0, pltpu.roll(v, 1, 0))
    after = jnp.where(w == 7, 0.0, pltpu.roll(v, ROWS - 1, 0))
    return before, after


def frames(v):
    zero = jnp.zeros((8, C), F32)
    before = jnp.concatenate([zero, v[0:56], zero, v[64:120]], axis=0)
    after = jnp.concatenate([v[8:64], zero, v[72:128], zero], axis=0)
    return before, after


def nn(a, b):
    return jnp.dot(a, b, preferred_element_type=F32)


def nt(a, b):
    return lax.dot_general(a, b, (((1,), (1,)), ((), ())), preferred_element_type=F32)


def tn(a, b):
    return lax.dot_general(a, b, (((0,), (0,)), ((), ())), preferred_element_type=F32)


def wide_space(v):
    before, after = columns(v)
    return jnp.concatenate([before, v, after], axis=1).astype(BF16)


def wide_time(v):
    before, after = frames(v)
    return jnp.concatenate([before, v, after], axis=1).astype(BF16)


def space_forward(wide, w):
    same = nn(wide, w[768:1536, :])
    top = nn(wide[HALF:], w[1536:2304, :])
    bottom = nn(wide[:HALF], w[0:768, :])
    return same + jnp.concatenate([top, bottom], axis=0)


def activate(pre):
    sigma = jax.nn.sigmoid(pre)
    hidden = (pre * sigma).astype(BF16).astype(F32)
    return hidden, sigma * (1.0 + pre * (1.0 - sigma))


def g_hidden_of(g, w):
    before, after = frames(g)
    out = nt(after.astype(BF16), w[SPACE : SPACE + 256, :])
    out = out + nt(g.astype(BF16), w[SPACE + 256 : SPACE + 512, :])
    return out + nt(before.astype(BF16), w[SPACE + 512 : SPACE + 768, :])


def space_backward(g_pre, w):
    before, after = columns(g_pre)
    same = top = bottom = None
    for q, v in enumerate((after, g_pre, before)):
        v = v.astype(BF16)
        a = nt(v, w[768 + 256 * q : 1024 + 256 * q, :])
        t = nt(v[HALF:], w[256 * q : 256 * q + 256, :])
        b = nt(v[:HALF], w[1536 + 256 * q : 1792 + 256 * q, :])
        same, top, bottom = (a, t, b) if same is None else (same + a, top + t, bottom + b)
    return same + jnp.concatenate([top, bottom], axis=0)


def g_hidden_turned(g, w):
    before, after = frames(g)
    wide = jnp.concatenate([after, g, before], axis=1).astype(BF16)
    return nn(wide, w[SPACE : SPACE + TIME, :])


def space_backward_turned(g_pre, w):
    before, after = columns(g_pre)
    wide = jnp.concatenate([after, g_pre, before], axis=1).astype(BF16)
    same = nn(wide, w[768:1536, :])
    top = nn(wide[HALF:], w[0:768, :])
    bottom = nn(wide[:HALF], w[1536:2304, :])
    return same + jnp.concatenate([top, bottom], axis=0)


def kernel(
    scale,
    clips_ref, cot_ref, ws_ref, wt_ref,
    out_s, out_t,
    wv, turned, cl, ct, xin, yout, bx, bg, gin,
    act, bact, xc, hc, gp, gb, dw, part, r1, s1, r2, s2, r3, fin,
    loc, wg_send, wg_recv, ws_send, ws_recv, wy_send, wy_recv,
    x_send, x_recv, bx_send, bx_recv, ct_send, ct_recv,
    go_send, gin_recv, bg_send, bg_recv,
    r1_send, r1_recv, r2_send, r2_recv, r3_send, r3_recv, r4_sem, up, down, answer,
):
    S = lax.axis_index("section")
    D = lax.axis_index("dp")
    half = S // 4
    x = S % 4
    y = D // 16
    z = (D // 2) % 8
    k = D % 2
    far = D + 8 - 16 * (z // 4)
    sibling = D + 1 - 2 * k
    end = jnp.logical_or(x == 0, x == 3)
    mine = jnp.where(x == 0, 1, 0)
    base = half * 4
    odd = y % 2
    lane = lax.rem(D, 16)
    above = lax.rem(y + 1, 4) * 16 + lane
    below = lax.rem(y + 3, 4) * 16 + lane

    def copy(src, dst, send, recv, section, dp):
        return pltpu.make_async_remote_copy(
            src_ref=src, dst_ref=dst, send_sem=send, recv_sem=recv,
            device_id={"section": section, "dp": dp}, device_id_type=MESH,
        )

    local = [
        pltpu.make_async_copy(clips_ref, cl, loc.at[0]),
        pltpu.make_async_copy(ws_ref, wv.at[x, 0:SPACE], loc.at[1]),
        pltpu.make_async_copy(wt_ref, wv.at[x, SPACE : SPACE + TIME], loc.at[2]),
    ]
    for c in local:
        c.start()

    barrier = pltpu.get_barrier_semaphore()

    def hello(section, dp):
        pl.semaphore_signal(
            barrier, inc=1, device_id={"section": section, "dp": dp}, device_id_type=MESH
        )

    hello(S, sibling)
    hello(S, above)
    hello(S, below)
    hello(base + lax.rem(x + 1, 4), D)
    hello(base + lax.rem(x + 3, 4), D)

    @pl.when(z > 0)
    def _():
        hello(S, D - 2)

    @pl.when(z < 7)
    def _():
        hello(S, D + 2)

    @pl.when(S == 0)
    def _():
        hello(4, far)

    @pl.when(S == 3)
    def _():
        hello(7, far)

    inner = jnp.logical_and(z > 0, z < 7)
    crossings = jnp.where(jnp.logical_or(S == 4, S == 7), 1, 0)
    pl.semaphore_wait(barrier, 6 + jnp.where(inner, 1, 0) + crossings)

    @pl.when(jnp.logical_or(S == 4, S == 7))
    def _():
        pl.semaphore_signal(
            answer, inc=1, device_id={"section": lax.rem(S + 4, 8), "dp": far}, device_id_type=MESH
        )

    def sweep(sem, step, first, last):
        @pl.when(z != first)
        def _():
            pl.semaphore_wait(sem, 1)

        @pl.when(z != last)
        def _():
            pl.semaphore_signal(
                sem, inc=1, device_id={"section": S, "dp": D + 2 * step}, device_id_type=MESH
            )

    def meet_line():
        @pl.when(z < 4)
        def _():
            sweep(up, 1, 0, 7)
            sweep(down, -1, 7, 0)

        @pl.when(z >= 4)
        def _():
            sweep(down, -1, 7, 0)
            sweep(up, 1, 0, 7)

    for c in local:
        c.wait()

    near = jnp.where(x % 2 == 1, 0, 3)
    passed = jnp.where(x % 2 == 0, 1, 2)
    other = jnp.where(x == 0, 3, 0)
    distant = jnp.where(x == 0, 2, 1)
    middle = jnp.logical_not(end)

    def between(c):
        return jnp.logical_or(c == 1, c == 2)

    def chunk_copy(j, c, parity, core, send, recv, section, dp):
        n = 8 * parity + 4 * core + 2 * (c % 2) + c // 2
        rows = pl.ds(pl.multiple_of(n * 192, 192), 192)
        return copy(wv.at[j, rows], wv.at[j, rows], send, recv, section, dp)

    def x_chunk(j, c, target, slot):
        return chunk_copy(j, c, odd, k, wg_send.at[slot, c], wg_recv.at[j, c], base + target, D)

    def y_chunk(j, c, parity):
        dp = jnp.where(c % 2 == 1, above, below)
        return chunk_copy(j, c, parity, k, wy_send.at[j, c], wy_recv.at[j, c], S, dp)

    def core_chunk(j, c, far_rows, core):
        parity = 1 - odd if far_rows else odd
        at = 4 * far_rows + c
        return chunk_copy(j, c, parity, core, ws_send.at[j, at], ws_recv.at[j, at], S, sibling)

    def each(body):
        def step(c, carry):
            body(c)
            return carry

        lax.fori_loop(0, 4, step, 0)

    def take_x(j, c):
        x_chunk(j, c, 0, 0).wait_recv()
        y_chunk(j, c, odd).start()

        @pl.when(jnp.logical_and(j == passed, jnp.logical_not(between(c))))
        def _():
            x_chunk(j, c, near, 2).start()

        core_chunk(j, c, 0, k).start()

    def take_y(j, c):
        y_chunk(j, c, 1 - odd).wait_recv()
        core_chunk(j, c, 1, k).start()

    def pass_middle():
        @pl.when(middle)
        def _():
            for c in (1, 2):
                x_chunk(passed, c, 0, 0).wait_recv()
                x_chunk(passed, c, near, 2).start()

    @each
    def _(c):
        x_chunk(x, c, near, 0).start()

        @pl.when(jnp.logical_and(middle, between(c)))
        def _():
            x_chunk(x, c, 3 - x, 1).start()

    cot_copy = copy(
        cot_ref.at[jnp.where(x == 1, 1, 0)], ct, ct_send, ct_recv, jnp.where(x == 1, 4, 7), far
    )

    @pl.when(half == 1)
    def _():
        pass_middle()

        @pl.when(jnp.logical_not(end))
        def _():
            meet_line()
            cot_copy.start()

    def rows_of(c, h):
        return pl.ds(pl.multiple_of(h * 128 + c * HALF, HALF), HALF)

    def keep(ref, c, value):
        ref[rows_of(c, 0), :] = value[:HALF]
        ref[rows_of(c, 1), :] = value[HALF:]

    def y_copy(c):
        return copy(yout.at[c], xin.at[c], x_send.at[c], x_recv.at[c], lax.rem(S + 1, 8), D)

    cross_copy = copy(yout.at[0], bx.at[0], x_send.at[0], bx_recv, 7, far)
    hand_copy = copy(yout.at[1], ct, x_send.at[1], ct_recv, 0, D)
    relay_copy = copy(ct, bx.at[0], ct_send, bx_recv, 4, far)

    def owner_hidden(c):
        wide = wide_space(xin[c].astype(F32))
        keep(xc, c, wide)
        hidden, slope = activate(space_forward(wide, wv.at[x]))
        act[c] = slope
        wide = wide_time(hidden)
        keep(hc, c, wide)
        return wide

    def forward(first):
        def clip(c, carry):
            if first:
                xin[c] = by_height(cl[c]).astype(BF16)
            else:
                y_copy(c).wait_recv()
            wide = owner_hidden(c)
            out = xin[c].astype(F32) + nn(wide, wv[x, SPACE : SPACE + TIME, :])
            yout[c] = out.astype(BF16)
            if first:
                y_copy(c).start()
            else:
                @pl.when(x < 3)
                def _():
                    y_copy(c).start()

                @pl.when(jnp.logical_and(x == 3, c == 0))
                def _():
                    pl.semaphore_wait(answer, 1)
                    cross_copy.start()

                @pl.when(jnp.logical_and(x == 3, c == 1))
                def _():
                    hand_copy.start()

            return carry

        lax.fori_loop(0, 2, clip, 0)

    @pl.when(S == 0)
    def _():
        forward(True)

    @pl.when(jnp.logical_or(S == 0, S == 3))
    def _():
        meet_line()

    @pl.when(end)
    def _():
        @each
        def _(c):
            take_x(passed, c)
            take_x(other, c)

    @pl.when(S == 0)
    def _():
        hand_copy.wait_recv()
        pl.semaphore_wait(answer, 1)
        relay_copy.start()

    @pl.when(jnp.logical_and(half == 0, x > 0))
    def _():
        forward(False)
        pass_middle()

        @pl.when(x < 3)
        def _():
            meet_line()

    def x_copy(j):
        return copy(bx.at[j], xin.at[mine], bx_send.at[j], x_recv.at[mine], base + j, D)

    def g_copy(j):
        return copy(bg.at[j + 1], gin.at[mine], go_send.at[j], gin_recv.at[mine], base + j, D)

    back_copy = copy(bg.at[0], bg.at[4], bg_send, bg_recv, lax.rem(S + 4, 8), far)

    @pl.when(end)
    def _():
        @each
        def _(c):
            take_x(distant, c)
            take_y(passed, c)
            take_y(other, c)
        @each
        def _(c):
            take_y(distant, c)
        @each
        def _(c):
            for j in (passed, other, distant):
                core_chunk(j, c, 0, 1 - k).wait_recv()
                core_chunk(j, c, 1, 1 - k).wait_recv()

        @pl.when(half == 0)
        def _():
            bx[0] = by_height(cl[mine]).astype(BF16)

        @pl.when(half == 1)
        def _():
            cross_copy.wait_recv()

        def layer(j, carry):
            @pl.when(half == 1)
            def _():
                @pl.when(j == x)
                def _():
                    xin[mine] = bx[j]

                @pl.when(j != x)
                def _():
                    x_copy(j).start()

            v = bx[j].astype(F32)
            hidden, slope = activate(space_forward(wide_space(v), wv.at[j]))
            bact[j] = slope

            @pl.when(j < 3)
            def _():
                out = v + nn(wide_time(hidden), wv[j, SPACE : SPACE + TIME, :])
                bx[j + 1] = out.astype(BF16)

            return carry

        lax.fori_loop(0, 4, layer, 0)

        @pl.when(half == 0)
        def _():
            def turn(n, carry):
                rows = pl.ds(pl.multiple_of((n % 12) * C, C), C)
                turned[n // 12, rows] = wv[n // 12, rows].T
                return carry

            lax.fori_loop(12, 48, turn, 0)
            back_copy.wait_recv()

        @pl.when(half == 1)
        def _():
            cot_copy.wait_recv()
            bg[4] = by_height(ct[...]).astype(BF16)

        def layers_back(w, g_hidden, g_space):
            def layer_back(i, carry):
                j = 3 - i

                @pl.when(j == x)
                def _():
                    gin[mine] = bg[j + 1]

                @pl.when(j != x)
                def _():
                    g_copy(j).start()

                @pl.when(j + half > 0)
                def _():
                    g = bg[j + 1].astype(F32)
                    g_pre = (g_hidden(g, w.at[j]) * bact[j]).astype(BF16).astype(F32)
                    bg[j] = (g + g_space(g_pre, w.at[j])).astype(BF16)

                return carry

            lax.fori_loop(0, 4, layer_back, 0)

        @pl.when(half == 0)
        def _():
            layers_back(turned, g_hidden_turned, space_backward_turned)

        @pl.when(half == 1)
        def _():
            layers_back(wv, g_hidden_of, space_backward)

        @pl.when(half == 1)
        def _():
            back_copy.start()
            meet_line()

    @pl.when(half == 1)
    def _():
        def clip(c, carry):
            @pl.when(jnp.logical_not(jnp.logical_and(end, c == mine)))
            def _():
                y_copy(c).wait_recv()

            owner_hidden(c)
            return carry

        lax.fori_loop(0, 2, clip, 0)

    def clip_back(i, carry):
        c = jnp.where(i == 0, mine, 1 - mine)

        @pl.when(jnp.logical_not(jnp.logical_and(end, c == mine)))
        def _():
            copy(gin.at[c], gin.at[c], go_send.at[0], gin_recv.at[c], S, D).wait_recv()

        keep(gb, c, gin[c])
        g = gin[c].astype(F32)
        keep(gp, c, (g_hidden_of(g, wv.at[x]) * act[c]).astype(BF16))
        return carry

    lax.fori_loop(0, 2, clip_back, 0)

    for q in range(3):
        lanes = slice(256 * q, 256 * q + 256)
        dw[SPACE + 256 * q : SPACE + 256 * q + 256, :] = tn(hc[:, lanes], gb[...])
        dw[256 * q : 256 * q + 256, :] = tn(xc[0:128, lanes], gp[128:256, :])
        dw[768 + 256 * q : 1024 + 256 * q, :] = tn(xc[:, lanes], gp[...])
        dw[1536 + 256 * q : 1792 + 256 * q, :] = tn(xc[128:256, lanes], gp[0:128, :])

    blocks = [lax.rem(y + i, 4) for i in (2, 1, 3, 0)]
    sides = (lax.rem(y + 1, 4), lax.rem(y + 3, 4))

    def core_step(i, column):
        yb = blocks[i]
        return copy(part.at[column, yb], r1.at[yb], r1_send.at[i], r1_recv.at[i], S, sibling)

    for i in range(4):
        def pack(b, carry):
            n = blocks[i] * 8 + b
            top = dw[pl.ds(pl.multiple_of(n * 72, 8), 72), :]
            low = dw[pl.ds(pl.multiple_of(SPACE + n * 24, 8), 24), :]
            block = jnp.concatenate([top, low], axis=0).astype(BF16)
            part[0, blocks[i], b] = block[:, 0:128]
            part[1, blocks[i], b] = block[:, 128:256]
            return carry

        lax.fori_loop(0, 8, pack, 0)
        core_step(i, 1 - k).start()

    def add_cores(yb, start, stop):
        def one(b, carry):
            s1[yb, b] = (part[k, yb, b].astype(F32) + r1[yb, b].astype(F32)).astype(BF16)
            return carry

        lax.fori_loop(start, stop, one, 0)

    def y_step(i, side):
        forth, back = sides[side], sides[1 - side]
        to = (forth, back, forth)[i]
        some = pl.ds(4 * side, 4)
        return copy(
            s1.at[blocks[0] if i == 0 else to, some], r2.at[i, some],
            r2_send.at[i, side], r2_recv.at[i, side], S, to * 16 + lane,
        )

    core_step(0, k).wait_recv()
    add_cores(blocks[0], 0, 8)
    y_step(0, 0).start()
    y_step(0, 1).start()
    for side in (1, 0):
        core_step(2 - side, k).wait_recv()
        add_cores(sides[1 - side], 4 * side, 4 * side + 4)
        y_step(1, side).start()
    for side in range(2):
        forth = sides[side]
        y_step(0, side).wait_recv()

        def add_relayed(b, carry):
            total = part[k, forth, b].astype(F32) + r1[forth, b].astype(F32) + r2[0, b].astype(F32)
            s1[forth, b] = total.astype(BF16)
            return carry

        lax.fori_loop(4 * side, 4 * side + 4, add_relayed, 0)
        y_step(2, side).start()
    core_step(3, k).wait_recv()
    for i in (1, 2):
        for side in range(2):
            y_step(i, side).wait_recv()
    def add_y(b, carry):
        total = part[k, y, b].astype(F32) + r1[y, b].astype(F32) + r2[1, b].astype(F32) + r2[2, b].astype(F32)
        s2[b] = total.astype(BF16)
        return carry

    lax.fori_loop(0, 8, add_y, 0)

    def z_step(i):
        to = lax.rem(z + i, 8)
        return copy(s2.at[to], r3.at[i - 1], r3_send.at[i - 1], r3_recv.at[i - 1], S, y * 16 + to * 2 + k)

    for i in range(1, 8):
        z_step(i).start()
    for i in range(1, 8):
        z_step(i).wait_recv()

    total = s2[z].astype(F32)
    for i in range(7):
        total = total + r3[i].astype(F32)
    fin[k] = total * scale

    final = copy(fin.at[k], fin.at[k], r4_sem.at[0], r4_sem.at[1], S, sibling)
    final.start()
    final.wait_send()
    copy(fin.at[1 - k], fin.at[1 - k], r4_sem.at[0], r4_sem.at[1], S, sibling).wait_recv()

    for core in range(2):
        @pl.when(k == core)
        def _():
            for side in range(2):
                lanes = slice(128 * side, 128 * side + 128)
                out_s[:, lanes] = fin[side, 36 * core : 36 * core + 36, :]
                out_t[:, lanes] = fin[side, 72 + 12 * core : 84 + 12 * core, :]

    for i in range(4):
        core_step(i, 1 - k).wait_send()
    for i in range(3):
        for side in range(2):
            y_step(i, side).wait_send()
    for i in range(1, 8):
        z_step(i).wait_send()
    @each
    def _(c):
        x_chunk(x, c, near, 0).wait_send()

        @pl.when(jnp.logical_and(middle, between(c)))
        def _():
            x_chunk(x, c, 3 - x, 1).wait_send()

        @pl.when(middle == between(c))
        def _():
            x_chunk(passed, c, near, 2).wait_send()

        @pl.when(end)
        def _():
            for j in (passed, other, distant):
                y_chunk(j, c, odd).wait_send()
                core_chunk(j, c, 0, k).wait_send()
                core_chunk(j, c, 1, k).wait_send()

    @pl.when(jnp.logical_or(S == 5, S == 6))
    def _():
        cot_copy.wait_send()

    @pl.when(S == 0)
    def _():
        relay_copy.wait_send()

    @pl.when(half == 0)
    def _():
        for c in range(2):
            y_copy(c).wait_send()

    @pl.when(end)
    def _():
        for i in range(1, 4):
            j = lax.rem(x + i, 4)
            g_copy(j).wait_send()

            @pl.when(half == 1)
            def _():
                x_copy(j).wait_send()

        @pl.when(half == 1)
        def _():
            back_copy.wait_send()


def body(clips, cotangent, spatial_kernel, temporal_kernel):
    micro = clips.shape[0]
    tile = clips.shape[1:]
    cells = tile[0] * tile[1] * tile[2]
    scale = 1.0 / math.sqrt(micro * lax.axis_size("dp") * cells)
    sem = pltpu.SemaphoreType.DMA
    vmem = pltpu.VMEM
    out_s, out_t = pl.pallas_call(
        functools.partial(kernel, scale),
        out_shape=(jax.ShapeDtypeStruct((36, C), F32), jax.ShapeDtypeStruct((12, C), F32)),
        in_specs=[pl.BlockSpec(memory_space=pltpu.HBM)] * 4,
        out_specs=(pl.BlockSpec(memory_space=pltpu.VMEM),) * 2,
        scratch_shapes=[
            vmem((4, SPACE + TIME, C), BF16),
            vmem((4, SPACE + TIME, C), BF16),
            vmem((2, ROWS, C), BF16),
            vmem((ROWS, C), BF16),
            vmem((2, ROWS, C), BF16),
            vmem((2, ROWS, C), BF16),
            vmem((4, ROWS, C), BF16),
            vmem((5, ROWS, C), BF16),
            vmem((2, ROWS, C), BF16),
            vmem((2, ROWS, C), F32),
            vmem((4, ROWS, C), F32),
            vmem((2 * ROWS, 3 * C), BF16),
            vmem((2 * ROWS, 3 * C), BF16),
            vmem((2 * ROWS, C), BF16),
            vmem((2 * ROWS, C), BF16),
            vmem((SPACE + TIME, C), F32),
            vmem((2, 4, 8, 96, 128), BF16),
            vmem((4, 8, 96, 128), BF16),
            vmem((4, 8, 96, 128), BF16),
            vmem((3, 8, 96, 128), BF16),
            vmem((8, 96, 128), BF16),
            vmem((7, 96, 128), BF16),
            vmem((2, 96, 128), F32),
            sem((3,)),
            sem((3, 4)),
            sem((4, 4)),
            sem((4, 8)),
            sem((4, 8)),
            sem((4, 4)),
            sem((4, 4)),
            sem((2,)),
            sem((2,)),
            sem((4,)),
            sem,
            sem,
            sem,
            sem((4,)),
            sem((2,)),
            sem,
            sem,
            sem((4,)),
            sem((4,)),
            sem((3, 2)),
            sem((3, 2)),
            sem((7,)),
            sem((7,)),
            sem((2,)),
            pltpu.SemaphoreType.REGULAR,
            pltpu.SemaphoreType.REGULAR,
            pltpu.SemaphoreType.REGULAR,
        ],
        compiler_params=pltpu.CompilerParams(
            collective_id=0, has_side_effects=True, vmem_limit_bytes=66_900_000
        ),
        name="window",
    )(
        clips.reshape(micro, cells, tile[3]),
        cotangent.reshape(micro, cells, tile[3]),
        spatial_kernel[0],
        temporal_kernel[0],
    )
    return (out_s[None], out_t[None])


def solution(mesh):
    return jax.shard_map(
        body,
        mesh=mesh,
        in_specs=(
            P("dp", None, None, None, None),
            P("dp", None, None, None, None),
            P("section", None, None),
            P("section", None, None),
        ),
        out_specs=(P("section", "dp", None), P("section", "dp", None)),
        check_vma=False,
    )
```

```python
import functools
import math

import jax
import jax.numpy as jnp
from jax import lax
from jax.experimental import pallas as pl
from jax.experimental.pallas import tpu as pltpu
from jax.sharding import PartitionSpec as P

MESH = pl.DeviceIdType.MESH
F32 = jnp.float32
BF16 = jnp.bfloat16
C = 256
ROWS = 128
HALF = 64
SPACE = 9 * C
TIME = 3 * C


def by_height(v):
    v = v.astype(F32).reshape(8, 2, 8, C)
    return jnp.concatenate([v[:, 0].reshape(HALF, C), v[:, 1].reshape(HALF, C)], axis=0)


def columns(v):
    w = lax.broadcasted_iota(jnp.int32, v.shape, 0) & 7
    before = jnp.where(w == 0, 0.0, pltpu.roll(v, 1, 0))
    after = jnp.where(w == 7, 0.0, pltpu.roll(v, ROWS - 1, 0))
    return before, after


def frames(v):
    zero = jnp.zeros((8, C), F32)
    before = jnp.concatenate([zero, v[0:56], zero, v[64:120]], axis=0)
    after = jnp.concatenate([v[8:64], zero, v[72:128], zero], axis=0)
    return before, after


def nn(a, b):
    return jnp.dot(a, b, preferred_element_type=F32)


def nt(a, b):
    return lax.dot_general(a, b, (((1,), (1,)), ((), ())), preferred_element_type=F32)


def tn(a, b):
    return lax.dot_general(a, b, (((0,), (0,)), ((), ())), preferred_element_type=F32)


def wide_space(v):
    before, after = columns(v)
    return jnp.concatenate([before, v, after], axis=1).astype(BF16)


def wide_time(v):
    before, after = frames(v)
    return jnp.concatenate([before, v, after], axis=1).astype(BF16)


def space_forward(wide, w):
    same = nn(wide, w[768:1536, :])
    top = nn(wide[HALF:], w[1536:2304, :])
    bottom = nn(wide[:HALF], w[0:768, :])
    return same + jnp.concatenate([top, bottom], axis=0)


def activate(pre):
    sigma = jax.nn.sigmoid(pre)
    hidden = (pre * sigma).astype(BF16).astype(F32)
    return hidden, sigma * (1.0 + pre * (1.0 - sigma))


def g_hidden_of(g, w):
    before, after = frames(g)
    out = nt(after.astype(BF16), w[SPACE : SPACE + 256, :])
    out = out + nt(g.astype(BF16), w[SPACE + 256 : SPACE + 512, :])
    return out + nt(before.astype(BF16), w[SPACE + 512 : SPACE + 768, :])


def space_backward(g_pre, w):
    before, after = columns(g_pre)
    same = top = bottom = None
    for q, v in enumerate((after, g_pre, before)):
        v = v.astype(BF16)
        a = nt(v, w[768 + 256 * q : 1024 + 256 * q, :])
        t = nt(v[HALF:], w[256 * q : 256 * q + 256, :])
        b = nt(v[:HALF], w[1536 + 256 * q : 1792 + 256 * q, :])
        same, top, bottom = (a, t, b) if same is None else (same + a, top + t, bottom + b)
    return same + jnp.concatenate([top, bottom], axis=0)


def g_hidden_turned(g, w):
    before, after = frames(g)
    wide = jnp.concatenate([after, g, before], axis=1).astype(BF16)
    return nn(wide, w[SPACE : SPACE + TIME, :])


def space_backward_turned(g_pre, w):
    before, after = columns(g_pre)
    wide = jnp.concatenate([after, g_pre, before], axis=1).astype(BF16)
    same = nn(wide, w[768:1536, :])
    top = nn(wide[HALF:], w[0:768, :])
    bottom = nn(wide[:HALF], w[1536:2304, :])
    return same + jnp.concatenate([top, bottom], axis=0)


def kernel(
    scale,
    clips_ref, cot_ref, ws_ref, wt_ref,
    out_s, out_t,
    wv, turned, cl, ct, xin, yout, bx, bg, gin,
    act, bact, xc, hc, gp, gb, dw, part, r1, s1, r2, s2, r3, fin,
    loc, wg_send, wg_recv, ws_send, ws_recv, wy_send, wy_recv,
    x_send, x_recv, bx_send, bx_recv, ct_send, ct_recv,
    go_send, gin_recv, bg_send, bg_recv,
    r1_send, r1_recv, r2_send, r2_recv, r3_send, r3_recv, r4_sem, up, down, answer,
):
    S = lax.axis_index("section")
    D = lax.axis_index("dp")
    half = S // 4
    x = S % 4
    y = D // 16
    z = (D // 2) % 8
    k = D % 2
    far = D + 14 - 4 * z
    sibling = D + 1 - 2 * k
    end = jnp.logical_or(x == 0, x == 3)
    mine = jnp.where(x == 0, 1, 0)
    base = half * 4
    odd = y % 2
    lane = lax.rem(D, 16)
    above = lax.rem(y + 1, 4) * 16 + lane
    below = lax.rem(y + 3, 4) * 16 + lane

    def copy(src, dst, send, recv, section, dp):
        return pltpu.make_async_remote_copy(
            src_ref=src, dst_ref=dst, send_sem=send, recv_sem=recv,
            device_id={"section": section, "dp": dp}, device_id_type=MESH,
        )

    local = [
        pltpu.make_async_copy(clips_ref, cl, loc.at[0]),
        pltpu.make_async_copy(ws_ref, wv.at[x, 0:SPACE], loc.at[1]),
        pltpu.make_async_copy(wt_ref, wv.at[x, SPACE : SPACE + TIME], loc.at[2]),
    ]
    for c in local:
        c.start()

    barrier = pltpu.get_barrier_semaphore()

    def hello(section, dp):
        pl.semaphore_signal(
            barrier, inc=1, device_id={"section": section, "dp": dp}, device_id_type=MESH
        )

    hello(S, sibling)
    hello(S, above)
    hello(S, below)
    hello(base + lax.rem(x + 1, 4), D)
    hello(base + lax.rem(x + 3, 4), D)

    @pl.when(z > 0)
    def _():
        hello(S, D - 2)

    @pl.when(z < 7)
    def _():
        hello(S, D + 2)

    @pl.when(S == 0)
    def _():
        hello(4, far)

    @pl.when(S == 3)
    def _():
        hello(7, far)

    inner = jnp.logical_and(z > 0, z < 7)
    crossings = jnp.where(jnp.logical_or(S == 4, S == 7), 1, 0)
    pl.semaphore_wait(barrier, 6 + jnp.where(inner, 1, 0) + crossings)

    @pl.when(jnp.logical_or(S == 4, S == 7))
    def _():
        pl.semaphore_signal(
            answer, inc=1, device_id={"section": lax.rem(S + 4, 8), "dp": far}, device_id_type=MESH
        )

    def sweep(sem, step, first, last):
        @pl.when(z != first)
        def _():
            pl.semaphore_wait(sem, 1)

        @pl.when(z != last)
        def _():
            pl.semaphore_signal(
                sem, inc=1, device_id={"section": S, "dp": D + 2 * step}, device_id_type=MESH
            )

    def meet_line():
        @pl.when(z < 4)
        def _():
            sweep(up, 1, 0, 7)
            sweep(down, -1, 7, 0)

        @pl.when(z >= 4)
        def _():
            sweep(down, -1, 7, 0)
            sweep(up, 1, 0, 7)

    for c in local:
        c.wait()

    near = jnp.where(x % 2 == 1, 0, 3)
    passed = jnp.where(x % 2 == 0, 1, 2)
    other = jnp.where(x == 0, 3, 0)
    distant = jnp.where(x == 0, 2, 1)
    middle = jnp.logical_not(end)

    def between(c):
        return jnp.logical_or(c == 1, c == 2)

    def chunk_copy(j, c, parity, core, send, recv, section, dp):
        n = 8 * parity + 4 * core + 2 * (c % 2) + c // 2
        rows = pl.ds(pl.multiple_of(n * 192, 192), 192)
        return copy(wv.at[j, rows], wv.at[j, rows], send, recv, section, dp)

    def x_chunk(j, c, target, slot):
        return chunk_copy(j, c, odd, k, wg_send.at[slot, c], wg_recv.at[j, c], base + target, D)

    def y_chunk(j, c, parity):
        dp = jnp.where(c % 2 == 1, above, below)
        return chunk_copy(j, c, parity, k, wy_send.at[j, c], wy_recv.at[j, c], S, dp)

    def core_chunk(j, c, far_rows, core):
        parity = 1 - odd if far_rows else odd
        at = 4 * far_rows + c
        return chunk_copy(j, c, parity, core, ws_send.at[j, at], ws_recv.at[j, at], S, sibling)

    def each(body):
        def step(c, carry):
            body(c)
            return carry

        lax.fori_loop(0, 4, step, 0)

    def take_x(j, c):
        x_chunk(j, c, 0, 0).wait_recv()
        y_chunk(j, c, odd).start()

        @pl.when(jnp.logical_and(j == passed, jnp.logical_not(between(c))))
        def _():
            x_chunk(j, c, near, 2).start()

        core_chunk(j, c, 0, k).start()

    def take_y(j, c):
        y_chunk(j, c, 1 - odd).wait_recv()
        core_chunk(j, c, 1, k).start()

    def pass_middle():
        @pl.when(middle)
        def _():
            for c in (1, 2):
                x_chunk(passed, c, 0, 0).wait_recv()
                x_chunk(passed, c, near, 2).start()

    @each
    def _(c):
        x_chunk(x, c, near, 0).start()

        @pl.when(jnp.logical_and(middle, between(c)))
        def _():
            x_chunk(x, c, 3 - x, 1).start()

    cot_copy = copy(
        cot_ref.at[jnp.where(x == 1, 1, 0)], ct, ct_send, ct_recv, jnp.where(x == 1, 4, 7), far
    )

    def turn(j, n):
        rows = pl.ds(pl.multiple_of(n * C, C), C)
        turned[j, rows] = wv[j, rows].T
        return 0

    @pl.when(half == 1)
    def _():
        pass_middle()

        @pl.when(end)
        def _():
            lax.fori_loop(0, 12, lambda n, carry: turn(x, n), 0)

        @pl.when(jnp.logical_not(end))
        def _():
            meet_line()
            cot_copy.start()

    def rows_of(c, h):
        return pl.ds(pl.multiple_of(h * 128 + c * HALF, HALF), HALF)

    def keep(ref, c, value):
        ref[rows_of(c, 0), :] = value[:HALF]
        ref[rows_of(c, 1), :] = value[HALF:]

    def y_copy(c):
        return copy(yout.at[c], xin.at[c], x_send.at[c], x_recv.at[c], lax.rem(S + 1, 8), D)

    cross_copy = copy(yout.at[0], bx.at[0], x_send.at[0], bx_recv, 7, far)
    hand_copy = copy(yout.at[1], ct, x_send.at[1], ct_recv, 0, D)
    relay_copy = copy(ct, bx.at[0], ct_send, bx_recv, 4, far)

    def owner_hidden(c):
        wide = wide_space(xin[c].astype(F32))
        keep(xc, c, wide)
        hidden, slope = activate(space_forward(wide, wv.at[x]))
        act[c] = slope
        wide = wide_time(hidden)
        keep(hc, c, wide)
        return wide

    def forward(first):
        def clip(c, carry):
            if first:
                xin[c] = by_height(cl[c]).astype(BF16)
            else:
                y_copy(c).wait_recv()
            wide = owner_hidden(c)
            out = xin[c].astype(F32) + nn(wide, wv[x, SPACE : SPACE + TIME, :])
            yout[c] = out.astype(BF16)
            if first:
                y_copy(c).start()
            else:
                @pl.when(x < 3)
                def _():
                    y_copy(c).start()

                @pl.when(jnp.logical_and(x == 3, c == 0))
                def _():
                    pl.semaphore_wait(answer, 1)
                    cross_copy.start()

                @pl.when(jnp.logical_and(x == 3, c == 1))
                def _():
                    hand_copy.start()

            return carry

        lax.fori_loop(0, 2, clip, 0)

    @pl.when(S == 0)
    def _():
        forward(True)

    @pl.when(jnp.logical_or(S == 0, S == 3))
    def _():
        meet_line()

    @pl.when(end)
    def _():
        @each
        def _(c):
            take_x(passed, c)
            take_x(other, c)

    @pl.when(S == 0)
    def _():
        hand_copy.wait_recv()
        pl.semaphore_wait(answer, 1)
        relay_copy.start()

    @pl.when(jnp.logical_and(half == 0, x > 0))
    def _():
        forward(False)
        pass_middle()

        @pl.when(x < 3)
        def _():
            meet_line()

    def x_copy(j):
        return copy(bx.at[j], xin.at[mine], bx_send.at[j], x_recv.at[mine], base + j, D)

    def g_copy(j):
        return copy(bg.at[j + 1], gin.at[mine], go_send.at[j], gin_recv.at[mine], base + j, D)

    back_copy = copy(bg.at[0], bg.at[4], bg_send, bg_recv, lax.rem(S + 4, 8), far)

    @pl.when(end)
    def _():
        @each
        def _(c):
            take_x(distant, c)
            take_y(passed, c)
            take_y(other, c)
        @each
        def _(c):
            take_y(distant, c)
        @each
        def _(c):
            for j in (passed, other, distant):
                core_chunk(j, c, 0, 1 - k).wait_recv()
                core_chunk(j, c, 1, 1 - k).wait_recv()

        @pl.when(half == 0)
        def _():
            bx[0] = by_height(cl[mine]).astype(BF16)

        @pl.when(half == 1)
        def _():
            cross_copy.wait_recv()

        def layer(j, carry):
            @pl.when(half == 1)
            def _():
                @pl.when(j == x)
                def _():
                    xin[mine] = bx[j]

                @pl.when(j != x)
                def _():
                    x_copy(j).start()

            v = bx[j].astype(F32)
            hidden, slope = activate(space_forward(wide_space(v), wv.at[j]))
            bact[j] = slope

            @pl.when(j < 3)
            def _():
                out = v + nn(wide_time(hidden), wv[j, SPACE : SPACE + TIME, :])
                bx[j + 1] = out.astype(BF16)

            return carry

        lax.fori_loop(0, 4, layer, 0)

        @pl.when(half == 0)
        def _():
            lax.fori_loop(12, 48, lambda n, carry: turn(n // 12, n % 12), 0)
            back_copy.wait_recv()

        @pl.when(half == 1)
        def _():
            cot_copy.wait_recv()
            bg[4] = by_height(ct[...]).astype(BF16)

        def hand_out(j):
            @pl.when(j == x)
            def _():
                gin[mine] = bg[j + 1]

            @pl.when(j != x)
            def _():
                g_copy(j).start()

        def layer_back(j, w, g_hidden, g_space):
            g = bg[j + 1].astype(F32)
            g_pre = (g_hidden(g, w.at[j]) * bact[j]).astype(BF16).astype(F32)
            bg[j] = (g + g_space(g_pre, w.at[j])).astype(BF16)

        def layers_back(is_turned, lowest):
            def step(i, carry):
                j = 3 - i
                hand_out(j)

                @pl.when(jnp.logical_and(j >= lowest, is_turned(j)))
                def _():
                    layer_back(j, turned, g_hidden_turned, space_backward_turned)

                @pl.when(jnp.logical_and(j >= lowest, jnp.logical_not(is_turned(j))))
                def _():
                    layer_back(j, wv, g_hidden_of, space_backward)

                return carry

            lax.fori_loop(0, 4, step, 0)

        layers_back(lambda j: jnp.logical_or(half == 0, j == x), 1 - half)

        @pl.when(half == 1)
        def _():
            back_copy.start()
            meet_line()

    @pl.when(half == 1)
    def _():
        def clip(c, carry):
            @pl.when(jnp.logical_not(jnp.logical_and(end, c == mine)))
            def _():
                y_copy(c).wait_recv()

            owner_hidden(c)
            return carry

        lax.fori_loop(0, 2, clip, 0)

    def clip_back(i, carry):
        c = jnp.where(i == 0, mine, 1 - mine)

        @pl.when(jnp.logical_not(jnp.logical_and(end, c == mine)))
        def _():
            copy(gin.at[c], gin.at[c], go_send.at[0], gin_recv.at[c], S, D).wait_recv()

        keep(gb, c, gin[c])
        g = gin[c].astype(F32)
        keep(gp, c, (g_hidden_of(g, wv.at[x]) * act[c]).astype(BF16))
        return carry

    lax.fori_loop(0, 2, clip_back, 0)

    for q in range(3):
        lanes = slice(256 * q, 256 * q + 256)
        dw[SPACE + 256 * q : SPACE + 256 * q + 256, :] = tn(hc[:, lanes], gb[...])
        dw[256 * q : 256 * q + 256, :] = tn(xc[0:128, lanes], gp[128:256, :])
        dw[768 + 256 * q : 1024 + 256 * q, :] = tn(xc[:, lanes], gp[...])
        dw[1536 + 256 * q : 1792 + 256 * q, :] = tn(xc[128:256, lanes], gp[0:128, :])

    blocks = [lax.rem(y + i, 4) for i in (2, 1, 3, 0)]
    sides = (lax.rem(y + 1, 4), lax.rem(y + 3, 4))

    def core_step(i, column):
        yb = blocks[i]
        return copy(part.at[column, yb], r1.at[yb], r1_send.at[i], r1_recv.at[i], S, sibling)

    for i in range(4):
        def pack(b, carry):
            n = blocks[i] * 8 + b
            top = dw[pl.ds(pl.multiple_of(n * 72, 8), 72), :]
            low = dw[pl.ds(pl.multiple_of(SPACE + n * 24, 8), 24), :]
            block = jnp.concatenate([top, low], axis=0).astype(BF16)
            part[0, blocks[i], b] = block[:, 0:128]
            part[1, blocks[i], b] = block[:, 128:256]
            return carry

        lax.fori_loop(0, 8, pack, 0)
        core_step(i, 1 - k).start()

    def part_rows(r):
        return slice(48 * r, 48 * r + 48)

    def add_cores(yb, start, stop, rows):
        def one(b, carry):
            s1[yb, b, rows] = (part[k, yb, b, rows].astype(F32) + r1[yb, b, rows].astype(F32)).astype(BF16)
            return carry

        lax.fori_loop(start, stop, one, 0)

    def y_step(i, side, r):
        forth, back = sides[side], sides[1 - side]
        to = (forth, back, forth)[i]
        some, rows = pl.ds(4 * side, 4), pl.ds(48 * r, 48)
        return copy(
            s1.at[blocks[0] if i == 0 else to, some, rows], r2.at[i, some, rows],
            r2_send.at[i, side, r], r2_recv.at[i, side, r], S, to * 16 + lane,
        )

    def z_step(i, r):
        to = lax.rem(z + i, 8)
        rows = pl.ds(48 * r, 48)
        return copy(
            s2.at[to, rows], r3.at[i - 1, rows], r3_send.at[i - 1, r], r3_recv.at[i - 1, r],
            S, y * 16 + to * 2 + k,
        )

    core_step(0, k).wait_recv()
    for r in range(2):
        add_cores(blocks[0], 0, 8, part_rows(r))
        for side in range(2):
            y_step(0, side, r).start()
    for side in (1, 0):
        core_step(2 - side, k).wait_recv()
        add_cores(sides[1 - side], 4 * side, 4 * side + 4, slice(0, 96))
        y_step(1, side, 0).start()
    for r in range(2):
        for side in range(2):
            forth, rows = sides[side], part_rows(r)
            y_step(0, side, r).wait_recv()

            def add_relayed(b, carry):
                total = part[k, forth, b, rows].astype(F32) + r1[forth, b, rows].astype(F32)
                s1[forth, b, rows] = (total + r2[0, b, rows].astype(F32)).astype(BF16)
                return carry

            lax.fori_loop(4 * side, 4 * side + 4, add_relayed, 0)
            y_step(2, side, r).start()
    for side in range(2):
        y_step(1, side, 1).start()
    core_step(3, k).wait_recv()
    for r in range(2):
        rows = part_rows(r)
        for i in (1, 2):
            for side in range(2):
                y_step(i, side, r).wait_recv()

        def add_y(b, carry):
            total = part[k, y, b, rows].astype(F32) + r1[y, b, rows].astype(F32)
            total = total + r2[1, b, rows].astype(F32) + r2[2, b, rows].astype(F32)
            s2[b, rows] = total.astype(BF16)
            return carry

        lax.fori_loop(0, 8, add_y, 0)
        for d in range(7, 0, -1):
            @pl.when(z + d < 8)
            def _():
                z_step(d, r).start()

            @pl.when(z >= d)
            def _():
                z_step(8 - d, r).start()

    for r in range(2):
        for i in range(1, 8):
            z_step(i, r).wait_recv()

    total = s2[z].astype(F32)
    for i in range(7):
        total = total + r3[i].astype(F32)
    fin[k] = total * scale

    final = copy(fin.at[k], fin.at[k], r4_sem.at[0], r4_sem.at[1], S, sibling)
    final.start()
    final.wait_send()
    copy(fin.at[1 - k], fin.at[1 - k], r4_sem.at[0], r4_sem.at[1], S, sibling).wait_recv()

    for core in range(2):
        @pl.when(k == core)
        def _():
            for side in range(2):
                lanes = slice(128 * side, 128 * side + 128)
                out_s[:, lanes] = fin[side, 36 * core : 36 * core + 36, :]
                out_t[:, lanes] = fin[side, 72 + 12 * core : 84 + 12 * core, :]

    for i in range(4):
        core_step(i, 1 - k).wait_send()
    for i in range(3):
        for side in range(2):
            for r in range(2):
                y_step(i, side, r).wait_send()
    for i in range(1, 8):
        for r in range(2):
            z_step(i, r).wait_send()
    @each
    def _(c):
        x_chunk(x, c, near, 0).wait_send()

        @pl.when(jnp.logical_and(middle, between(c)))
        def _():
            x_chunk(x, c, 3 - x, 1).wait_send()

        @pl.when(middle == between(c))
        def _():
            x_chunk(passed, c, near, 2).wait_send()

        @pl.when(end)
        def _():
            for j in (passed, other, distant):
                y_chunk(j, c, odd).wait_send()
                core_chunk(j, c, 0, k).wait_send()
                core_chunk(j, c, 1, k).wait_send()

    @pl.when(jnp.logical_or(S == 5, S == 6))
    def _():
        cot_copy.wait_send()

    @pl.when(S == 0)
    def _():
        relay_copy.wait_send()

    @pl.when(half == 0)
    def _():
        for c in range(2):
            y_copy(c).wait_send()

    @pl.when(end)
    def _():
        for i in range(1, 4):
            j = lax.rem(x + i, 4)
            g_copy(j).wait_send()

            @pl.when(half == 1)
            def _():
                x_copy(j).wait_send()

        @pl.when(half == 1)
        def _():
            back_copy.wait_send()


def body(clips, cotangent, spatial_kernel, temporal_kernel):
    micro = clips.shape[0]
    tile = clips.shape[1:]
    cells = tile[0] * tile[1] * tile[2]
    scale = 1.0 / math.sqrt(micro * lax.axis_size("dp") * cells)
    sem = pltpu.SemaphoreType.DMA
    vmem = pltpu.VMEM
    out_s, out_t = pl.pallas_call(
        functools.partial(kernel, scale),
        out_shape=(jax.ShapeDtypeStruct((36, C), F32), jax.ShapeDtypeStruct((12, C), F32)),
        in_specs=[pl.BlockSpec(memory_space=pltpu.HBM)] * 4,
        out_specs=(pl.BlockSpec(memory_space=pltpu.VMEM),) * 2,
        scratch_shapes=[
            vmem((4, SPACE + TIME, C), BF16),
            vmem((4, SPACE + TIME, C), BF16),
            vmem((2, ROWS, C), BF16),
            vmem((ROWS, C), BF16),
            vmem((2, ROWS, C), BF16),
            vmem((2, ROWS, C), BF16),
            vmem((4, ROWS, C), BF16),
            vmem((5, ROWS, C), BF16),
            vmem((2, ROWS, C), BF16),
            vmem((2, ROWS, C), F32),
            vmem((4, ROWS, C), F32),
            vmem((2 * ROWS, 3 * C), BF16),
            vmem((2 * ROWS, 3 * C), BF16),
            vmem((2 * ROWS, C), BF16),
            vmem((2 * ROWS, C), BF16),
            vmem((SPACE + TIME, C), F32),
            vmem((2, 4, 8, 96, 128), BF16),
            vmem((4, 8, 96, 128), BF16),
            vmem((4, 8, 96, 128), BF16),
            vmem((3, 8, 96, 128), BF16),
            vmem((8, 96, 128), BF16),
            vmem((7, 96, 128), BF16),
            vmem((2, 96, 128), F32),
            sem((3,)),
            sem((3, 4)),
            sem((4, 4)),
            sem((4, 8)),
            sem((4, 8)),
            sem((4, 4)),
            sem((4, 4)),
            sem((2,)),
            sem((2,)),
            sem((4,)),
            sem,
            sem,
            sem,
            sem((4,)),
            sem((2,)),
            sem,
            sem,
            sem((4,)),
            sem((4,)),
            sem((3, 2, 2)),
            sem((3, 2, 2)),
            sem((7, 2)),
            sem((7, 2)),
            sem((2,)),
            pltpu.SemaphoreType.REGULAR,
            pltpu.SemaphoreType.REGULAR,
            pltpu.SemaphoreType.REGULAR,
        ],
        compiler_params=pltpu.CompilerParams(
            collective_id=0, has_side_effects=True, vmem_limit_bytes=66_900_000
        ),
        name="window",
    )(
        clips.reshape(micro, cells, tile[3]),
        cotangent.reshape(micro, cells, tile[3]),
        spatial_kernel[0],
        temporal_kernel[0],
    )
    return (out_s[None], out_t[None])


def solution(mesh):
    return jax.shard_map(
        body,
        mesh=mesh,
        in_specs=(
            P("dp", None, None, None, None),
            P("dp", None, None, None, None),
            P("section", None, None),
            P("section", None, None),
        ),
        out_specs=(P("section", "dp", None), P("section", "dp", None)),
        check_vma=False,
    )
```

```python
import functools
import math

import jax
import jax.numpy as jnp
from jax import lax
from jax.experimental import pallas as pl
from jax.experimental.pallas import tpu as pltpu
from jax.sharding import PartitionSpec as P

MESH = pl.DeviceIdType.MESH
F32 = jnp.float32
BF16 = jnp.bfloat16
C = 256
ROWS = 128
HALF = 64
SPACE = 9 * C
TIME = 3 * C


def by_height(v):
    v = v.astype(F32).reshape(8, 2, 8, C)
    return jnp.concatenate([v[:, 0].reshape(HALF, C), v[:, 1].reshape(HALF, C)], axis=0)


def columns(v):
    w = lax.broadcasted_iota(jnp.int32, v.shape, 0) & 7
    before = jnp.where(w == 0, 0.0, pltpu.roll(v, 1, 0))
    after = jnp.where(w == 7, 0.0, pltpu.roll(v, ROWS - 1, 0))
    return before, after


def frames(v):
    zero = jnp.zeros((8, C), F32)
    before = jnp.concatenate([zero, v[0:56], zero, v[64:120]], axis=0)
    after = jnp.concatenate([v[8:64], zero, v[72:128], zero], axis=0)
    return before, after


def nn(a, b):
    return jnp.dot(a, b, preferred_element_type=F32)


def nt(a, b):
    return lax.dot_general(a, b, (((1,), (1,)), ((), ())), preferred_element_type=F32)


def tn(a, b):
    return lax.dot_general(a, b, (((0,), (0,)), ((), ())), preferred_element_type=F32)


def wide_space(v):
    before, after = columns(v)
    return jnp.concatenate([before, v, after], axis=1).astype(BF16)


def wide_time(v):
    before, after = frames(v)
    return jnp.concatenate([before, v, after], axis=1).astype(BF16)


def space_forward(wide, w):
    same = nn(wide, w[768:1536, :])
    top = nn(wide[HALF:], w[1536:2304, :])
    bottom = nn(wide[:HALF], w[0:768, :])
    return same + jnp.concatenate([top, bottom], axis=0)


def activate(pre):
    sigma = jax.nn.sigmoid(pre)
    hidden = (pre * sigma).astype(BF16).astype(F32)
    return hidden, sigma * (1.0 + pre * (1.0 - sigma))


def g_hidden_of(g, w):
    before, after = frames(g)
    out = nt(after.astype(BF16), w[SPACE : SPACE + 256, :])
    out = out + nt(g.astype(BF16), w[SPACE + 256 : SPACE + 512, :])
    return out + nt(before.astype(BF16), w[SPACE + 512 : SPACE + 768, :])


def space_backward(g_pre, w):
    before, after = columns(g_pre)
    same = top = bottom = None
    for q, v in enumerate((after, g_pre, before)):
        v = v.astype(BF16)
        a = nt(v, w[768 + 256 * q : 1024 + 256 * q, :])
        t = nt(v[HALF:], w[256 * q : 256 * q + 256, :])
        b = nt(v[:HALF], w[1536 + 256 * q : 1792 + 256 * q, :])
        same, top, bottom = (a, t, b) if same is None else (same + a, top + t, bottom + b)
    return same + jnp.concatenate([top, bottom], axis=0)


def g_hidden_turned(g, w):
    before, after = frames(g)
    wide = jnp.concatenate([after, g, before], axis=1).astype(BF16)
    return nn(wide, w[SPACE : SPACE + TIME, :])


def space_backward_turned(g_pre, w):
    before, after = columns(g_pre)
    wide = jnp.concatenate([after, g_pre, before], axis=1).astype(BF16)
    same = nn(wide, w[768:1536, :])
    top = nn(wide[HALF:], w[0:768, :])
    bottom = nn(wide[:HALF], w[1536:2304, :])
    return same + jnp.concatenate([top, bottom], axis=0)


def kernel(
    scale,
    clips_ref, cot_ref, ws_ref, wt_ref,
    out_s, out_t,
    wv, turned, cl, ct, xin, yout, bx, bg, gin,
    act, bact, xc, hc, gp, gb, dw, part, r1, s1, r2, s2, r3, fin,
    loc, wg_send, wg_recv, ws_send, ws_recv, wy_send, wy_recv,
    x_send, x_recv, bx_send, bx_recv, ct_send, ct_recv,
    go_send, gin_recv, bg_send, bg_recv,
    r1_send, r1_recv, r2_send, r2_recv, r3_send, r3_recv, r4_sem, up, down, answer,
):
    S = lax.axis_index("section")
    D = lax.axis_index("dp")
    half = S // 4
    x = S % 4
    y = D // 16
    z = (D // 2) % 8
    k = D % 2
    far = D + 14 - 4 * z
    sibling = D + 1 - 2 * k
    end = jnp.logical_or(x == 0, x == 3)
    mine = jnp.where(x == 0, 1, 0)
    base = half * 4
    odd = y % 2
    lane = lax.rem(D, 16)
    above = lax.rem(y + 1, 4) * 16 + lane
    below = lax.rem(y + 3, 4) * 16 + lane

    def copy(src, dst, send, recv, section, dp):
        return pltpu.make_async_remote_copy(
            src_ref=src, dst_ref=dst, send_sem=send, recv_sem=recv,
            device_id={"section": section, "dp": dp}, device_id_type=MESH,
        )

    local = [
        pltpu.make_async_copy(clips_ref, cl, loc.at[0]),
        pltpu.make_async_copy(ws_ref, wv.at[x, 0:SPACE], loc.at[1]),
        pltpu.make_async_copy(wt_ref, wv.at[x, SPACE : SPACE + TIME], loc.at[2]),
    ]
    for c in local:
        c.start()

    barrier = pltpu.get_barrier_semaphore()

    def hello(section, dp):
        pl.semaphore_signal(
            barrier, inc=1, device_id={"section": section, "dp": dp}, device_id_type=MESH
        )

    hello(S, sibling)
    hello(S, above)
    hello(S, below)
    hello(base + lax.rem(x + 1, 4), D)
    hello(base + lax.rem(x + 3, 4), D)

    @pl.when(z > 0)
    def _():
        hello(S, D - 2)

    @pl.when(z < 7)
    def _():
        hello(S, D + 2)

    @pl.when(S == 0)
    def _():
        hello(4, far)

    @pl.when(S == 3)
    def _():
        hello(7, far)

    inner = jnp.logical_and(z > 0, z < 7)
    crossings = jnp.where(jnp.logical_or(S == 4, S == 7), 1, 0)
    pl.semaphore_wait(barrier, 6 + jnp.where(inner, 1, 0) + crossings)

    @pl.when(jnp.logical_or(S == 4, S == 7))
    def _():
        pl.semaphore_signal(
            answer, inc=1, device_id={"section": lax.rem(S + 4, 8), "dp": far}, device_id_type=MESH
        )

    def sweep(sem, step, first, last):
        @pl.when(z != first)
        def _():
            pl.semaphore_wait(sem, 1)

        @pl.when(z != last)
        def _():
            pl.semaphore_signal(
                sem, inc=1, device_id={"section": S, "dp": D + 2 * step}, device_id_type=MESH
            )

    def meet_line():
        @pl.when(z < 4)
        def _():
            sweep(up, 1, 0, 7)
            sweep(down, -1, 7, 0)

        @pl.when(z >= 4)
        def _():
            sweep(down, -1, 7, 0)
            sweep(up, 1, 0, 7)

    for c in local:
        c.wait()

    near = jnp.where(x % 2 == 1, 0, 3)
    passed = jnp.where(x % 2 == 0, 1, 2)
    other = jnp.where(x == 0, 3, 0)
    distant = jnp.where(x == 0, 2, 1)
    middle = jnp.logical_not(end)

    def between(c):
        return jnp.logical_or(c == 1, c == 2)

    def chunk_copy(j, c, parity, core, send, recv, section, dp):
        n = 8 * parity + 4 * core + 2 * (c % 2) + c // 2
        rows = pl.ds(pl.multiple_of(n * 192, 192), 192)
        return copy(wv.at[j, rows], wv.at[j, rows], send, recv, section, dp)

    def x_chunk(j, c, target, slot):
        return chunk_copy(j, c, odd, k, wg_send.at[slot, c], wg_recv.at[j, c], base + target, D)

    def y_chunk(j, c, parity):
        dp = jnp.where(c % 2 == 1, above, below)
        return chunk_copy(j, c, parity, k, wy_send.at[j, c], wy_recv.at[j, c], S, dp)

    def core_chunk(j, c, far_rows, core):
        parity = 1 - odd if far_rows else odd
        at = 4 * far_rows + c
        return chunk_copy(j, c, parity, core, ws_send.at[j, at], ws_recv.at[j, at], S, sibling)

    def each(body):
        def step(c, carry):
            body(c)
            return carry

        lax.fori_loop(0, 4, step, 0)

    def take_x(j, c):
        x_chunk(j, c, 0, 0).wait_recv()
        y_chunk(j, c, odd).start()

        @pl.when(jnp.logical_and(j == passed, jnp.logical_not(between(c))))
        def _():
            x_chunk(j, c, near, 2).start()

        core_chunk(j, c, 0, k).start()

    def take_y(j, c):
        y_chunk(j, c, 1 - odd).wait_recv()
        core_chunk(j, c, 1, k).start()

    def pass_middle():
        @pl.when(middle)
        def _():
            for c in (1, 2):
                x_chunk(passed, c, 0, 0).wait_recv()
                x_chunk(passed, c, near, 2).start()

    @each
    def _(c):
        x_chunk(x, c, near, 0).start()

        @pl.when(jnp.logical_and(middle, between(c)))
        def _():
            x_chunk(x, c, 3 - x, 1).start()

    cot_copy = copy(
        cot_ref.at[jnp.where(x == 1, 1, 0)], ct, ct_send, ct_recv, jnp.where(x == 1, 4, 7), far
    )

    def turn(j, n):
        rows = pl.ds(pl.multiple_of(n * C, C), C)
        turned[j, rows] = wv[j, rows].T
        return 0

    @pl.when(half == 1)
    def _():
        pass_middle()

        @pl.when(end)
        def _():
            lax.fori_loop(0, 12, lambda n, carry: turn(x, n), 0)

        @pl.when(jnp.logical_not(end))
        def _():
            meet_line()
            cot_copy.start()
            lax.fori_loop(9, 12, lambda n, carry: turn(x, n), 0)

    def rows_of(c, h):
        return pl.ds(pl.multiple_of(h * 128 + c * HALF, HALF), HALF)

    def keep(ref, c, value):
        ref[rows_of(c, 0), :] = value[:HALF]
        ref[rows_of(c, 1), :] = value[HALF:]

    def y_copy(c):
        return copy(yout.at[c], xin.at[c], x_send.at[c], x_recv.at[c], lax.rem(S + 1, 8), D)

    cross_copy = copy(yout.at[0], bx.at[0], x_send.at[0], bx_recv, 7, far)
    hand_copy = copy(yout.at[1], ct, x_send.at[1], ct_recv, 0, D)
    relay_copy = copy(ct, bx.at[0], ct_send, bx_recv, 4, far)

    def owner_hidden(c):
        wide = wide_space(xin[c].astype(F32))
        keep(xc, c, wide)
        hidden, slope = activate(space_forward(wide, wv.at[x]))
        act[c] = slope
        wide = wide_time(hidden)
        keep(hc, c, wide)
        return wide

    def forward(first):
        def clip(c, carry):
            if first:
                xin[c] = by_height(cl[c]).astype(BF16)
            else:
                y_copy(c).wait_recv()
            wide = owner_hidden(c)
            out = xin[c].astype(F32) + nn(wide, wv[x, SPACE : SPACE + TIME, :])
            yout[c] = out.astype(BF16)
            if first:
                y_copy(c).start()
            else:
                @pl.when(x < 3)
                def _():
                    y_copy(c).start()

                @pl.when(jnp.logical_and(x == 3, c == 0))
                def _():
                    pl.semaphore_wait(answer, 1)
                    cross_copy.start()

                @pl.when(jnp.logical_and(x == 3, c == 1))
                def _():
                    hand_copy.start()

            return carry

        lax.fori_loop(0, 2, clip, 0)

    @pl.when(S == 0)
    def _():
        forward(True)

    @pl.when(jnp.logical_or(S == 0, S == 3))
    def _():
        meet_line()

    @pl.when(end)
    def _():
        @each
        def _(c):
            take_x(passed, c)
            take_x(other, c)

    @pl.when(S == 0)
    def _():
        hand_copy.wait_recv()
        pl.semaphore_wait(answer, 1)
        relay_copy.start()

    @pl.when(jnp.logical_and(half == 0, x > 0))
    def _():
        forward(False)
        pass_middle()

        @pl.when(x < 3)
        def _():
            meet_line()
            lax.fori_loop(9, 12, lambda n, carry: turn(x, n), 0)

    def x_copy(j):
        return copy(bx.at[j], xin.at[mine], bx_send.at[j], x_recv.at[mine], base + j, D)

    def g_copy(j):
        return copy(bg.at[j + 1], gin.at[mine], go_send.at[j], gin_recv.at[mine], base + j, D)

    back_copy = copy(bg.at[0], bg.at[4], bg_send, bg_recv, lax.rem(S + 4, 8), far)

    @pl.when(end)
    def _():
        @each
        def _(c):
            take_x(distant, c)
            take_y(passed, c)
            take_y(other, c)
        @each
        def _(c):
            take_y(distant, c)
        @each
        def _(c):
            for j in (passed, other, distant):
                core_chunk(j, c, 0, 1 - k).wait_recv()
                core_chunk(j, c, 1, 1 - k).wait_recv()

        @pl.when(half == 0)
        def _():
            bx[0] = by_height(cl[mine]).astype(BF16)

        @pl.when(half == 1)
        def _():
            cross_copy.wait_recv()

        def layer(j, carry):
            @pl.when(half == 1)
            def _():
                @pl.when(j == x)
                def _():
                    xin[mine] = bx[j]

                @pl.when(j != x)
                def _():
                    x_copy(j).start()

            v = bx[j].astype(F32)
            hidden, slope = activate(space_forward(wide_space(v), wv.at[j]))
            bact[j] = slope

            @pl.when(j < 3)
            def _():
                out = v + nn(wide_time(hidden), wv[j, SPACE : SPACE + TIME, :])
                bx[j + 1] = out.astype(BF16)

            return carry

        lax.fori_loop(0, 4, layer, 0)

        @pl.when(half == 0)
        def _():
            lax.fori_loop(0, 48, lambda n, carry: turn(n // 12, n % 12), 0)
            back_copy.wait_recv()

        @pl.when(half == 1)
        def _():
            cot_copy.wait_recv()
            bg[4] = by_height(ct[...]).astype(BF16)

        def hand_out(j):
            @pl.when(j == x)
            def _():
                gin[mine] = bg[j + 1]

            @pl.when(j != x)
            def _():
                g_copy(j).start()

        def layer_back(j, w, g_hidden, g_space):
            g = bg[j + 1].astype(F32)
            g_pre = (g_hidden(g, w.at[j]) * bact[j]).astype(BF16).astype(F32)
            bg[j] = (g + g_space(g_pre, w.at[j])).astype(BF16)

        def layers_back(is_turned, lowest):
            def step(i, carry):
                j = 3 - i
                hand_out(j)

                @pl.when(jnp.logical_and(j >= lowest, is_turned(j)))
                def _():
                    layer_back(j, turned, g_hidden_turned, space_backward_turned)

                @pl.when(jnp.logical_and(j >= lowest, jnp.logical_not(is_turned(j))))
                def _():
                    layer_back(j, wv, g_hidden_of, space_backward)

                return carry

            lax.fori_loop(0, 4, step, 0)

        layers_back(lambda j: jnp.logical_or(half == 0, j == x), 1 - half)

        @pl.when(half == 1)
        def _():
            back_copy.start()
            meet_line()

    @pl.when(half == 1)
    def _():
        def clip(c, carry):
            @pl.when(jnp.logical_not(jnp.logical_and(end, c == mine)))
            def _():
                y_copy(c).wait_recv()

            owner_hidden(c)
            return carry

        lax.fori_loop(0, 2, clip, 0)

    def clip_back(i, carry):
        c = jnp.where(i == 0, mine, 1 - mine)

        @pl.when(jnp.logical_not(jnp.logical_and(end, c == mine)))
        def _():
            copy(gin.at[c], gin.at[c], go_send.at[0], gin_recv.at[c], S, D).wait_recv()

        keep(gb, c, gin[c])
        g = gin[c].astype(F32)
        keep(gp, c, (g_hidden_turned(g, turned.at[x]) * act[c]).astype(BF16))
        return carry

    lax.fori_loop(0, 2, clip_back, 0)

    for q in range(3):
        lanes = slice(256 * q, 256 * q + 256)
        dw[SPACE + 256 * q : SPACE + 256 * q + 256, :] = tn(hc[:, lanes], gb[...])
        dw[256 * q : 256 * q + 256, :] = tn(xc[0:128, lanes], gp[128:256, :])
        dw[768 + 256 * q : 1024 + 256 * q, :] = tn(xc[:, lanes], gp[...])
        dw[1536 + 256 * q : 1792 + 256 * q, :] = tn(xc[128:256, lanes], gp[0:128, :])

    blocks = [lax.rem(y + i, 4) for i in (2, 1, 3, 0)]
    sides = (lax.rem(y + 1, 4), lax.rem(y + 3, 4))

    def core_step(i, column):
        yb = blocks[i]
        return copy(part.at[column, yb], r1.at[yb], r1_send.at[i], r1_recv.at[i], S, sibling)

    for i in range(4):
        def pack(b, carry):
            n = blocks[i] * 8 + b
            top = dw[pl.ds(pl.multiple_of(n * 72, 8), 72), :]
            low = dw[pl.ds(pl.multiple_of(SPACE + n * 24, 8), 24), :]
            block = jnp.concatenate([top, low], axis=0).astype(BF16)
            part[0, blocks[i], b] = block[:, 0:128]
            part[1, blocks[i], b] = block[:, 128:256]
            return carry

        lax.fori_loop(0, 8, pack, 0)
        core_step(i, 1 - k).start()

    def part_rows(r):
        return slice(48 * r, 48 * r + 48)

    def add_cores(yb, start, stop, rows):
        def one(b, carry):
            s1[yb, b, rows] = (part[k, yb, b, rows].astype(F32) + r1[yb, b, rows].astype(F32)).astype(BF16)
            return carry

        lax.fori_loop(start, stop, one, 0)

    def y_step(i, side, r):
        forth, back = sides[side], sides[1 - side]
        to = (forth, back, forth)[i]
        some, rows = pl.ds(4 * side, 4), pl.ds(48 * r, 48)
        return copy(
            s1.at[blocks[0] if i == 0 else to, some, rows], r2.at[i, some, rows],
            r2_send.at[i, side, r], r2_recv.at[i, side, r], S, to * 16 + lane,
        )

    def z_step(i, r):
        to = lax.rem(z + i, 8)
        rows = pl.ds(48 * r, 48)
        return copy(
            s2.at[to, rows], r3.at[i - 1, rows], r3_send.at[i - 1, r], r3_recv.at[i - 1, r],
            S, y * 16 + to * 2 + k,
        )

    core_step(0, k).wait_recv()
    for r in range(2):
        add_cores(blocks[0], 0, 8, part_rows(r))
        for side in range(2):
            y_step(0, side, r).start()
    for side in (1, 0):
        core_step(2 - side, k).wait_recv()
        add_cores(sides[1 - side], 4 * side, 4 * side + 4, slice(0, 96))
        y_step(1, side, 0).start()
    for r in range(2):
        for side in range(2):
            forth, rows = sides[side], part_rows(r)
            y_step(0, side, r).wait_recv()

            def add_relayed(b, carry):
                total = part[k, forth, b, rows].astype(F32) + r1[forth, b, rows].astype(F32)
                s1[forth, b, rows] = (total + r2[0, b, rows].astype(F32)).astype(BF16)
                return carry

            lax.fori_loop(4 * side, 4 * side + 4, add_relayed, 0)
            y_step(2, side, r).start()
    for side in range(2):
        y_step(1, side, 1).start()
    core_step(3, k).wait_recv()
    for r in range(2):
        rows = part_rows(r)
        for i in (1, 2):
            for side in range(2):
                y_step(i, side, r).wait_recv()

        def add_y(b, carry):
            total = part[k, y, b, rows].astype(F32) + r1[y, b, rows].astype(F32)
            total = total + r2[1, b, rows].astype(F32) + r2[2, b, rows].astype(F32)
            s2[b, rows] = total.astype(BF16)
            return carry

        lax.fori_loop(0, 8, add_y, 0)
        for d in range(7, 0, -1):
            @pl.when(z + d < 8)
            def _():
                z_step(d, r).start()

            @pl.when(z >= d)
            def _():
                z_step(8 - d, r).start()

    for r in range(2):
        for i in range(1, 8):
            z_step(i, r).wait_recv()

    total = s2[z].astype(F32)
    for i in range(7):
        total = total + r3[i].astype(F32)
    fin[k] = total * scale

    final = copy(fin.at[k], fin.at[k], r4_sem.at[0], r4_sem.at[1], S, sibling)
    final.start()
    final.wait_send()
    copy(fin.at[1 - k], fin.at[1 - k], r4_sem.at[0], r4_sem.at[1], S, sibling).wait_recv()

    for core in range(2):
        @pl.when(k == core)
        def _():
            for side in range(2):
                lanes = slice(128 * side, 128 * side + 128)
                out_s[:, lanes] = fin[side, 36 * core : 36 * core + 36, :]
                out_t[:, lanes] = fin[side, 72 + 12 * core : 84 + 12 * core, :]

    for i in range(4):
        core_step(i, 1 - k).wait_send()
    for i in range(3):
        for side in range(2):
            for r in range(2):
                y_step(i, side, r).wait_send()
    for i in range(1, 8):
        for r in range(2):
            z_step(i, r).wait_send()
    @each
    def _(c):
        x_chunk(x, c, near, 0).wait_send()

        @pl.when(jnp.logical_and(middle, between(c)))
        def _():
            x_chunk(x, c, 3 - x, 1).wait_send()

        @pl.when(middle == between(c))
        def _():
            x_chunk(passed, c, near, 2).wait_send()

        @pl.when(end)
        def _():
            for j in (passed, other, distant):
                y_chunk(j, c, odd).wait_send()
                core_chunk(j, c, 0, k).wait_send()
                core_chunk(j, c, 1, k).wait_send()

    @pl.when(jnp.logical_or(S == 5, S == 6))
    def _():
        cot_copy.wait_send()

    @pl.when(S == 0)
    def _():
        relay_copy.wait_send()

    @pl.when(half == 0)
    def _():
        for c in range(2):
            y_copy(c).wait_send()

    @pl.when(end)
    def _():
        for i in range(1, 4):
            j = lax.rem(x + i, 4)
            g_copy(j).wait_send()

            @pl.when(half == 1)
            def _():
                x_copy(j).wait_send()

        @pl.when(half == 1)
        def _():
            back_copy.wait_send()


def body(clips, cotangent, spatial_kernel, temporal_kernel):
    micro = clips.shape[0]
    tile = clips.shape[1:]
    cells = tile[0] * tile[1] * tile[2]
    scale = 1.0 / math.sqrt(micro * lax.axis_size("dp") * cells)
    sem = pltpu.SemaphoreType.DMA
    vmem = pltpu.VMEM
    out_s, out_t = pl.pallas_call(
        functools.partial(kernel, scale),
        out_shape=(jax.ShapeDtypeStruct((36, C), F32), jax.ShapeDtypeStruct((12, C), F32)),
        in_specs=[pl.BlockSpec(memory_space=pltpu.HBM)] * 4,
        out_specs=(pl.BlockSpec(memory_space=pltpu.VMEM),) * 2,
        scratch_shapes=[
            vmem((4, SPACE + TIME, C), BF16),
            vmem((4, SPACE + TIME, C), BF16),
            vmem((2, ROWS, C), BF16),
            vmem((ROWS, C), BF16),
            vmem((2, ROWS, C), BF16),
            vmem((2, ROWS, C), BF16),
            vmem((4, ROWS, C), BF16),
            vmem((5, ROWS, C), BF16),
            vmem((2, ROWS, C), BF16),
            vmem((2, ROWS, C), F32),
            vmem((4, ROWS, C), F32),
            vmem((2 * ROWS, 3 * C), BF16),
            vmem((2 * ROWS, 3 * C), BF16),
            vmem((2 * ROWS, C), BF16),
            vmem((2 * ROWS, C), BF16),
            vmem((SPACE + TIME, C), F32),
            vmem((2, 4, 8, 96, 128), BF16),
            vmem((4, 8, 96, 128), BF16),
            vmem((4, 8, 96, 128), BF16),
            vmem((3, 8, 96, 128), BF16),
            vmem((8, 96, 128), BF16),
            vmem((7, 96, 128), BF16),
            vmem((2, 96, 128), F32),
            sem((3,)),
            sem((3, 4)),
            sem((4, 4)),
            sem((4, 8)),
            sem((4, 8)),
            sem((4, 4)),
            sem((4, 4)),
            sem((2,)),
            sem((2,)),
            sem((4,)),
            sem,
            sem,
            sem,
            sem((4,)),
            sem((2,)),
            sem,
            sem,
            sem((4,)),
            sem((4,)),
            sem((3, 2, 2)),
            sem((3, 2, 2)),
            sem((7, 2)),
            sem((7, 2)),
            sem((2,)),
            pltpu.SemaphoreType.REGULAR,
            pltpu.SemaphoreType.REGULAR,
            pltpu.SemaphoreType.REGULAR,
        ],
        compiler_params=pltpu.CompilerParams(
            collective_id=0, has_side_effects=True, vmem_limit_bytes=66_900_000
        ),
        name="window",
    )(
        clips.reshape(micro, cells, tile[3]),
        cotangent.reshape(micro, cells, tile[3]),
        spatial_kernel[0],
        temporal_kernel[0],
    )
    return (out_s[None], out_t[None])


def solution(mesh):
    return jax.shard_map(
        body,
        mesh=mesh,
        in_specs=(
            P("dp", None, None, None, None),
            P("dp", None, None, None, None),
            P("section", None, None),
            P("section", None, None),
        ),
        out_specs=(P("section", "dp", None), P("section", "dp", None)),
        check_vma=False,
    )
```
